256 devices in a mesh: freq: 32 (over x, z_lo, core), mz: 8 (over y, z_hi).
Axes of the slice: x: 4, y: 4, z: 8 (z_hi: 2, z_lo: 4; z = z_hi * 4 + z_lo), core: 2. Of those that a mesh axis runs over, the one named last changes fastest.
Arguments:
- intensity: bfloat16 [8, 6144, 4096], P(None, 'freq', 'mz'), may hold values from -6 to 6
- elution: float32 [6144, 64], P(('freq', 'mz')), may hold values from -6 to 6
- loadings: float32 [8, 64], replicated, may hold values from 0.0005 to 0.01
- shifts: int32 [8, 64], replicated, may hold values from 0 to 255
- bin_weight: float32 [6144], replicated, may hold values from 0.25 to 4
Outputs:
- spectral: float32 [64, 4096], P(None, ('mz', 'freq'))
The draws below stay inside these ranges and needn't reach their ends.
All inputs are finite; a program needn't handle non-finite values.
Results may differ from the reference program's by a relative error of at most 0.0003.
Values may be sent and summed in bfloat16 or wider, within the bound.
A program may use at most 64 MiB of HBM per device.

```python
import math
import jax
import jax.numpy as jnp
from jax import lax

T_SIZE = 6144
M = 4096
R = 64
K = 8
N_FREQ = 32


def plant(entries, stream_key, smallest, largest):
    spot = [jax.random.randint(jax.random.fold_in(stream_key, axis), (), 0, length) for axis, length in enumerate(entries.shape)]
    longest = entries.shape.index(max(entries.shape))
    neighbour = spot[:longest] + [(spot[longest] + 1) % entries.shape[longest]] + spot[longest + 1:]
    return entries.at[tuple(spot)].set(smallest).at[tuple(neighbour)].set(largest)


def level_of(key, extent, pieces, low, top_value):
    def one(dim, blocks):
        draws = jax.random.uniform(jax.random.fold_in(jax.random.fold_in(key, 6), dim), (blocks,), jnp.float32, low / len(pieces), top_value / len(pieces))
        return jnp.repeat(jnp.exp(draws), extent[dim] // blocks).reshape((-1,) + (1,) * (len(extent) - dim - 1))

    level = one(*pieces[0])
    for cut in pieces[1:]:
        level = level * one(*cut)
    return level


def normal_values(key, extent, deviation, reach, cuts=(), held_as=jnp.bfloat16):
    values = jax.random.normal(key, extent, jnp.float32) * deviation
    if len(cuts) > 0:
        values = level_of(key, extent, cuts, -0.22, 0.18) * values
    return jnp.clip(values, min=-reach, max=reach).astype(held_as)


def setup_inputs(seed: int = 0) -> dict:
    seeds = jax.random.split(jax.random.key(seed), 6)
    intensity = normal_values(seeds[0], (K, T_SIZE, M), 1.0, 6.0, ((1, 32), (2, 8)))
    elution = normal_values(seeds[1], (T_SIZE, R), 1.0, 6.0, ((0, 256),), jnp.float32)
    loadings = jnp.clip(jnp.exp(jax.random.uniform(seeds[2], (K, R), jnp.float32, math.log(0.0005), math.log(0.01))), 0.0005, 0.01)
    shifts = plant(jax.random.randint(seeds[3], (K, R), 0, 256), jax.random.fold_in(seeds[3], 1), 0, 255).astype(jnp.int32)
    bin_weight = jnp.clip(jnp.exp(jax.random.uniform(seeds[4], (T_SIZE,), jnp.float32, math.log(0.25), math.log(4.0))), 0.25, 4.0)
    return dict(intensity=intensity, elution=elution, loadings=loadings, shifts=shifts, bin_weight=bin_weight)


PRECISE = lax.Precision.HIGHEST

def turn_angle(product, length):
    return 2.0 * math.pi / length * (product % length).astype(jnp.float32)

def cholesky_solve(gram_matrix, numerator):
    factor = jnp.linalg.cholesky(gram_matrix)
    middle = lax.linalg.triangular_solve(factor, numerator, left_side=True, lower=True)
    return lax.linalg.triangular_solve(factor, middle, left_side=True, lower=True, transpose_a=True)

def reference(intensity, elution, loadings, shifts, bin_weight):
    freq_count = N_FREQ
    bin_count = T_SIZE // freq_count
    norm_scale = 1.0 / math.sqrt(T_SIZE)
    dev_ids = jnp.arange(freq_count, dtype=jnp.int32)
    bin_ids = jnp.arange(bin_count, dtype=jnp.int32)
    dev_angle = turn_angle(dev_ids[:, None] * dev_ids[None, :], freq_count)
    cos_dev = jnp.cos(dev_angle)
    sin_dev = jnp.sin(dev_angle)
    twiddle = turn_angle(dev_ids[:, None] * bin_ids[None, :], T_SIZE)
    twid_cos = jnp.cos(twiddle)[:, :, None]
    twid_sin = jnp.sin(twiddle)[:, :, None]
    bin_angle = turn_angle(bin_ids[:, None] * bin_ids[None, :], bin_count)
    cos_bin = jnp.cos(bin_angle)
    sin_bin = jnp.sin(bin_angle)
    stacked = elution.reshape(freq_count, bin_count * R)
    part_re = jnp.dot(cos_dev, stacked, precision=PRECISE).reshape(freq_count, bin_count, R)
    part_im = -jnp.dot(sin_dev, stacked, precision=PRECISE).reshape(freq_count, bin_count, R)
    turn_re = part_re * twid_cos + part_im * twid_sin
    turn_im = part_im * twid_cos - part_re * twid_sin
    spec_re = (jnp.einsum('bq,aqr->abr', cos_bin, turn_re, precision=PRECISE) + jnp.einsum('bq,aqr->abr', sin_bin, turn_im, precision=PRECISE)) * norm_scale
    spec_im = (jnp.einsum('bq,aqr->abr', cos_bin, turn_im, precision=PRECISE) - jnp.einsum('bq,aqr->abr', sin_bin, turn_re, precision=PRECISE)) * norm_scale
    weights_grid = bin_weight.reshape(bin_count, freq_count).T[:, :, None]
    freq_index = dev_ids[:, None] + freq_count * bin_ids[None, :]

    def one_run(totals, inputs):
        run_data, run_amp, run_lag = inputs
        phase = turn_angle(freq_index[:, :, None] * run_lag[None, None, :], T_SIZE)
        phase_cos = jnp.cos(phase)
        phase_sin = jnp.sin(phase)
        model_re = run_amp * (spec_re * phase_cos + spec_im * phase_sin)
        model_im = run_amp * (spec_im * phase_cos - spec_re * phase_sin)
        wmod_re = weights_grid * model_re
        wmod_im = weights_grid * model_im
        gram_part = jnp.einsum('abr,abs->rs', wmod_re, model_re, precision=PRECISE) + jnp.einsum('abr,abs->rs', wmod_im, model_im, precision=PRECISE)
        back_re = jnp.einsum('abr,bq->aqr', wmod_re, cos_bin, precision=PRECISE) - jnp.einsum('abr,bq->aqr', wmod_im, sin_bin, precision=PRECISE)
        back_im = jnp.einsum('abr,bq->aqr', wmod_re, sin_bin, precision=PRECISE) + jnp.einsum('abr,bq->aqr', wmod_im, cos_bin, precision=PRECISE)
        samples = run_data.astype(jnp.float32).reshape(freq_count, bin_count * M)
        raw_re = jnp.dot(cos_dev, samples, precision=PRECISE).reshape(freq_count, bin_count, M)
        raw_im = -jnp.dot(sin_dev, samples, precision=PRECISE).reshape(freq_count, bin_count, M)
        half_re = raw_re * twid_cos + raw_im * twid_sin
        half_im = raw_im * twid_cos - raw_re * twid_sin
        num_part = jnp.dot(back_re.reshape(T_SIZE, R).T, half_re.reshape(T_SIZE, M), precision=PRECISE) + jnp.dot(back_im.reshape(T_SIZE, R).T, half_im.reshape(T_SIZE, M), precision=PRECISE)
        return ((totals[0] + num_part, totals[1] + gram_part), None)
    start = (jnp.zeros((R, M), jnp.float32), jnp.zeros((R, R), jnp.float32))
    (numerator, gram_matrix), _ = lax.scan(one_run, start, (intensity, loadings, shifts))
    numerator = numerator * norm_scale
    return cholesky_solve(gram_matrix, numerator)
```

```python
import functools
import math

import jax
import jax.numpy as jnp
import numpy as np
from jax import lax
from jax.experimental import pallas as pl
from jax.experimental.pallas import tpu as pltpu
from jax.sharding import PartitionSpec as P

MESH = pl.DeviceIdType.MESH
HIGHEST = lax.Precision.HIGHEST
F32 = jnp.float32
BF16 = jnp.bfloat16

LENGTH = 6144
ROWS = 48
LANES = 128
RUNS = 8
COMP = 64
BLOCK = 192
CHANNELS = 512
FREQ = 32
OWN = 16
WINDOW = 512


def transform_tables():
    x48 = np.arange(ROWS)
    b128 = np.arange(LANES)
    inner = 2.0 * np.pi / ROWS * ((x48[:, None] * x48[None, :]) % ROWS)
    middle = 2.0 * np.pi / LENGTH * ((x48[:, None] * b128[None, :]) % LENGTH)
    outer = 2.0 * np.pi / LANES * ((b128[:, None] * b128[None, :]) % LANES)
    first = np.concatenate([np.cos(inner), np.sin(inner)], axis=0)
    turn = np.concatenate([np.cos(middle), np.sin(middle)], axis=0)
    last = np.concatenate([np.cos(outer), -np.sin(outer)], axis=0) / LENGTH
    return [jnp.asarray(t.astype(np.float32)) for t in (first, turn, last)]


def split(value):
    high = value.astype(BF16)
    low = (value - high.astype(F32)).astype(BF16)
    return high, low


def half_turn(value):
    return pltpu.roll(value, 64, 1)


def lag_weights(weight, first, turn, last, flip):
    inner = jnp.dot(first, weight, precision=HIGHEST, preferred_element_type=F32)
    cos_part, sin_part = inner[:ROWS], inner[ROWS:]
    tcos, tsin = turn[:ROWS], turn[ROWS:]
    real = cos_part * tcos - sin_part * tsin
    imag = cos_part * tsin + sin_part * tcos
    both = jnp.concatenate([real, imag], axis=1)
    by_x = jnp.dot(both, last, precision=HIGHEST, preferred_element_type=F32)
    padded = jnp.concatenate([by_x, jnp.zeros((LANES - ROWS, LANES), F32)], axis=0)
    flip[...] = jnp.transpose(padded)
    lane = lax.broadcasted_iota(jnp.int32, (16, LANES), 1)

    def part(index, shift):
        rows = flip[pl.ds(index, 16, stride=8), :]
        return rows if shift == 0 else pltpu.roll(rows, shift, 1)

    first_row = jnp.where(lane < 48, part(0, 0), jnp.where(lane < 96, part(1, 48), part(2, 96)))
    second_row = jnp.where(
        lane < 16, part(2, 96), jnp.where(lane < 64, part(3, 16), jnp.where(lane < 112, part(4, 64), part(5, 112)))
    )
    third_row = jnp.where(lane < 32, part(5, 112), jnp.where(lane < 80, part(6, 32), part(7, 80)))
    return first_row, second_row, third_row


def shifted(window, amount):
    value = window
    for bit in (128, 64, 32, 16, 8):
        rows = BLOCK + bit
        value = jnp.where((amount & bit) != 0, value[bit : bit + rows], value[0:rows])
    for bit in (4, 2, 1):
        value = jnp.where((amount & bit) != 0, pltpu.roll(value, value.shape[0] - bit, 0), value)
    return pltpu.roll(value, value.shape[0] - 1, 0)[0:BLOCK]


def kernel(
    elution_ref,
    loadings_ref,
    shifts_ref,
    weight_ref,
    first_ref,
    turn_ref,
    last_ref,
    intensity_ref,
    out_ref,
    samples,
    mine,
    theirs,
    blocks,
    profile,
    lags,
    flip,
    toeplitz,
    total,
    window,
    gram_send,
    gram_core,
    gram_x,
    gram_z,
    num_send,
    num_recv,
    load_sem,
    pair_sem,
    z_send,
    z_recv,
    p_send,
    p_recv,
    q_send,
    q_recv,
    swap_send,
    swap_recv,
    gram_sems,
    num_sems,
    num_recv_sems,
):
    freq = lax.axis_index("freq")
    mz = lax.axis_index("mz")
    core = freq % 2
    z_lo = (freq // 2) % 4
    x = freq // 8
    y = mz // 2
    z_hi = mz % 2
    p = x * (1 - core) + y * core
    q = y * (1 - core) + x * core

    def at(x_to, y_to, z_to, core_to):
        return (x_to * 8 + (z_to % 4) * 2 + core_to, y_to * 2 + z_to // 4)

    def at_pq(p_to, q_to):
        return at(p_to * (1 - core) + q_to * core, q_to * (1 - core) + p_to * core, z_hi * 4 + z_lo, core)

    partner = (freq + 1 - 2 * core, mz)
    z_mine = z_hi * 4 + z_lo

    barrier = pltpu.get_barrier_semaphore()

    def greet(step, carry):
        pl.semaphore_signal(barrier, inc=1, device_id=((freq + step) % FREQ, mz), device_id_type=MESH)
        return carry

    lax.fori_loop(1, FREQ, greet, 0)
    for step in range(1, 4):
        pl.semaphore_signal(
            barrier, inc=1, device_id=(freq, ((y + step) % 4) * 2 + z_hi), device_id_type=MESH
        )
    for step in range(4):
        pl.semaphore_signal(
            barrier, inc=1, device_id=at(x, y, (1 - z_hi) * 4 + step, core), device_id_type=MESH
        )

    load = pltpu.make_async_copy(intensity_ref, samples, load_sem)
    load.start()
    own_rows = elution_ref[...]
    mine[...] = jnp.concatenate([own_rows, own_rows], axis=1)

    lag_rows = lag_weights(weight_ref[...], first_ref[...], turn_ref[...], last_ref[...], flip)
    for z in range(3):
        lags[z] = lag_rows[z]

    pl.semaphore_wait(barrier, FREQ - 1 + 3 + 4)

    def remote(source, target, send, recv, device):
        return pltpu.make_async_remote_copy(
            src_ref=source, dst_ref=target, send_sem=send, recv_sem=recv, device_id=device, device_id_type=MESH
        )

    pair = remote(mine, theirs, pair_sem.at[0], pair_sem.at[1], partner)
    pair.start()
    pair.wait()
    lane24 = lax.broadcasted_iota(jnp.int32, (24, LANES), 1)
    side = (lane24 // 64) == core
    z_copies = []
    for step in range(1, 8):
        z_to = (z_mine + step) % 8
        z_copies.append(
            remote(
                blocks.at[core, q, p, z_lo],
                blocks.at[core, q, p, z_lo],
                z_send.at[step - 1],
                z_recv.at[z_lo],
                at(x, y, z_to, core),
            )
        )

    @pl.when(z_hi == core)
    def _():
        blocks[core, q, p, z_lo] = jnp.where(side, mine[...], theirs[...])
        for copy in z_copies:
            copy.start()

    row = lax.broadcasted_iota(jnp.int32, (LANES, LANES), 0)
    lane = lax.broadcasted_iota(jnp.int32, (LANES, LANES), 1)
    upper = lane >= row

    def turned(z, g):
        base = jnp.broadcast_to(lags[z, pl.ds(g, 1), :], (LANES, LANES))
        return pltpu.roll(base, 0, 1, stride=1, stride_axis=0)

    def build(g, before):
        for z in range(3):
            here = turned(z, g)
            high, low = split(jnp.where(upper, here, before))
            toeplitz[0, 3 * g + z] = high
            toeplitz[1, 3 * g + z] = low
            before = here
        return before

    lax.fori_loop(0, 16, build, turned(2, 15))

    for source in range(4):

        @pl.when(jnp.logical_or(z_hi != core, z_lo != source))
        def _(source=source):
            spot = blocks.at[core, q, p, source]
            remote(spot, spot, z_send.at[0], z_recv.at[source], partner).wait_recv()

    swaps = [remote(blocks.at[core, q, p], blocks.at[core, q, p], swap_send.at[0], swap_recv.at[0], partner)]
    swaps[0].start()
    p_copies = []
    for step in range(1, 4):
        copy = remote(
            blocks.at[core, q, p],
            blocks.at[core, q, p],
            p_send.at[step - 1],
            p_recv.at[step - 1],
            at_pq((p + step) % 4, q),
        )
        copy.start()
        p_copies.append(copy)
    for step in range(1, 4):
        spot = blocks.at[core, q, (p + 4 - step) % 4]
        remote(spot, spot, p_send.at[step - 1], p_recv.at[step - 1], partner).wait_recv()
        swap = remote(spot, spot, swap_send.at[step], swap_recv.at[step], partner)
        swap.start()
        swaps.append(swap)
    q_copies = []
    for step in range(1, 4):
        copy = remote(
            blocks.at[core, q], blocks.at[core, q], q_send.at[step - 1], q_recv.at[step - 1], at_pq(p, (q + step) % 4)
        )
        copy.start()
        q_copies.append(copy)
    for step in range(1, 4):
        spot = blocks.at[core, (q + 4 - step) % 4]
        remote(spot, spot, q_send.at[step - 1], q_recv.at[step - 1], partner).wait_recv()
        swap = remote(spot, spot, swap_send.at[3 + step], swap_recv.at[3 + step], partner)
        swap.start()
        swaps.append(swap)
    other = 1 - core
    spot = blocks.at[other, p, q]
    remote(spot, spot, swap_send.at[0], swap_recv.at[0], partner).wait_recv()
    for step in range(1, 4):
        spot = blocks.at[other, p, (q + 4 - step) % 4]
        remote(spot, spot, swap_send.at[step], swap_recv.at[step], partner).wait_recv()
    for step in range(1, 4):
        spot = blocks.at[other, (p + 4 - step) % 4]
        remote(spot, spot, swap_send.at[3 + step], swap_recv.at[3 + step], partner).wait_recv()

    left = lax.broadcasted_iota(jnp.int32, (24, LANES), 1) < 64

    def unpack(index, carry):
        x_at = index // 4
        zl_at = index % 4
        low_rows, high_rows = [], []
        for y_at in range(4):
            for zh_at in range(2):
                if zh_at == 0:
                    block = blocks[0, y_at, x_at, zl_at]
                else:
                    block = blocks[1, x_at, y_at, zl_at]
                rounded = block.astype(BF16).astype(F32)
                rest = block - rounded
                low_rows.append(jnp.where(left, rounded, half_turn(rest)))
                high_rows.append(jnp.where(left, half_turn(rounded), rest))
        start = pl.multiple_of(index * 384, 128)
        profile[pl.ds(start, BLOCK), :] = jnp.concatenate(low_rows, axis=0).astype(BF16)
        profile[pl.ds(start + BLOCK, BLOCK), :] = jnp.concatenate(high_rows, axis=0).astype(BF16)
        return carry

    lax.fori_loop(0, 16, unpack, 0)
    profile[LENGTH : LENGTH + WINDOW, :] = profile[0:WINDOW, :]

    begin = ((freq * 3 + 96 - 4) // 2) % ROWS
    total[...] = jnp.zeros_like(total)

    def filtered(tile, carry):
        pieces = []
        for part in range(2):
            for row_block in (0, 2):
                spot = 2 * tile + 2 * ROWS - begin - row_block
                pieces.append(
                    jnp.concatenate([toeplitz[part, spot % ROWS], toeplitz[part, (spot + 1) % ROWS]], axis=1)
                )
        start = pl.multiple_of(tile * 256, 128)
        rows = jnp.concatenate([profile[pl.ds(start, 256), :], profile[pl.ds(start + 128, 256), :]], axis=1)
        total[...] += jnp.dot(jnp.concatenate(pieces, axis=0), rows, preferred_element_type=F32)
        return carry

    lax.fori_loop(0, 24, filtered, 0)
    for row_block in range(4):
        base = (row_block // 2) * 128
        cut = pl.ds((row_block % 2) * 128, 128)
        value = total[pl.ds(base, 128), cut] + total[pl.ds(256 + base, 128), cut]
        window[0, pl.ds(row_block * 128, 128), :] = value + half_turn(value)
        start = pl.multiple_of(begin * 128 + row_block * 128, 128)
        value = profile[pl.ds(start, 128), :].astype(F32)
        window[1, pl.ds(row_block * 128, 128), :] = value + half_turn(value)

    skip = pl.multiple_of((freq % 2) * 64, 64)
    load.wait()
    filtered_rows = window[0, pl.ds(skip, 448), :]
    plain_rows = window[1, pl.ds(skip, 448), :]
    quad = jnp.zeros((256, 256), F32)
    numer = jnp.zeros((COMP, CHANNELS), F32)
    stacks = []
    for pair_at in range(RUNS // 2):
        amount = jnp.concatenate([shifts_ref[2 * pair_at : 2 * pair_at + 1], shifts_ref[2 * pair_at + 1 : 2 * pair_at + 2]], axis=1)
        gain = jnp.concatenate(
            [loadings_ref[2 * pair_at : 2 * pair_at + 1], loadings_ref[2 * pair_at + 1 : 2 * pair_at + 2]], axis=1
        )
        moved = jnp.transpose(shifted(filtered_rows, 255 - amount) * gain)
        model_high, model_low = split(shifted(plain_rows, 255 - amount) * gain)
        high, low = split(moved)
        stacks.append((high, low))
        quad = quad + jnp.dot(
            jnp.concatenate([high, low], axis=0),
            jnp.concatenate([model_high, model_low], axis=1),
            preferred_element_type=F32,
        )
    corner = quad[:128, :128] + quad[:128, 128:] + quad[128:, :128]
    gram_own = corner[:64] + half_turn(corner[64:])
    left32 = lax.broadcasted_iota(jnp.int32, (32, LANES), 1) < 64
    gram_send[0] = jnp.where(left32, gram_own[:32], half_turn(gram_own[32:]))
    core_copy = remote(gram_send.at[0], gram_core, gram_sems.at[0], gram_sems.at[1], partner)
    core_copy.start()

    for run in range(RUNS):
        high, low = stacks[run // 2]
        cut = slice((run % 2) * 64, (run % 2) * 64 + 64)
        both = jnp.dot(
            jnp.concatenate([high[cut], low[cut]], axis=0), samples[run], preferred_element_type=F32
        )
        numer = numer + both[:64] + both[64:]
    by_channel = jnp.transpose(numer).reshape(FREQ, 2, 8, COMP)
    num_send[...] = jnp.concatenate([by_channel[:, 0], by_channel[:, 1]], axis=2)

    def num_copy(step):
        to = (freq + step) % FREQ
        return remote(num_send.at[to], num_recv.at[freq], num_sems.at[step], num_recv_sems.at[step], (to, mz))

    def send_num(step, carry):
        num_copy(step).start()
        return carry

    core_copy.wait()
    gram_send[1] = gram_send[0] + gram_core[...]
    x_copies = []
    for step in range(1, 4):
        copy = remote(
            gram_send.at[1],
            gram_x.at[step - 1],
            gram_sems.at[1 + step],
            gram_sems.at[4 + step],
            at((x + step) % 4, y, z_mine, core),
        )
        copy.start()
        x_copies.append(copy)
    lax.fori_loop(1, FREQ, send_num, 0)
    for copy in x_copies:
        copy.wait()
    gram_send[2] = (gram_send[1] + gram_x[0]) + (gram_x[1] + gram_x[2])
    z_grams = []
    for step in range(1, 4):
        copy = remote(
            gram_send.at[2],
            gram_z.at[step - 1],
            gram_sems.at[7 + step],
            gram_sems.at[10 + step],
            at(x, y, z_hi * 4 + (z_lo + step) % 4, core),
        )
        copy.start()
        z_grams.append(copy)
    for copy in z_grams:
        copy.wait()
    packed = (gram_send[2] + gram_z[0]) + (gram_z[1] + gram_z[2])

    row64 = lax.broadcasted_iota(jnp.int32, (COMP, LANES), 0)
    lane64 = lax.broadcasted_iota(jnp.int32, (COMP, LANES), 1)
    unit = (lane64 == row64 + COMP).astype(F32)
    matrix = jnp.where(lane64 < COMP, jnp.concatenate([packed, half_turn(packed)], axis=0), unit)
    for step in range(COMP):
        pivot = matrix[step : step + 1, :]
        scaled = pivot * (1.0 / matrix[step : step + 1, step : step + 1])
        matrix = jnp.where(row64 == step, scaled, matrix - matrix[:, step : step + 1] * scaled)
    inverse = matrix[:, COMP:]

    def wait_num(step, carry):
        source = (freq + FREQ - step) % FREQ
        copy = remote(num_send.at[source], num_recv.at[source], num_sems.at[step], num_recv_sems.at[step], (source, mz))
        copy.wait_recv()
        return carry

    lax.fori_loop(1, FREQ, wait_num, 0)
    num_recv[freq] = num_send[freq]
    summed = jnp.sum(num_recv[...], axis=0)
    own_channels = jnp.concatenate([summed[:, :64], summed[:, 64:]], axis=0)
    out_ref[...] = lax.dot_general(
        inverse, own_channels, (((1,), (1,)), ((), ())), precision=HIGHEST, preferred_element_type=F32
    )

    @pl.when(z_hi == core)
    def _():
        for copy in z_copies:
            copy.wait_send()

    for copy in p_copies + q_copies + swaps:
        copy.wait_send()

    def drain(step, carry):
        num_copy(step).wait_send()
        return carry

    lax.fori_loop(1, FREQ, drain, 0)


def on_device(intensity, elution, loadings, shifts, bin_weight):
    first, turn, last = transform_tables()
    vmem = pl.BlockSpec(memory_space=pltpu.VMEM)
    dma = pltpu.SemaphoreType.DMA
    return pl.pallas_call(
        kernel,
        out_shape=jax.ShapeDtypeStruct((COMP, OWN), F32),
        in_specs=[vmem] * 7 + [pl.BlockSpec(memory_space=pl.ANY)],
        out_specs=vmem,
        scratch_shapes=[
            pltpu.VMEM((RUNS, BLOCK, CHANNELS), BF16),
            pltpu.VMEM((24, LANES), F32),
            pltpu.VMEM((24, LANES), F32),
            pltpu.VMEM((2, 4, 4, 4, 24, LANES), F32),
            pltpu.VMEM((LENGTH + WINDOW, LANES), BF16),
            pltpu.VMEM((3, 16, LANES), F32),
            pltpu.VMEM((LANES, LANES), F32),
            pltpu.VMEM((2, ROWS, LANES, LANES), BF16),
            pltpu.VMEM((512, 256), F32),
            pltpu.VMEM((2, WINDOW, LANES), F32),
            pltpu.VMEM((3, 32, LANES), F32),
            pltpu.VMEM((32, LANES), F32),
            pltpu.VMEM((3, 32, LANES), F32),
            pltpu.VMEM((3, 32, LANES), F32),
            pltpu.VMEM((FREQ, 8, LANES), F32),
            pltpu.VMEM((FREQ, 8, LANES), F32),
            dma,
            dma((2,)),
            dma((7,)),
            dma((4,)),
            dma((3,)),
            dma((3,)),
            dma((3,)),
            dma((3,)),
            dma((7,)),
            dma((7,)),
            dma((14,)),
            dma((FREQ,)),
            dma((FREQ,)),
        ],
        compiler_params=pltpu.CompilerParams(
            collective_id=0, has_side_effects=True, vmem_limit_bytes=48 * 1024 * 1024
        ),
    )(elution, loadings, shifts, bin_weight.reshape(ROWS, LANES), first, turn, last, intensity)


def solution(mesh):
    in_specs = (P(None, "freq", "mz"), P(("freq", "mz"), None), P(), P(), P())
    out_specs = P(None, ("mz", "freq"))
    return jax.shard_map(on_device, mesh=mesh, in_specs=in_specs, out_specs=out_specs, check_vma=False)
```

```python
import functools
import math

import jax
import jax.numpy as jnp
import numpy as np
from jax import lax
from jax.experimental import pallas as pl
from jax.experimental.pallas import tpu as pltpu
from jax.sharding import PartitionSpec as P

MESH = pl.DeviceIdType.MESH
HIGHEST = lax.Precision.HIGHEST
F32 = jnp.float32
BF16 = jnp.bfloat16

LENGTH = 6144
ROWS = 48
LANES = 128
RUNS = 8
COMP = 64
BLOCK = 192
CHANNELS = 512
FREQ = 32
OWN = 16
WINDOW = 512


def transform_tables():
    x48 = np.arange(ROWS)
    b128 = np.arange(LANES)
    inner = 2.0 * np.pi / ROWS * ((x48[:, None] * x48[None, :]) % ROWS)
    middle = 2.0 * np.pi / LENGTH * ((x48[:, None] * b128[None, :]) % LENGTH)
    outer = 2.0 * np.pi / LANES * ((b128[:, None] * b128[None, :]) % LANES)
    first = np.concatenate([np.cos(inner), np.sin(inner)], axis=0)
    first = np.pad(first, ((0, 0), (0, LANES - ROWS)))
    turn = np.concatenate([np.cos(middle), np.sin(middle)], axis=0)
    last = np.concatenate([np.cos(outer), -np.sin(outer)], axis=0) / LENGTH
    return jnp.asarray(np.concatenate([first, turn, last], axis=0).astype(np.float32))


def split(value):
    high = value.astype(BF16)
    low = (value - high.astype(F32)).astype(BF16)
    return high, low


def half_turn(value):
    return pltpu.roll(value, 64, 1)


def lag_weights(weight, first, turn, last, flip):
    inner = jnp.dot(first, weight, precision=HIGHEST, preferred_element_type=F32)
    cos_part, sin_part = inner[:ROWS], inner[ROWS:]
    tcos, tsin = turn[:ROWS], turn[ROWS:]
    real = cos_part * tcos - sin_part * tsin
    imag = cos_part * tsin + sin_part * tcos
    both = jnp.concatenate([real, imag], axis=1)
    by_x = jnp.dot(both, last, precision=HIGHEST, preferred_element_type=F32)
    padded = jnp.concatenate([by_x, jnp.zeros((LANES - ROWS, LANES), F32)], axis=0)
    flip[...] = jnp.transpose(padded)
    lane = lax.broadcasted_iota(jnp.int32, (16, LANES), 1)

    def part(index, shift):
        rows = flip[pl.ds(index, 16, stride=8), :]
        return rows if shift == 0 else pltpu.roll(rows, shift, 1)

    first_row = jnp.where(lane < 48, part(0, 0), jnp.where(lane < 96, part(1, 48), part(2, 96)))
    second_row = jnp.where(
        lane < 16, part(2, 96), jnp.where(lane < 64, part(3, 16), jnp.where(lane < 112, part(4, 64), part(5, 112)))
    )
    third_row = jnp.where(lane < 32, part(5, 112), jnp.where(lane < 80, part(6, 32), part(7, 80)))
    return first_row, second_row, third_row


def shifted(window, amount):
    value = window
    for bit in (128, 64, 32, 16, 8):
        rows = BLOCK + bit
        value = jnp.where((amount & bit) != 0, value[bit : bit + rows], value[0:rows])
    for bit in (4, 2, 1):
        value = jnp.where((amount & bit) != 0, pltpu.roll(value, value.shape[0] - bit, 0), value)
    return pltpu.roll(value, value.shape[0] - 1, 0)[0:BLOCK]


def kernel(
    elution_hbm,
    loadings_hbm,
    shifts_hbm,
    weight_hbm,
    tables_hbm,
    intensity_hbm,
    out_ref,
    elution_ref,
    loadings_ref,
    shifts_ref,
    weight_ref,
    tables_ref,
    samples,
    mine,
    theirs,
    blocks,
    profile,
    lags,
    flip,
    toeplitz,
    total,
    window,
    gram_send,
    gram_core,
    gram_x,
    gram_z,
    num_send,
    num_recv,
    load_sems,
    pair_sem,
    z_send,
    z_recv,
    p_send,
    p_recv,
    q_send,
    q_recv,
    swap_send,
    swap_recv,
    gram_sems,
    num_sems,
    num_recv_sems,
):
    freq = lax.axis_index("freq")
    mz = lax.axis_index("mz")
    core = freq % 2
    z_lo = (freq // 2) % 4
    x = freq // 8
    y = mz // 2
    z_hi = mz % 2
    p = x * (1 - core) + y * core
    q = y * (1 - core) + x * core

    def at(x_to, y_to, z_to, core_to):
        return (x_to * 8 + (z_to % 4) * 2 + core_to, y_to * 2 + z_to // 4)

    def at_pq(p_to, q_to):
        return at(p_to * (1 - core) + q_to * core, q_to * (1 - core) + p_to * core, z_hi * 4 + z_lo, core)

    partner = (freq + 1 - 2 * core, mz)
    z_mine = z_hi * 4 + z_lo

    loads = [
        pltpu.make_async_copy(source, target, load_sems.at[index])
        for index, (source, target) in enumerate(
            (
                (elution_hbm, elution_ref),
                (weight_hbm, weight_ref),
                (tables_hbm, tables_ref),
                (loadings_hbm, loadings_ref),
                (shifts_hbm, shifts_ref),
                (intensity_hbm, samples),
            )
        )
    ]
    for load in loads:
        load.start()
    barrier = pltpu.get_barrier_semaphore()

    def greet(step, carry):
        pl.semaphore_signal(barrier, inc=1, device_id=((freq + step) % FREQ, mz), device_id_type=MESH)
        return carry

    lax.fori_loop(1, FREQ, greet, 0)
    for step in range(1, 4):
        pl.semaphore_signal(
            barrier, inc=1, device_id=(freq, ((y + step) % 4) * 2 + z_hi), device_id_type=MESH
        )
    for step in range(4):
        pl.semaphore_signal(
            barrier, inc=1, device_id=at(x, y, (1 - z_hi) * 4 + step, core), device_id_type=MESH
        )

    loads[0].wait()
    own_rows = elution_ref[...]
    mine[...] = jnp.concatenate([own_rows, own_rows], axis=1)

    loads[1].wait()
    loads[2].wait()
    lag_rows = lag_weights(
        weight_ref[...], tables_ref[:96, :ROWS], tables_ref[96:192], tables_ref[192:448], flip
    )
    for z in range(3):
        lags[z] = lag_rows[z]

    pl.semaphore_wait(barrier, FREQ - 1 + 3 + 4)

    def remote(source, target, send, recv, device):
        return pltpu.make_async_remote_copy(
            src_ref=source, dst_ref=target, send_sem=send, recv_sem=recv, device_id=device, device_id_type=MESH
        )

    pair = remote(mine, theirs, pair_sem.at[0], pair_sem.at[1], partner)
    pair.start()
    pair.wait()
    lane24 = lax.broadcasted_iota(jnp.int32, (24, LANES), 1)
    side = (lane24 // 64) == core
    z_copies = []
    for step in range(1, 8):
        z_to = (z_mine + step) % 8
        z_copies.append(
            remote(
                blocks.at[core, q, p, z_lo],
                blocks.at[core, q, p, z_lo],
                z_send.at[step - 1],
                z_recv.at[z_lo],
                at(x, y, z_to, core),
            )
        )

    @pl.when(z_hi == core)
    def _():
        blocks[core, q, p, z_lo] = jnp.where(side, mine[...], theirs[...])
        for copy in z_copies:
            copy.start()

    row = lax.broadcasted_iota(jnp.int32, (LANES, LANES), 0)
    lane = lax.broadcasted_iota(jnp.int32, (LANES, LANES), 1)
    upper = lane >= row

    def turned(z, g):
        base = jnp.broadcast_to(lags[z, pl.ds(g, 1), :], (LANES, LANES))
        return pltpu.roll(base, 0, 1, stride=1, stride_axis=0)

    def build(g, before):
        for z in range(3):
            here = turned(z, g)
            high, low = split(jnp.where(upper, here, before))
            toeplitz[0, 3 * g + z] = high
            toeplitz[1, 3 * g + z] = low
            before = here
        return before

    lax.fori_loop(0, 16, build, turned(2, 15))

    for source in range(4):

        @pl.when(jnp.logical_or(z_hi != core, z_lo != source))
        def _(source=source):
            spot = blocks.at[core, q, p, source]
            remote(spot, spot, z_send.at[0], z_recv.at[source], partner).wait_recv()

    swaps = [remote(blocks.at[core, q, p], blocks.at[core, q, p], swap_send.at[0], swap_recv.at[0], partner)]
    swaps[0].start()
    p_copies = []
    for step in range(1, 4):
        copy = remote(
            blocks.at[core, q, p],
            blocks.at[core, q, p],
            p_send.at[step - 1],
            p_recv.at[step - 1],
            at_pq((p + step) % 4, q),
        )
        copy.start()
        p_copies.append(copy)
    for step in range(1, 4):
        spot = blocks.at[core, q, (p + 4 - step) % 4]
        remote(spot, spot, p_send.at[step - 1], p_recv.at[step - 1], partner).wait_recv()
        swap = remote(spot, spot, swap_send.at[step], swap_recv.at[step], partner)
        swap.start()
        swaps.append(swap)
    q_copies = []
    for step in range(1, 4):
        copy = remote(
            blocks.at[core, q], blocks.at[core, q], q_send.at[step - 1], q_recv.at[step - 1], at_pq(p, (q + step) % 4)
        )
        copy.start()
        q_copies.append(copy)
    for step in range(1, 4):
        spot = blocks.at[core, (q + 4 - step) % 4]
        remote(spot, spot, q_send.at[step - 1], q_recv.at[step - 1], partner).wait_recv()
        swap = remote(spot, spot, swap_send.at[3 + step], swap_recv.at[3 + step], partner)
        swap.start()
        swaps.append(swap)
    other = 1 - core
    spot = blocks.at[other, p, q]
    remote(spot, spot, swap_send.at[0], swap_recv.at[0], partner).wait_recv()
    for step in range(1, 4):
        spot = blocks.at[other, p, (q + 4 - step) % 4]
        remote(spot, spot, swap_send.at[step], swap_recv.at[step], partner).wait_recv()
    for step in range(1, 4):
        spot = blocks.at[other, (p + 4 - step) % 4]
        remote(spot, spot, swap_send.at[3 + step], swap_recv.at[3 + step], partner).wait_recv()

    left = lax.broadcasted_iota(jnp.int32, (24, LANES), 1) < 64

    def unpack(index, carry):
        x_at = index // 4
        zl_at = index % 4
        low_rows, high_rows = [], []
        for y_at in range(4):
            for zh_at in range(2):
                if zh_at == 0:
                    block = blocks[0, y_at, x_at, zl_at]
                else:
                    block = blocks[1, x_at, y_at, zl_at]
                rounded = block.astype(BF16).astype(F32)
                rest = block - rounded
                low_rows.append(jnp.where(left, rounded, half_turn(rest)))
                high_rows.append(jnp.where(left, half_turn(rounded), rest))
        start = pl.multiple_of(index * 384, 128)
        profile[pl.ds(start, BLOCK), :] = jnp.concatenate(low_rows, axis=0).astype(BF16)
        profile[pl.ds(start + BLOCK, BLOCK), :] = jnp.concatenate(high_rows, axis=0).astype(BF16)
        return carry

    lax.fori_loop(0, 16, unpack, 0)
    profile[LENGTH : LENGTH + WINDOW, :] = profile[0:WINDOW, :]

    begin = ((freq * 3 + 96 - 4) // 2) % ROWS
    total[...] = jnp.zeros_like(total)

    def filtered(tile, carry):
        pieces = []
        for part in range(2):
            for row_block in (0, 2):
                spot = 2 * tile + 2 * ROWS - begin - row_block
                pieces.append(
                    jnp.concatenate([toeplitz[part, spot % ROWS], toeplitz[part, (spot + 1) % ROWS]], axis=1)
                )
        start = pl.multiple_of(tile * 256, 128)
        rows = jnp.concatenate([profile[pl.ds(start, 256), :], profile[pl.ds(start + 128, 256), :]], axis=1)
        total[...] += jnp.dot(jnp.concatenate(pieces, axis=0), rows, preferred_element_type=F32)
        return carry

    lax.fori_loop(0, 24, filtered, 0)
    for row_block in range(4):
        base = (row_block // 2) * 128
        cut = pl.ds((row_block % 2) * 128, 128)
        value = total[pl.ds(base, 128), cut] + total[pl.ds(256 + base, 128), cut]
        window[0, pl.ds(row_block * 128, 128), :] = value + half_turn(value)
        start = pl.multiple_of(begin * 128 + row_block * 128, 128)
        value = profile[pl.ds(start, 128), :].astype(F32)
        window[1, pl.ds(row_block * 128, 128), :] = value + half_turn(value)

    skip = pl.multiple_of((freq % 2) * 64, 64)
    for load in loads[3:]:
        load.wait()
    filtered_rows = window[0, pl.ds(skip, 448), :]
    plain_rows = window[1, pl.ds(skip, 448), :]
    quad = jnp.zeros((256, 256), F32)
    numer = jnp.zeros((COMP, CHANNELS), F32)
    stacks = []
    for pair_at in range(RUNS // 2):
        amount = jnp.concatenate([shifts_ref[2 * pair_at : 2 * pair_at + 1], shifts_ref[2 * pair_at + 1 : 2 * pair_at + 2]], axis=1)
        gain = jnp.concatenate(
            [loadings_ref[2 * pair_at : 2 * pair_at + 1], loadings_ref[2 * pair_at + 1 : 2 * pair_at + 2]], axis=1
        )
        moved = jnp.transpose(shifted(filtered_rows, 255 - amount) * gain)
        model_high, model_low = split(shifted(plain_rows, 255 - amount) * gain)
        high, low = split(moved)
        stacks.append((high, low))
        quad = quad + jnp.dot(
            jnp.concatenate([high, low], axis=0),
            jnp.concatenate([model_high, model_low], axis=1),
            preferred_element_type=F32,
        )
    corner = quad[:128, :128] + quad[:128, 128:] + quad[128:, :128]
    gram_own = corner[:64] + half_turn(corner[64:])
    left32 = lax.broadcasted_iota(jnp.int32, (32, LANES), 1) < 64
    gram_send[0] = jnp.where(left32, gram_own[:32], half_turn(gram_own[32:]))
    core_copy = remote(gram_send.at[0], gram_core, gram_sems.at[0], gram_sems.at[1], partner)
    core_copy.start()

    for run in range(RUNS):
        high, low = stacks[run // 2]
        cut = slice((run % 2) * 64, (run % 2) * 64 + 64)
        both = jnp.dot(
            jnp.concatenate([high[cut], low[cut]], axis=0), samples[run], preferred_element_type=F32
        )
        numer = numer + both[:64] + both[64:]
    by_channel = jnp.transpose(numer).reshape(FREQ, 2, 8, COMP)
    num_send[...] = jnp.concatenate([by_channel[:, 0], by_channel[:, 1]], axis=2)

    def num_copy(step):
        to = (freq + step) % FREQ
        return remote(num_send.at[to], num_recv.at[freq], num_sems.at[step], num_recv_sems.at[step], (to, mz))

    def send_num(step, carry):
        num_copy(step).start()
        return carry

    core_copy.wait()
    gram_send[1] = gram_send[0] + gram_core[...]
    x_copies = []
    for step in range(1, 4):
        copy = remote(
            gram_send.at[1],
            gram_x.at[step - 1],
            gram_sems.at[1 + step],
            gram_sems.at[4 + step],
            at((x + step) % 4, y, z_mine, core),
        )
        copy.start()
        x_copies.append(copy)
    for copy in x_copies:
        copy.wait()
    gram_send[2] = (gram_send[1] + gram_x[0]) + (gram_x[1] + gram_x[2])
    z_grams = []
    for step in range(1, 4):
        copy = remote(
            gram_send.at[2],
            gram_z.at[step - 1],
            gram_sems.at[7 + step],
            gram_sems.at[10 + step],
            at(x, y, z_hi * 4 + (z_lo + step) % 4, core),
        )
        copy.start()
        z_grams.append(copy)
    lax.fori_loop(1, FREQ, send_num, 0)
    for copy in z_grams:
        copy.wait()
    packed = (gram_send[2] + gram_z[0]) + (gram_z[1] + gram_z[2])

    row64 = lax.broadcasted_iota(jnp.int32, (COMP, LANES), 0)
    lane64 = lax.broadcasted_iota(jnp.int32, (COMP, LANES), 1)
    unit = (lane64 == row64 + COMP).astype(F32)
    matrix = jnp.where(lane64 < COMP, jnp.concatenate([packed, half_turn(packed)], axis=0), unit)
    for step in range(0, COMP, 2):
        one = jnp.broadcast_to(matrix[:, step : step + 1], matrix.shape)
        two = jnp.broadcast_to(matrix[:, step + 1 : step + 2], matrix.shape)
        top, low = matrix[step : step + 1], matrix[step + 1 : step + 2]
        one_top, one_low = one[step : step + 1], one[step + 1 : step + 2]
        two_top, two_low = two[step : step + 1], two[step + 1 : step + 2]
        scale = 1.0 / (one_top * two_low - two_top * one_low)
        top_new = (two_low * top - two_top * low) * scale
        low_new = (one_top * low - one_low * top) * scale
        rest = matrix - one * top_new - two * low_new
        matrix = jnp.where(row64 == step, top_new, jnp.where(row64 == step + 1, low_new, rest))
    inverse = matrix[:, COMP:]

    def wait_num(step, carry):
        source = (freq + FREQ - step) % FREQ
        copy = remote(num_send.at[source], num_recv.at[source], num_sems.at[step], num_recv_sems.at[step], (source, mz))
        copy.wait_recv()
        return carry

    lax.fori_loop(1, FREQ, wait_num, 0)
    num_recv[freq] = num_send[freq]
    summed = jnp.sum(num_recv[...], axis=0)
    own_channels = jnp.concatenate([summed[:, :64], summed[:, 64:]], axis=0)
    out_ref[...] = lax.dot_general(
        own_channels, inverse, (((1,), (1,)), ((), ())), precision=HIGHEST, preferred_element_type=F32
    )

    @pl.when(z_hi == core)
    def _():
        for copy in z_copies:
            copy.wait_send()

    for copy in p_copies + q_copies + swaps:
        copy.wait_send()

    def drain(step, carry):
        num_copy(step).wait_send()
        return carry

    lax.fori_loop(1, FREQ, drain, 0)


def on_device(intensity, elution, loadings, shifts, bin_weight):
    vmem = pl.BlockSpec(memory_space=pltpu.VMEM)
    dma = pltpu.SemaphoreType.DMA
    by_channel = pl.pallas_call(
        kernel,
        out_shape=jax.ShapeDtypeStruct((OWN, COMP), F32),
        in_specs=[pl.BlockSpec(memory_space=pltpu.HBM)] * 6,
        out_specs=vmem,
        scratch_shapes=[
            pltpu.VMEM((24, COMP), F32),
            pltpu.VMEM((RUNS, COMP), F32),
            pltpu.VMEM((RUNS, COMP), jnp.int32),
            pltpu.VMEM((ROWS, LANES), F32),
            pltpu.VMEM((448, LANES), F32),
            pltpu.VMEM((RUNS, BLOCK, CHANNELS), BF16),
            pltpu.VMEM((24, LANES), F32),
            pltpu.VMEM((24, LANES), F32),
            pltpu.VMEM((2, 4, 4, 4, 24, LANES), F32),
            pltpu.VMEM((LENGTH + WINDOW, LANES), BF16),
            pltpu.VMEM((3, 16, LANES), F32),
            pltpu.VMEM((LANES, LANES), F32),
            pltpu.VMEM((2, ROWS, LANES, LANES), BF16),
            pltpu.VMEM((512, 256), F32),
            pltpu.VMEM((2, WINDOW, LANES), F32),
            pltpu.VMEM((3, 32, LANES), F32),
            pltpu.VMEM((32, LANES), F32),
            pltpu.VMEM((3, 32, LANES), F32),
            pltpu.VMEM((3, 32, LANES), F32),
            pltpu.VMEM((FREQ, 8, LANES), F32),
            pltpu.VMEM((FREQ, 8, LANES), F32),
            dma((6,)),
            dma((2,)),
            dma((7,)),
            dma((4,)),
            dma((3,)),
            dma((3,)),
            dma((3,)),
            dma((3,)),
            dma((7,)),
            dma((7,)),
            dma((14,)),
            dma((FREQ,)),
            dma((FREQ,)),
        ],
        compiler_params=pltpu.CompilerParams(
            collective_id=0, has_side_effects=True, vmem_limit_bytes=67043328
        ),
    )(elution, loadings, shifts, bin_weight.reshape(ROWS, LANES), transform_tables(), intensity)
    return by_channel.T


def solution(mesh):
    in_specs = (P(None, "freq", "mz"), P(("freq", "mz"), None), P(), P(), P())
    out_specs = P(None, ("mz", "freq"))
    return jax.shard_map(on_device, mesh=mesh, in_specs=in_specs, out_specs=out_specs, check_vma=False)
```

```python
import functools
import math

import jax
import jax.numpy as jnp
import numpy as np
from jax import lax
from jax.experimental import pallas as pl
from jax.experimental.pallas import tpu as pltpu
from jax.sharding import PartitionSpec as P

MESH = pl.DeviceIdType.MESH
HIGHEST = lax.Precision.HIGHEST
F32 = jnp.float32
BF16 = jnp.bfloat16

LENGTH = 6144
ROWS = 48
LANES = 128
RUNS = 8
COMP = 64
BLOCK = 192
CHANNELS = 512
FREQ = 32
OWN = 16
SLAB = 1536
WINDOW = 512


def transform_tables():
    x48 = np.arange(ROWS)
    b128 = np.arange(LANES)
    inner = 2.0 * np.pi / ROWS * ((x48[:, None] * x48[None, :]) % ROWS)
    middle = 2.0 * np.pi / LENGTH * ((x48[:, None] * b128[None, :]) % LENGTH)
    outer = 2.0 * np.pi / LANES * ((b128[:, None] * b128[None, :]) % LANES)
    first = np.concatenate([np.cos(inner), np.sin(inner)], axis=0)
    first = np.pad(first, ((0, 0), (0, LANES - ROWS)))
    turn = np.concatenate([np.cos(middle), np.sin(middle)], axis=0)
    last = np.concatenate([np.cos(outer), -np.sin(outer)], axis=0) / LENGTH
    return jnp.asarray(np.concatenate([first, turn, last], axis=0).astype(np.float32))


def split(value):
    high = value.astype(BF16)
    low = (value - high.astype(F32)).astype(BF16)
    return high, low


def half_turn(value):
    return pltpu.roll(value, 64, 1)


def lag_weights(weight, first, turn, last, flip):
    inner = jnp.dot(first, weight, precision=HIGHEST, preferred_element_type=F32)
    cos_part, sin_part = inner[:ROWS], inner[ROWS:]
    tcos, tsin = turn[:ROWS], turn[ROWS:]
    real = cos_part * tcos - sin_part * tsin
    imag = cos_part * tsin + sin_part * tcos
    both = jnp.concatenate([real, imag], axis=1)
    by_x = jnp.dot(both, last, precision=HIGHEST, preferred_element_type=F32)
    padded = jnp.concatenate([by_x, jnp.zeros((LANES - ROWS, LANES), F32)], axis=0)
    flip[...] = jnp.transpose(padded)
    lane = lax.broadcasted_iota(jnp.int32, (16, LANES), 1)

    def part(index, shift):
        rows = flip[pl.ds(index, 16, stride=8), :]
        return rows if shift == 0 else pltpu.roll(rows, shift, 1)

    first_row = jnp.where(lane < 48, part(0, 0), jnp.where(lane < 96, part(1, 48), part(2, 96)))
    second_row = jnp.where(
        lane < 16, part(2, 96), jnp.where(lane < 64, part(3, 16), jnp.where(lane < 112, part(4, 64), part(5, 112)))
    )
    third_row = jnp.where(lane < 32, part(5, 112), jnp.where(lane < 80, part(6, 32), part(7, 80)))
    return first_row, second_row, third_row


def shifted(window, amount):
    value = window
    for bit in (128, 64, 32, 16, 8):
        rows = BLOCK + bit
        value = jnp.where((amount & bit) != 0, value[bit : bit + rows], value[0:rows])
    for bit in (4, 2, 1):
        value = jnp.where((amount & bit) != 0, pltpu.roll(value, value.shape[0] - bit, 0), value)
    return pltpu.roll(value, value.shape[0] - 1, 0)[0:BLOCK]


def kernel(
    elution_hbm,
    loadings_hbm,
    shifts_hbm,
    weight_hbm,
    tables_hbm,
    intensity_hbm,
    out_ref,
    elution_ref,
    loadings_ref,
    shifts_ref,
    weight_ref,
    tables_ref,
    samples,
    mine,
    theirs,
    blocks,
    profile,
    slab,
    lags,
    flip,
    toeplitz,
    total,
    window,
    gram_send,
    gram_core,
    gram_x,
    gram_z,
    num_send,
    num_recv,
    load_sems,
    pair_sem,
    z_send,
    z_recv,
    second_send,
    third_send,
    own_recv,
    swap_send,
    swap_recv,
    gram_sems,
    num_sems,
    num_recv_sems,
):
    freq = lax.axis_index("freq")
    mz = lax.axis_index("mz")
    core = freq % 2
    z_lo = (freq // 2) % 4
    x = freq // 8
    y = mz // 2
    z_hi = mz % 2
    p = x * (1 - core) + y * core
    q = y * (1 - core) + x * core

    def at(x_to, y_to, z_to, core_to):
        return (x_to * 8 + (z_to % 4) * 2 + core_to, y_to * 2 + z_to // 4)

    def at_pq(p_to, q_to):
        return at(p_to * (1 - core) + q_to * core, q_to * (1 - core) + p_to * core, z_hi * 4 + z_lo, core)

    partner = (freq + 1 - 2 * core, mz)
    z_mine = z_hi * 4 + z_lo

    loads = [
        pltpu.make_async_copy(source, target, load_sems.at[index])
        for index, (source, target) in enumerate(
            (
                (elution_hbm, elution_ref),
                (weight_hbm, weight_ref),
                (tables_hbm, tables_ref),
                (loadings_hbm, loadings_ref),
                (shifts_hbm, shifts_ref),
                (intensity_hbm, samples),
            )
        )
    ]
    for load in loads:
        load.start()
    barrier = pltpu.get_barrier_semaphore()

    def greet(step, carry):
        pl.semaphore_signal(barrier, inc=1, device_id=((freq + step) % FREQ, mz), device_id_type=MESH)
        return carry

    lax.fori_loop(1, FREQ, greet, 0)
    for step in range(1, 4):
        pl.semaphore_signal(
            barrier, inc=1, device_id=(freq, ((y + step) % 4) * 2 + z_hi), device_id_type=MESH
        )
    for step in range(4):
        pl.semaphore_signal(
            barrier, inc=1, device_id=at(x, y, (1 - z_hi) * 4 + step, core), device_id_type=MESH
        )

    loads[0].wait()
    own_rows = elution_ref[...]
    mine[...] = jnp.concatenate([own_rows, own_rows], axis=1)

    loads[1].wait()
    loads[2].wait()
    lag_rows = lag_weights(
        weight_ref[...], tables_ref[:96, :ROWS], tables_ref[96:192], tables_ref[192:448], flip
    )
    for z in range(3):
        lags[z] = lag_rows[z]

    pl.semaphore_wait(barrier, FREQ - 1 + 3 + 4)

    def remote(source, target, send, recv, device):
        return pltpu.make_async_remote_copy(
            src_ref=source, dst_ref=target, send_sem=send, recv_sem=recv, device_id=device, device_id_type=MESH
        )

    pair = remote(mine, theirs, pair_sem.at[0], pair_sem.at[1], partner)
    pair.start()
    pair.wait()
    lane24 = lax.broadcasted_iota(jnp.int32, (24, LANES), 1)
    side = (lane24 // 64) == core
    z_copies = []
    for step in range(1, 8):
        own = blocks.at[core, x, y, z_lo]
        z_to = (z_mine + step) % 8
        z_copies.append(remote(own, own, z_send.at[step - 1], z_recv.at[z_lo], at(x, y, z_to, core)))

    @pl.when(z_hi == core)
    def _():
        blocks[core, x, y, z_lo] = jnp.where(side, mine[...], theirs[...])
        for copy in z_copies:
            copy.start()

    row = lax.broadcasted_iota(jnp.int32, (LANES, LANES), 0)
    lane = lax.broadcasted_iota(jnp.int32, (LANES, LANES), 1)
    upper = lane >= row

    def turned(z, g):
        base = jnp.broadcast_to(lags[z, pl.ds(g, 1), :], (LANES, LANES))
        return pltpu.roll(base, 0, 1, stride=1, stride_axis=0)

    def build(g, before):
        for z in range(3):
            here = turned(z, g)
            high, low = split(jnp.where(upper, here, before))
            toeplitz[0, 3 * g + z] = high
            toeplitz[1, 3 * g + z] = low
            before = here
        return before

    lax.fori_loop(0, 16, build, turned(2, 15))

    for source in range(4):

        @pl.when(jnp.logical_or(z_hi != core, z_lo != source))
        def _(source=source):
            spot = blocks.at[core, x, y, source]
            remote(spot, spot, z_send.at[0], z_recv.at[source], partner).wait_recv()

    def offsets(a, b):
        return (a * (1 - core) + b * core, b * (1 - core) + a * core)

    def piece(colour, dx, dy):
        return blocks.at[colour, (x + dx) % 4, (y + dy) % 4]

    sent = []

    def begin_copy(source, send, recv, device):
        copy = remote(source, source, send, recv, device)
        copy.start()
        sent.append(copy)

    def swap(dx, dy):
        begin_copy(piece(core, dx, dy), swap_send.at[dx, dy], swap_recv.at[dx, dy], partner)

    def third(a):
        for step in (1, 3, 2):
            dx, dy = offsets(a, 4 - step)
            begin_copy(
                piece(core, *offsets(a, 0)),
                third_send.at[a, step - 1],
                own_recv.at[dx, dy],
                at_pq(p, (q + step) % 4),
            )

    def arrived(dx, dy):
        spot = piece(core, dx, dy)
        remote(spot, spot, swap_send.at[0, 0], own_recv.at[dx, dy], partner).wait_recv()
        swap(dx, dy)

    def swapped(dx, dy):
        spot = piece(1 - core, dx, dy)
        remote(spot, spot, swap_send.at[0, 0], swap_recv.at[dx, dy], partner).wait_recv()

    for step in (1, 3, 2):
        dx, dy = offsets(4 - step, 0)
        begin_copy(
            piece(core, 0, 0), second_send.at[step - 1], own_recv.at[dx, dy], at_pq((p + step) % 4, q)
        )
    third(0)
    swap(0, 0)
    for a in (3, 1):
        arrived(*offsets(a, 0))
        third(a)
    for b in (3, 1):
        arrived(*offsets(0, b))
    arrived(*offsets(2, 0))
    third(2)
    arrived(*offsets(0, 2))

    left = lax.broadcasted_iota(jnp.int32, (24, LANES), 1) < 64
    begin = ((freq * 3 + 96 - 4) // 2) % ROWS
    slab[0:128, :] = jnp.zeros((128, LANES), BF16)
    slab[128 + SLAB : 256 + SLAB, :] = jnp.zeros((128, LANES), BF16)

    def unpack(dx):
        x_at = (x + dx) % 4

        def unpack_one(zl_at, carry):
            low_rows, high_rows = [], []
            for y_at in range(4):
                for colour in range(2):
                    block = blocks[colour, x_at, y_at, zl_at]
                    rounded = block.astype(BF16).astype(F32)
                    rest = block - rounded
                    low_rows.append(jnp.where(left, rounded, half_turn(rest)))
                    high_rows.append(jnp.where(left, half_turn(rounded), rest))
            rows = jnp.concatenate(low_rows + high_rows, axis=0).astype(BF16)
            start = pl.multiple_of(zl_at * 384, 128)
            slab[pl.ds(128 + start, 384), :] = rows
            profile[pl.ds(pl.multiple_of(x_at * SLAB, 128) + start, 384), :] = rows
            return carry

        lax.fori_loop(0, 4, unpack_one, 0)

    def filtered(dx):
        first = ((x + dx) % 4) * 12 - 1 + 2 * ROWS - begin
        lines = []
        for part in range(2):
            for row_block in (0, 2):
                lines.append(
                    jnp.concatenate(
                        [toeplitz[part, (first + step - row_block) % ROWS] for step in range(13)], axis=1
                    )
                )
        rows = jnp.concatenate([slab[0 : 128 + SLAB, :], slab[128 : 256 + SLAB, :]], axis=1)
        value = jnp.dot(jnp.concatenate(lines, axis=0), rows, preferred_element_type=F32)
        if dx == 0:
            total[...] = value
        else:
            total[...] += value

    for dy in range(4):
        swapped(0, dy)
    unpack(0)
    filtered(0)
    for dy in (3, 1, 2):
        arrived(3, dy)
    for dy in (3, 1, 2):
        arrived(1, dy)
    for dy in range(4):
        swapped(3, dy)
    unpack(3)
    filtered(3)
    for dy in (3, 1, 2):
        arrived(2, dy)
    for dy in range(4):
        swapped(1, dy)
    unpack(1)
    filtered(1)
    for dy in range(4):
        swapped(2, dy)
    unpack(2)
    filtered(2)

    for row_block in range(4):
        base = (row_block // 2) * 128
        cut = pl.ds((row_block % 2) * 128, 128)
        value = total[pl.ds(base, 128), cut] + total[pl.ds(256 + base, 128), cut]
        window[0, pl.ds(row_block * 128, 128), :] = value + half_turn(value)
        start = pl.multiple_of(((begin + row_block) % ROWS) * 128, 128)
        value = profile[pl.ds(start, 128), :].astype(F32)
        window[1, pl.ds(row_block * 128, 128), :] = value + half_turn(value)

    skip = pl.multiple_of((freq % 2) * 64, 64)
    for load in loads[3:]:
        load.wait()
    filtered_rows = window[0, pl.ds(skip, 448), :]
    plain_rows = window[1, pl.ds(skip, 448), :]
    quad = jnp.zeros((256, 256), F32)
    numer = jnp.zeros((COMP, CHANNELS), F32)
    stacks = []
    for pair_at in range(RUNS // 2):
        amount = jnp.concatenate([shifts_ref[2 * pair_at : 2 * pair_at + 1], shifts_ref[2 * pair_at + 1 : 2 * pair_at + 2]], axis=1)
        gain = jnp.concatenate(
            [loadings_ref[2 * pair_at : 2 * pair_at + 1], loadings_ref[2 * pair_at + 1 : 2 * pair_at + 2]], axis=1
        )
        moved = jnp.transpose(shifted(filtered_rows, 255 - amount) * gain)
        model_high, model_low = split(shifted(plain_rows, 255 - amount) * gain)
        high, low = split(moved)
        stacks.append((high, low))
        quad = quad + jnp.dot(
            jnp.concatenate([high, low], axis=0),
            jnp.concatenate([model_high, model_low], axis=1),
            preferred_element_type=F32,
        )
    corner = quad[:128, :128] + quad[:128, 128:] + quad[128:, :128]
    gram_own = corner[:64] + half_turn(corner[64:])
    left32 = lax.broadcasted_iota(jnp.int32, (32, LANES), 1) < 64
    gram_send[0] = jnp.where(left32, gram_own[:32], half_turn(gram_own[32:]))
    core_copy = remote(gram_send.at[0], gram_core, gram_sems.at[0], gram_sems.at[1], partner)
    core_copy.start()

    for run in range(RUNS):
        high, low = stacks[run // 2]
        cut = slice((run % 2) * 64, (run % 2) * 64 + 64)
        both = jnp.dot(
            jnp.concatenate([high[cut], low[cut]], axis=0), samples[run], preferred_element_type=F32
        )
        numer = numer + both[:64] + both[64:]
    by_channel = jnp.transpose(numer).reshape(FREQ, 2, 8, COMP)
    num_send[...] = jnp.concatenate([by_channel[:, 0], by_channel[:, 1]], axis=2)

    def num_copy(step):
        to = (freq + step) % FREQ
        return remote(num_send.at[to], num_recv.at[freq], num_sems.at[step], num_recv_sems.at[step], (to, mz))

    def send_num(step, carry):
        num_copy(step).start()
        return carry

    core_copy.wait()
    gram_send[1] = gram_send[0] + gram_core[...]
    x_copies = []
    for step in range(1, 4):
        copy = remote(
            gram_send.at[1],
            gram_x.at[step - 1],
            gram_sems.at[1 + step],
            gram_sems.at[4 + step],
            at((x + step) % 4, y, z_mine, core),
        )
        copy.start()
        x_copies.append(copy)
    for copy in x_copies:
        copy.wait()
    gram_send[2] = (gram_send[1] + gram_x[0]) + (gram_x[1] + gram_x[2])
    z_grams = []
    for step in range(1, 4):
        copy = remote(
            gram_send.at[2],
            gram_z.at[step - 1],
            gram_sems.at[7 + step],
            gram_sems.at[10 + step],
            at(x, y, z_hi * 4 + (z_lo + step) % 4, core),
        )
        copy.start()
        z_grams.append(copy)
    lax.fori_loop(1, FREQ, send_num, 0)
    for copy in z_grams:
        copy.wait()
    packed = (gram_send[2] + gram_z[0]) + (gram_z[1] + gram_z[2])

    row64 = lax.broadcasted_iota(jnp.int32, (COMP, LANES), 0)
    lane64 = lax.broadcasted_iota(jnp.int32, (COMP, LANES), 1)
    unit = (lane64 == row64 + COMP).astype(F32)
    matrix = jnp.where(lane64 < COMP, jnp.concatenate([packed, half_turn(packed)], axis=0), unit)
    for step in range(0, COMP, 2):
        one = jnp.broadcast_to(matrix[:, step : step + 1], matrix.shape)
        two = jnp.broadcast_to(matrix[:, step + 1 : step + 2], matrix.shape)
        top, low = matrix[step : step + 1], matrix[step + 1 : step + 2]
        one_top, one_low = one[step : step + 1], one[step + 1 : step + 2]
        two_top, two_low = two[step : step + 1], two[step + 1 : step + 2]
        scale = 1.0 / (one_top * two_low - two_top * one_low)
        top_new = (two_low * top - two_top * low) * scale
        low_new = (one_top * low - one_low * top) * scale
        rest = matrix - one * top_new - two * low_new
        matrix = jnp.where(row64 == step, top_new, jnp.where(row64 == step + 1, low_new, rest))
    inverse = matrix[:, COMP:]

    def wait_num(step, carry):
        source = (freq + FREQ - step) % FREQ
        copy = remote(num_send.at[source], num_recv.at[source], num_sems.at[step], num_recv_sems.at[step], (source, mz))
        copy.wait_recv()
        return carry

    lax.fori_loop(1, FREQ, wait_num, 0)
    num_recv[freq] = num_send[freq]
    summed = jnp.sum(num_recv[...], axis=0)
    own_channels = jnp.concatenate([summed[:, :64], summed[:, 64:]], axis=0)
    out_ref[...] = lax.dot_general(
        own_channels, inverse, (((1,), (1,)), ((), ())), precision=HIGHEST, preferred_element_type=F32
    )

    @pl.when(z_hi == core)
    def _():
        for copy in z_copies:
            copy.wait_send()

    for copy in sent:
        copy.wait_send()

    def drain(step, carry):
        num_copy(step).wait_send()
        return carry

    lax.fori_loop(1, FREQ, drain, 0)


def on_device(intensity, elution, loadings, shifts, bin_weight):
    vmem = pl.BlockSpec(memory_space=pltpu.VMEM)
    dma = pltpu.SemaphoreType.DMA
    by_channel = pl.pallas_call(
        kernel,
        out_shape=jax.ShapeDtypeStruct((OWN, COMP), F32),
        in_specs=[pl.BlockSpec(memory_space=pltpu.HBM)] * 6,
        out_specs=vmem,
        scratch_shapes=[
            pltpu.VMEM((24, COMP), F32),
            pltpu.VMEM((RUNS, COMP), F32),
            pltpu.VMEM((RUNS, COMP), jnp.int32),
            pltpu.VMEM((ROWS, LANES), F32),
            pltpu.VMEM((448, LANES), F32),
            pltpu.VMEM((RUNS, BLOCK, CHANNELS), BF16),
            pltpu.VMEM((24, LANES), F32),
            pltpu.VMEM((24, LANES), F32),
            pltpu.VMEM((2, 4, 4, 4, 24, LANES), F32),
            pltpu.VMEM((LENGTH, LANES), BF16),
            pltpu.VMEM((SLAB + 256, LANES), BF16),
            pltpu.VMEM((3, 16, LANES), F32),
            pltpu.VMEM((LANES, LANES), F32),
            pltpu.VMEM((2, ROWS, LANES, LANES), BF16),
            pltpu.VMEM((512, 256), F32),
            pltpu.VMEM((2, WINDOW, LANES), F32),
            pltpu.VMEM((3, 32, LANES), F32),
            pltpu.VMEM((32, LANES), F32),
            pltpu.VMEM((3, 32, LANES), F32),
            pltpu.VMEM((3, 32, LANES), F32),
            pltpu.VMEM((FREQ, 8, LANES), F32),
            pltpu.VMEM((FREQ, 8, LANES), F32),
            dma((6,)),
            dma((2,)),
            dma((7,)),
            dma((4,)),
            dma((3,)),
            dma((4, 3)),
            dma((4, 4)),
            dma((4, 4)),
            dma((4, 4)),
            dma((14,)),
            dma((FREQ,)),
            dma((FREQ,)),
        ],
        compiler_params=pltpu.CompilerParams(
            collective_id=0, has_side_effects=True, vmem_limit_bytes=67043328
        ),
    )(elution, loadings, shifts, bin_weight.reshape(ROWS, LANES), transform_tables(), intensity)
    return by_channel.T


def solution(mesh):
    in_specs = (P(None, "freq", "mz"), P(("freq", "mz"), None), P(), P(), P())
    out_specs = P(None, ("mz", "freq"))
    return jax.shard_map(on_device, mesh=mesh, in_specs=in_specs, out_specs=out_specs, check_vma=False)
```

```python
import functools
import math

import jax
import jax.numpy as jnp
import numpy as np
from jax import lax
from jax.experimental import pallas as pl
from jax.experimental.pallas import tpu as pltpu
from jax.sharding import PartitionSpec as P

MESH = pl.DeviceIdType.MESH
HIGHEST = lax.Precision.HIGHEST
F32 = jnp.float32
BF16 = jnp.bfloat16

LENGTH = 6144
ROWS = 48
LANES = 128
RUNS = 8
COMP = 64
BLOCK = 192
CHANNELS = 512
FREQ = 32
OWN = 16
SLAB = 1536
STEPS = (1, 3, 2)
WINDOW = 512


def transform_tables():
    x48 = np.arange(ROWS)
    b128 = np.arange(LANES)
    inner = 2.0 * np.pi / ROWS * ((x48[:, None] * x48[None, :]) % ROWS)
    middle = 2.0 * np.pi / LENGTH * ((x48[:, None] * b128[None, :]) % LENGTH)
    outer = 2.0 * np.pi / LANES * ((b128[:, None] * b128[None, :]) % LANES)
    first = np.concatenate([np.cos(inner), np.sin(inner)], axis=0)
    first = np.pad(first, ((0, 0), (0, LANES - ROWS)))
    turn = np.concatenate([np.cos(middle), np.sin(middle)], axis=0)
    last = np.concatenate([np.cos(outer), -np.sin(outer)], axis=0) / LENGTH
    return jnp.asarray(np.concatenate([first, turn, last], axis=0).astype(np.float32))


def split(value):
    high = value.astype(BF16)
    low = (value - high.astype(F32)).astype(BF16)
    return high, low


def half_turn(value):
    return pltpu.roll(value, 64, 1)


def lag_weights(weight, first, turn, last, flip):
    inner = jnp.dot(first, weight, precision=HIGHEST, preferred_element_type=F32)
    cos_part, sin_part = inner[:ROWS], inner[ROWS:]
    tcos, tsin = turn[:ROWS], turn[ROWS:]
    real = cos_part * tcos - sin_part * tsin
    imag = cos_part * tsin + sin_part * tcos
    both = jnp.concatenate([real, imag], axis=1)
    by_x = jnp.dot(both, last, precision=HIGHEST, preferred_element_type=F32)
    padded = jnp.concatenate([by_x, jnp.zeros((LANES - ROWS, LANES), F32)], axis=0)
    flip[...] = jnp.transpose(padded)
    lane = lax.broadcasted_iota(jnp.int32, (16, LANES), 1)

    def part(index, shift):
        rows = flip[pl.ds(index, 16, stride=8), :]
        return rows if shift == 0 else pltpu.roll(rows, shift, 1)

    first_row = jnp.where(lane < 48, part(0, 0), jnp.where(lane < 96, part(1, 48), part(2, 96)))
    second_row = jnp.where(
        lane < 16, part(2, 96), jnp.where(lane < 64, part(3, 16), jnp.where(lane < 112, part(4, 64), part(5, 112)))
    )
    third_row = jnp.where(lane < 32, part(5, 112), jnp.where(lane < 80, part(6, 32), part(7, 80)))
    return first_row, second_row, third_row


def shifted(window, amount):
    value = window
    for bit in (128, 64, 32, 16, 8):
        rows = BLOCK + bit
        value = jnp.where((amount & bit) != 0, value[bit : bit + rows], value[0:rows])
    for bit in (4, 2, 1):
        value = jnp.where((amount & bit) != 0, pltpu.roll(value, value.shape[0] - bit, 0), value)
    return pltpu.roll(value, value.shape[0] - 1, 0)[0:BLOCK]


def kernel(
    elution_hbm,
    loadings_hbm,
    shifts_hbm,
    weight_hbm,
    tables_hbm,
    intensity_hbm,
    out_ref,
    elution_ref,
    loadings_ref,
    shifts_ref,
    weight_ref,
    tables_ref,
    samples,
    packed_rows,
    gathered,
    blocks,
    profile,
    slab,
    lags,
    flip,
    toeplitz,
    total,
    window,
    gram_send,
    gram_core,
    gram_x,
    gram_z,
    num_send,
    num_recv,
    load_sems,
    z_send,
    z_recv,
    second_send,
    third_send,
    own_recv,
    swap_send,
    swap_recv,
    gram_sems,
    num_sems,
    num_recv_sems,
):
    freq = lax.axis_index("freq")
    mz = lax.axis_index("mz")
    core = freq % 2
    z_lo = (freq // 2) % 4
    x = freq // 8
    y = mz // 2
    z_hi = mz % 2
    def at(x_to, y_to, z_to, core_to):
        return (x_to * 8 + (z_to % 4) * 2 + core_to, y_to * 2 + z_to // 4)

    partner = (freq + 1 - 2 * core, mz)
    z_mine = z_hi * 4 + z_lo

    loads = [
        pltpu.make_async_copy(source, target, load_sems.at[index])
        for index, (source, target) in enumerate(
            (
                (elution_hbm, elution_ref),
                (weight_hbm, weight_ref),
                (tables_hbm, tables_ref),
                (loadings_hbm, loadings_ref),
                (shifts_hbm, shifts_ref),
                (intensity_hbm, samples),
            )
        )
    ]
    for load in loads:
        load.start()
    barrier = pltpu.get_barrier_semaphore()

    def greet(step, carry):
        pl.semaphore_signal(barrier, inc=1, device_id=((freq + step) % FREQ, mz), device_id_type=MESH)
        return carry

    lax.fori_loop(1, FREQ, greet, 0)
    for step in range(1, 4):
        pl.semaphore_signal(
            barrier, inc=1, device_id=(freq, ((y + step) % 4) * 2 + z_hi), device_id_type=MESH
        )
    for step in range(8):
        pl.semaphore_signal(
            barrier,
            inc=1,
            device_id=at(x, y, (1 - z_hi) * 4 + step % 4, step // 4),
            device_id_type=MESH,
        )

    loads[0].wait()
    own_rows = elution_ref[...]
    beside = jnp.concatenate([own_rows[16:24], own_rows[16:24]], axis=0)
    packed_rows[...] = jnp.concatenate([own_rows[0:16], beside], axis=1)

    loads[1].wait()
    loads[2].wait()
    lag_rows = lag_weights(
        weight_ref[...], tables_ref[:96, :ROWS], tables_ref[96:192], tables_ref[192:448], flip
    )
    for z in range(3):
        lags[z] = lag_rows[z]

    pl.semaphore_wait(barrier, FREQ - 1 + 3 + 8)

    def remote(source, target, send, recv, device):
        return pltpu.make_async_remote_copy(
            src_ref=source, dst_ref=target, send_sem=send, recv_sem=recv, device_id=device, device_id_type=MESH
        )

    z_copies = [
        remote(
            packed_rows,
            gathered.at[z_lo, core],
            z_send.at[step],
            z_recv.at[z_lo, core],
            at(x, y, (z_mine + step) % 8, z_hi),
        )
        for step in range(8)
    ]
    for copy in z_copies[1:]:
        copy.start()

    @pl.when(z_hi != core)
    def _():
        z_copies[0].start()

    @pl.when(z_hi == core)
    def _():
        gathered[z_lo, core] = packed_rows[...]

    close = z_lo // 2
    near = close * (1 - abs(z_hi - core)) + (1 - close) * abs(z_hi - core)

    def half_of(colour_is_own, half):
        return near if (half == 0) == colour_is_own else 1 - near

    left16 = lax.broadcasted_iota(jnp.int32, (16, LANES), 1) < 64
    left8 = left16[:8]

    def merge(half):
        for index in range(2):
            source = 2 * half_of(True, half) + index
            for source_core in range(2):
                itself = jnp.logical_and(z_hi == core, jnp.logical_and(z_lo == source, core == source_core))

                @pl.when(jnp.logical_not(itself))
                def _(source=source, source_core=source_core):
                    spot = gathered.at[source, source_core]
                    remote(packed_rows, spot, z_send.at[0], z_recv.at[source, source_core], partner).wait_recv()

            zero, one = gathered[source, 0], gathered[source, 1]
            blocks[core, x, y, source, 0:16] = jnp.where(left16, zero, half_turn(one))
            blocks[core, x, y, source, 16:24] = jnp.where(left8, half_turn(zero[:8]), one[:8])

    def piece(colour_is_own, colour, dx, dy, half):
        start = 2 * half_of(colour_is_own, half)
        return blocks.at[colour, (x + dx) % 4, (y + dy) % 4, pl.ds(start, 2)]

    class Colour:
        def __init__(self, colour):
            self.colour = colour

        def offsets(self, a, b):
            return (a, b) if self.colour == 0 else (b, a)

        def send(self, a, b, a_step, b_step, half, sem):
            source = piece(True, self.colour, *self.offsets(a, b), half)
            to_x, to_y = self.offsets(a_step, b_step)
            dx, dy = self.offsets((a - a_step) % 4, (b - b_step) % 4)
            device = at((x + to_x) % 4, (y + to_y) % 4, z_mine, self.colour)
            remote(source, source, sem, own_recv.at[dx, dy, half], device).start()

        def second(self, half):
            for step in STEPS:
                self.send(0, 0, step, 0, half, second_send.at[step - 1, half])

        def third(self, a, half):
            for step in STEPS:
                self.send(a, 0, 0, step, half, third_send.at[a, step - 1, half])

        def arrived(self, a, b, half):
            dx, dy = self.offsets(a, b)
            spot = piece(True, self.colour, dx, dy, half)
            remote(spot, spot, swap_send.at[0, 0, 0], own_recv.at[dx, dy, half], partner).wait_recv()
            if b == 0:
                self.third(a, half)
            self.swap(dx, dy, half)

        def swap(self, dx, dy, half):
            spot = piece(True, self.colour, dx, dy, half)
            remote(spot, spot, swap_send.at[dx, dy, half], swap_recv.at[dx, dy, half], partner).start()

        def open_up(self, half):
            if self.colour == 0:
                self.third(0, half)
                self.second(half)
            else:
                self.second(half)
                self.third(0, half)
            self.swap(0, 0, half)

        def first_arrivals(self, half):
            for a, b in ((3, 0), (1, 0), (0, 3), (0, 1), (2, 0), (0, 2)):
                self.arrived(a, b, half)

    def for_each_core(action):
        for colour in range(2):
            pl.when(core == colour)(functools.partial(action, Colour(colour)))

    def swapped(dx):
        for half in range(2):
            for dy in range(4):
                spot = piece(False, 1 - core, dx, dy, half)
                remote(spot, spot, swap_send.at[0, 0, 0], swap_recv.at[dx, dy, half], partner).wait_recv()

    def arrivals(spots):
        def action(colour):
            for half in range(2):
                for dx, dy in spots:
                    colour.arrived(*colour.offsets(dx, dy), half)

        return action

    row = lax.broadcasted_iota(jnp.int32, (LANES, LANES), 0)
    lane = lax.broadcasted_iota(jnp.int32, (LANES, LANES), 1)
    upper = lane >= row

    def turned(z, g):
        base = jnp.broadcast_to(lags[z, pl.ds(g, 1), :], (LANES, LANES))
        return pltpu.roll(base, 0, 1, stride=1, stride_axis=0)

    def build(g, before):
        for z in range(3):
            here = turned(z, g)
            high, low = split(jnp.where(upper, here, before))
            toeplitz[0, 3 * g + z] = high
            toeplitz[1, 3 * g + z] = low
            before = here
        return before

    lax.fori_loop(0, 16, build, turned(2, 15))

    merge(0)
    for_each_core(lambda colour: colour.open_up(0))
    merge(1)
    for_each_core(lambda colour: colour.open_up(1))
    slab[0:128, :] = jnp.zeros((128, LANES), BF16)
    slab[128 + SLAB : 256 + SLAB, :] = jnp.zeros((128, LANES), BF16)
    for_each_core(lambda colour: colour.first_arrivals(0))
    for_each_core(lambda colour: colour.first_arrivals(1))

    left = lax.broadcasted_iota(jnp.int32, (24, LANES), 1) < 64
    begin = ((freq * 3 + 96 - 4) // 2) % ROWS

    def unpack(dx):
        x_at = (x + dx) % 4

        def unpack_one(zl_at, carry):
            low_rows, high_rows = [], []
            for y_at in range(4):
                for colour in range(2):
                    block = blocks[colour, x_at, y_at, zl_at]
                    rounded = block.astype(BF16).astype(F32)
                    rest = block - rounded
                    low_rows.append(jnp.where(left, rounded, half_turn(rest)))
                    high_rows.append(jnp.where(left, half_turn(rounded), rest))
            rows = jnp.concatenate(low_rows + high_rows, axis=0).astype(BF16)
            start = pl.multiple_of(zl_at * 384, 128)
            slab[pl.ds(128 + start, 384), :] = rows
            profile[pl.ds(pl.multiple_of(x_at * SLAB, 128) + start, 384), :] = rows
            return carry

        lax.fori_loop(0, 4, unpack_one, 0)

    def filtered(dx):
        first = ((x + dx) % 4) * 12 - 1 + 2 * ROWS - begin
        lines = []
        for part in range(2):
            for row_block in (0, 2):
                lines.append(
                    jnp.concatenate(
                        [toeplitz[part, (first + step - row_block) % ROWS] for step in range(13)], axis=1
                    )
                )
        rows = jnp.concatenate([slab[0 : 128 + SLAB, :], slab[128 : 256 + SLAB, :]], axis=1)
        value = jnp.dot(jnp.concatenate(lines, axis=0), rows, preferred_element_type=F32)
        if dx == 0:
            total[...] = value
        else:
            total[...] += value

    swapped(0)
    unpack(0)
    filtered(0)
    for_each_core(arrivals(((3, 3), (3, 1), (3, 2), (1, 3), (1, 1), (1, 2))))
    swapped(3)
    unpack(3)
    filtered(3)
    for_each_core(arrivals(((2, 3), (2, 1), (2, 2))))
    swapped(1)
    unpack(1)
    filtered(1)
    swapped(2)
    unpack(2)
    filtered(2)

    for row_block in range(4):
        base = (row_block // 2) * 128
        cut = pl.ds((row_block % 2) * 128, 128)
        value = total[pl.ds(base, 128), cut] + total[pl.ds(256 + base, 128), cut]
        window[0, pl.ds(row_block * 128, 128), :] = value + half_turn(value)
        start = pl.multiple_of(((begin + row_block) % ROWS) * 128, 128)
        value = profile[pl.ds(start, 128), :].astype(F32)
        window[1, pl.ds(row_block * 128, 128), :] = value + half_turn(value)

    skip = pl.multiple_of((freq % 2) * 64, 64)
    for load in loads[3:]:
        load.wait()
    filtered_rows = window[0, pl.ds(skip, 448), :]
    plain_rows = window[1, pl.ds(skip, 448), :]
    quad = jnp.zeros((256, 256), F32)
    numer = jnp.zeros((COMP, CHANNELS), F32)
    stacks = []
    for pair_at in range(RUNS // 2):
        amount = jnp.concatenate([shifts_ref[2 * pair_at : 2 * pair_at + 1], shifts_ref[2 * pair_at + 1 : 2 * pair_at + 2]], axis=1)
        gain = jnp.concatenate(
            [loadings_ref[2 * pair_at : 2 * pair_at + 1], loadings_ref[2 * pair_at + 1 : 2 * pair_at + 2]], axis=1
        )
        moved = jnp.transpose(shifted(filtered_rows, 255 - amount) * gain)
        model_high, model_low = split(shifted(plain_rows, 255 - amount) * gain)
        high, low = split(moved)
        stacks.append((high, low))
        quad = quad + jnp.dot(
            jnp.concatenate([high, low], axis=0),
            jnp.concatenate([model_high, model_low], axis=1),
            preferred_element_type=F32,
        )
    corner = quad[:128, :128] + quad[:128, 128:] + quad[128:, :128]
    gram_own = corner[:64] + half_turn(corner[64:])
    left32 = lax.broadcasted_iota(jnp.int32, (32, LANES), 1) < 64
    gram_send[0] = jnp.where(left32, gram_own[:32], half_turn(gram_own[32:]))
    core_copy = remote(gram_send.at[0], gram_core, gram_sems.at[0], gram_sems.at[1], partner)
    core_copy.start()

    for run in range(RUNS):
        high, low = stacks[run // 2]
        cut = slice((run % 2) * 64, (run % 2) * 64 + 64)
        both = jnp.dot(
            jnp.concatenate([high[cut], low[cut]], axis=0), samples[run], preferred_element_type=F32
        )
        numer = numer + both[:64] + both[64:]
    by_channel = jnp.transpose(numer).reshape(FREQ, 2, 8, COMP)
    num_send[...] = jnp.concatenate([by_channel[:, 0], by_channel[:, 1]], axis=2)

    def num_copy(step):
        to = (freq + step) % FREQ
        return remote(num_send.at[to], num_recv.at[freq], num_sems.at[step], num_recv_sems.at[step], (to, mz))

    def send_num(step, carry):
        num_copy(step).start()
        return carry

    core_copy.wait()
    gram_send[1] = gram_send[0] + gram_core[...]
    x_copies = []
    for step in range(1, 4):
        copy = remote(
            gram_send.at[1],
            gram_x.at[step - 1],
            gram_sems.at[1 + step],
            gram_sems.at[4 + step],
            at((x + step) % 4, y, z_mine, core),
        )
        copy.start()
        x_copies.append(copy)
    for copy in x_copies:
        copy.wait()
    gram_send[2] = (gram_send[1] + gram_x[0]) + (gram_x[1] + gram_x[2])
    z_grams = []
    for step in range(1, 4):
        copy = remote(
            gram_send.at[2],
            gram_z.at[step - 1],
            gram_sems.at[7 + step],
            gram_sems.at[10 + step],
            at(x, y, z_hi * 4 + (z_lo + step) % 4, core),
        )
        copy.start()
        z_grams.append(copy)
    lax.fori_loop(1, FREQ, send_num, 0)
    for copy in z_grams:
        copy.wait()
    packed = (gram_send[2] + gram_z[0]) + (gram_z[1] + gram_z[2])

    row64 = lax.broadcasted_iota(jnp.int32, (COMP, LANES), 0)
    lane64 = lax.broadcasted_iota(jnp.int32, (COMP, LANES), 1)
    unit = (lane64 == row64 + COMP).astype(F32)
    matrix = jnp.where(lane64 < COMP, jnp.concatenate([packed, half_turn(packed)], axis=0), unit)
    for step in range(0, COMP, 2):
        one = jnp.broadcast_to(matrix[:, step : step + 1], matrix.shape)
        two = jnp.broadcast_to(matrix[:, step + 1 : step + 2], matrix.shape)
        top, low = matrix[step : step + 1], matrix[step + 1 : step + 2]
        one_top, one_low = one[step : step + 1], one[step + 1 : step + 2]
        two_top, two_low = two[step : step + 1], two[step + 1 : step + 2]
        scale = 1.0 / (one_top * two_low - two_top * one_low)
        top_new = (two_low * top - two_top * low) * scale
        low_new = (one_top * low - one_low * top) * scale
        rest = matrix - one * top_new - two * low_new
        matrix = jnp.where(row64 == step, top_new, jnp.where(row64 == step + 1, low_new, rest))
    inverse = matrix[:, COMP:]

    def wait_num(step, carry):
        source = (freq + FREQ - step) % FREQ
        copy = remote(num_send.at[source], num_recv.at[source], num_sems.at[step], num_recv_sems.at[step], (source, mz))
        copy.wait_recv()
        return carry

    lax.fori_loop(1, FREQ, wait_num, 0)
    num_recv[freq] = num_send[freq]
    summed = jnp.sum(num_recv[...], axis=0)
    own_channels = jnp.concatenate([summed[:, :64], summed[:, 64:]], axis=0)
    out_ref[...] = lax.dot_general(
        own_channels, inverse, (((1,), (1,)), ((), ())), precision=HIGHEST, preferred_element_type=F32
    )

    for copy in z_copies[1:]:
        copy.wait_send()

    @pl.when(z_hi != core)
    def _():
        z_copies[0].wait_send()

    part = blocks.at[0, 0, 0, 0:2]
    for half in range(2):
        for step in range(3):
            remote(part, part, second_send.at[step, half], z_recv.at[0, 0], partner).wait_send()
            for a in range(4):
                remote(part, part, third_send.at[a, step, half], z_recv.at[0, 0], partner).wait_send()
        for dx in range(4):
            for dy in range(4):
                remote(part, part, swap_send.at[dx, dy, half], z_recv.at[0, 0], partner).wait_send()

    def drain(step, carry):
        num_copy(step).wait_send()
        return carry

    lax.fori_loop(1, FREQ, drain, 0)


def on_device(intensity, elution, loadings, shifts, bin_weight):
    vmem = pl.BlockSpec(memory_space=pltpu.VMEM)
    dma = pltpu.SemaphoreType.DMA
    def held(value):
        return pltpu.with_memory_space_constraint(value, pltpu.HBM)

    by_channel = pl.pallas_call(
        kernel,
        out_shape=jax.ShapeDtypeStruct((OWN, COMP), F32),
        in_specs=[pl.BlockSpec(memory_space=pltpu.HBM)] * 6,
        out_specs=vmem,
        scratch_shapes=[
            pltpu.VMEM((24, COMP), F32),
            pltpu.VMEM((RUNS, COMP), F32),
            pltpu.VMEM((RUNS, COMP), jnp.int32),
            pltpu.VMEM((ROWS, LANES), F32),
            pltpu.VMEM((448, LANES), F32),
            pltpu.VMEM((RUNS, BLOCK, CHANNELS), BF16),
            pltpu.VMEM((16, LANES), F32),
            pltpu.VMEM((4, 2, 16, LANES), F32),
            pltpu.VMEM((2, 4, 4, 4, 24, LANES), F32),
            pltpu.VMEM((LENGTH, LANES), BF16),
            pltpu.VMEM((SLAB + 256, LANES), BF16),
            pltpu.VMEM((3, 16, LANES), F32),
            pltpu.VMEM((LANES, LANES), F32),
            pltpu.VMEM((2, ROWS, LANES, LANES), BF16),
            pltpu.VMEM((512, 256), F32),
            pltpu.VMEM((2, WINDOW, LANES), F32),
            pltpu.VMEM((3, 32, LANES), F32),
            pltpu.VMEM((32, LANES), F32),
            pltpu.VMEM((3, 32, LANES), F32),
            pltpu.VMEM((3, 32, LANES), F32),
            pltpu.VMEM((FREQ, 8, LANES), F32),
            pltpu.VMEM((FREQ, 8, LANES), F32),
            dma((6,)),
            dma((8,)),
            dma((4, 2)),
            dma((3, 2)),
            dma((4, 3, 2)),
            dma((4, 4, 2)),
            dma((4, 4, 2)),
            dma((4, 4, 2)),
            dma((14,)),
            dma((FREQ,)),
            dma((FREQ,)),
        ],
        compiler_params=pltpu.CompilerParams(
            collective_id=0, has_side_effects=True, vmem_limit_bytes=32 * 1024 * 1024
        ),
    )(*map(held, (elution, loadings, shifts, bin_weight.reshape(ROWS, LANES), transform_tables(), intensity)))
    return by_channel.T


def solution(mesh):
    in_specs = (P(None, "freq", "mz"), P(("freq", "mz"), None), P(), P(), P())
    out_specs = P(None, ("mz", "freq"))
    return jax.shard_map(on_device, mesh=mesh, in_specs=in_specs, out_specs=out_specs, check_vma=False)
```

```python
import functools
import math

import jax
import jax.numpy as jnp
import numpy as np
from jax import lax
from jax.experimental import pallas as pl
from jax.experimental.pallas import tpu as pltpu
from jax.sharding import PartitionSpec as P

MESH = pl.DeviceIdType.MESH
HIGHEST = lax.Precision.HIGHEST
F32 = jnp.float32
BF16 = jnp.bfloat16

LENGTH = 6144
ROWS = 48
LANES = 128
RUNS = 8
COMP = 64
BLOCK = 192
CHANNELS = 512
FREQ = 32
OWN = 16
SLAB = 1536
STEPS = (1, 3, 2)
WINDOW = 512


def transform_tables():
    x48 = np.arange(ROWS)
    b128 = np.arange(LANES)
    inner = 2.0 * np.pi / ROWS * ((x48[:, None] * x48[None, :]) % ROWS)
    middle = 2.0 * np.pi / LENGTH * ((x48[:, None] * b128[None, :]) % LENGTH)
    outer = 2.0 * np.pi / LANES * ((b128[:, None] * b128[None, :]) % LANES)
    first = np.concatenate([np.cos(inner), np.sin(inner)], axis=0)
    first = np.pad(first, ((0, 0), (0, LANES - ROWS)))
    turn = np.concatenate([np.cos(middle), np.sin(middle)], axis=0)
    last = np.concatenate([np.cos(outer), -np.sin(outer)], axis=0) / LENGTH
    return jnp.asarray(np.concatenate([first, turn, last], axis=0).astype(np.float32))


def split(value):
    high = value.astype(BF16)
    low = (value - high.astype(F32)).astype(BF16)
    return high, low


def half_turn(value):
    return pltpu.roll(value, 64, 1)


def lag_weights(weight, first, turn, last, flip):
    inner = jnp.dot(first, weight, precision=HIGHEST, preferred_element_type=F32)
    cos_part, sin_part = inner[:ROWS], inner[ROWS:]
    tcos, tsin = turn[:ROWS], turn[ROWS:]
    real = cos_part * tcos - sin_part * tsin
    imag = cos_part * tsin + sin_part * tcos
    both = jnp.concatenate([real, imag], axis=1)
    by_x = jnp.dot(both, last, precision=HIGHEST, preferred_element_type=F32)
    padded = jnp.concatenate([by_x, jnp.zeros((LANES - ROWS, LANES), F32)], axis=0)
    flip[...] = jnp.transpose(padded)
    lane = lax.broadcasted_iota(jnp.int32, (16, LANES), 1)

    def part(index, shift):
        rows = flip[pl.ds(index, 16, stride=8), :]
        return rows if shift == 0 else pltpu.roll(rows, shift, 1)

    first_row = jnp.where(lane < 48, part(0, 0), jnp.where(lane < 96, part(1, 48), part(2, 96)))
    second_row = jnp.where(
        lane < 16, part(2, 96), jnp.where(lane < 64, part(3, 16), jnp.where(lane < 112, part(4, 64), part(5, 112)))
    )
    third_row = jnp.where(lane < 32, part(5, 112), jnp.where(lane < 80, part(6, 32), part(7, 80)))
    return first_row, second_row, third_row


def shifted(window, amount):
    value = window
    for bit in (128, 64, 32, 16, 8):
        rows = BLOCK + bit
        value = jnp.where((amount & bit) != 0, value[bit : bit + rows], value[0:rows])
    for bit in (4, 2, 1):
        value = jnp.where((amount & bit) != 0, pltpu.roll(value, value.shape[0] - bit, 0), value)
    return pltpu.roll(value, value.shape[0] - 1, 0)[0:BLOCK]


def kernel(
    elution_hbm,
    loadings_hbm,
    shifts_hbm,
    weight_hbm,
    tables_hbm,
    intensity_hbm,
    out_ref,
    elution_ref,
    loadings_ref,
    shifts_ref,
    weight_ref,
    tables_ref,
    samples,
    packed_rows,
    gathered,
    blocks,
    profile,
    slab,
    lags,
    flip,
    toeplitz,
    total,
    window,
    gram_send,
    gram_core,
    gram_x,
    gram_z,
    num_send,
    num_recv,
    load_sems,
    z_send,
    z_recv,
    second_send,
    third_send,
    own_recv,
    swap_send,
    swap_recv,
    gram_sems,
    num_sem,
):
    freq = lax.axis_index("freq")
    mz = lax.axis_index("mz")
    core = freq % 2
    z_lo = (freq // 2) % 4
    x = freq // 8
    y = mz // 2
    z_hi = mz % 2
    def at(x_to, y_to, z_to, core_to):
        return (x_to * 8 + (z_to % 4) * 2 + core_to, y_to * 2 + z_to // 4)

    partner = (freq + 1 - 2 * core, mz)
    z_mine = z_hi * 4 + z_lo

    barrier = pltpu.get_barrier_semaphore()

    for step in range(8):
        pl.semaphore_signal(
            barrier,
            inc=1,
            device_id=at(x, y, (1 - z_hi) * 4 + step % 4, step // 4),
            device_id_type=MESH,
        )
    for step in range(1, 4):
        pl.semaphore_signal(
            barrier, inc=1, device_id=(freq, ((y + step) % 4) * 2 + z_hi), device_id_type=MESH
        )
    def greet(step, carry):
        pl.semaphore_signal(barrier, inc=1, device_id=((freq + step) % FREQ, mz), device_id_type=MESH)
        return carry

    lax.fori_loop(1, FREQ, greet, 0)
    loads = [
        pltpu.make_async_copy(source, target, load_sems.at[index])
        for index, (source, target) in enumerate(
            (
                (elution_hbm, elution_ref),
                (weight_hbm, weight_ref),
                (tables_hbm, tables_ref),
                (loadings_hbm, loadings_ref),
                (shifts_hbm, shifts_ref),
                (intensity_hbm, samples),
            )
        )
    ]
    for load in loads:
        load.start()
    loads[0].wait()
    own_rows = elution_ref[...]
    beside = jnp.concatenate([own_rows[16:24], own_rows[16:24]], axis=0)
    packed_rows[...] = jnp.concatenate([own_rows[0:16], beside], axis=1)

    loads[1].wait()
    loads[2].wait()
    lag_rows = lag_weights(
        weight_ref[...], tables_ref[:96, :ROWS], tables_ref[96:192], tables_ref[192:448], flip
    )
    for z in range(3):
        lags[z] = lag_rows[z]

    pl.semaphore_wait(barrier, FREQ - 1 + 3 + 8)

    def remote(source, target, send, recv, device):
        return pltpu.make_async_remote_copy(
            src_ref=source, dst_ref=target, send_sem=send, recv_sem=recv, device_id=device, device_id_type=MESH
        )

    z_copies = [
        remote(
            packed_rows,
            gathered.at[z_lo, core],
            z_send.at[step],
            z_recv.at[z_lo, core],
            at(x, y, (z_mine + step) % 8, z_hi),
        )
        for step in range(8)
    ]
    for copy in z_copies[1:]:
        copy.start()

    @pl.when(z_hi != core)
    def _():
        z_copies[0].start()

    @pl.when(z_hi == core)
    def _():
        gathered[z_lo, core] = packed_rows[...]

    close = z_lo // 2
    near = close * (1 - abs(z_hi - core)) + (1 - close) * abs(z_hi - core)

    def half_of(colour_is_own, half):
        return near if (half == 0) == colour_is_own else 1 - near

    left16 = lax.broadcasted_iota(jnp.int32, (16, LANES), 1) < 64
    left8 = left16[:8]

    def merge(half):
        for index in range(2):
            source = 2 * half_of(True, half) + index
            for source_core in range(2):
                itself = jnp.logical_and(z_hi == core, jnp.logical_and(z_lo == source, core == source_core))

                @pl.when(jnp.logical_not(itself))
                def _(source=source, source_core=source_core):
                    spot = gathered.at[source, source_core]
                    remote(packed_rows, spot, z_send.at[0], z_recv.at[source, source_core], partner).wait_recv()

            zero, one = gathered[source, 0], gathered[source, 1]
            blocks[core, x, y, source, 0:16] = jnp.where(left16, zero, half_turn(one))
            blocks[core, x, y, source, 16:24] = jnp.where(left8, half_turn(zero[:8]), one[:8])

    def piece(colour_is_own, colour, dx, dy, half):
        start = 2 * half_of(colour_is_own, half)
        return blocks.at[colour, (x + dx) % 4, (y + dy) % 4, pl.ds(start, 2)]

    class Colour:
        def __init__(self, colour):
            self.colour = colour

        def offsets(self, a, b):
            return (a, b) if self.colour == 0 else (b, a)

        def send(self, a, b, a_step, b_step, half, sem):
            source = piece(True, self.colour, *self.offsets(a, b), half)
            to_x, to_y = self.offsets(a_step, b_step)
            dx, dy = self.offsets((a - a_step) % 4, (b - b_step) % 4)
            device = at((x + to_x) % 4, (y + to_y) % 4, z_mine, self.colour)
            remote(source, source, sem, own_recv.at[dx, dy, half], device).start()

        def second(self, half):
            for step in STEPS:
                self.send(0, 0, step, 0, half, second_send)

        def third(self, a, half):
            for step in STEPS:
                self.send(a, 0, 0, step, half, third_send)

        def arrived(self, a, b, half):
            dx, dy = self.offsets(a, b)
            spot = piece(True, self.colour, dx, dy, half)
            remote(spot, spot, swap_send, own_recv.at[dx, dy, half], partner).wait_recv()
            if b == 0:
                self.third(a, half)
            self.swap(dx, dy, half)

        def swap(self, dx, dy, half):
            spot = piece(True, self.colour, dx, dy, half)
            remote(spot, spot, swap_send, swap_recv.at[dx, dy, half], partner).start()

        def open_up(self, half):
            if self.colour == 0:
                self.third(0, half)
                self.second(half)
            else:
                self.second(half)
                self.third(0, half)
            self.swap(0, 0, half)

        def first_arrivals(self, half):
            for a, b in ((3, 0), (1, 0), (0, 3), (0, 1), (2, 0), (0, 2)):
                self.arrived(a, b, half)

    def for_each_core(action):
        for colour in range(2):
            pl.when(core == colour)(functools.partial(action, Colour(colour)))

    def swapped(dx):
        for half in range(2):
            for dy in range(4):
                spot = piece(False, 1 - core, dx, dy, half)
                remote(spot, spot, swap_send, swap_recv.at[dx, dy, half], partner).wait_recv()

    def arrivals(spots):
        def action(colour):
            for half in range(2):
                for dx, dy in spots:
                    colour.arrived(*colour.offsets(dx, dy), half)

        return action

    row = lax.broadcasted_iota(jnp.int32, (LANES, LANES), 0)
    lane = lax.broadcasted_iota(jnp.int32, (LANES, LANES), 1)
    upper = lane >= row

    def turned(z, g):
        base = jnp.broadcast_to(lags[z, pl.ds(g, 1), :], (LANES, LANES))
        return pltpu.roll(base, 0, 1, stride=1, stride_axis=0)

    def build(g, before):
        for z in range(3):
            here = turned(z, g)
            high, low = split(jnp.where(upper, here, before))
            toeplitz[0, 3 * g + z] = high
            toeplitz[1, 3 * g + z] = low
            before = here
        return before

    lax.fori_loop(0, 16, build, turned(2, 15))

    merge(0)
    for_each_core(lambda colour: colour.open_up(0))
    merge(1)
    for_each_core(lambda colour: colour.open_up(1))
    slab[0:128, :] = jnp.zeros((128, LANES), BF16)
    slab[128 + SLAB : 256 + SLAB, :] = jnp.zeros((128, LANES), BF16)
    for_each_core(lambda colour: colour.first_arrivals(0))
    for_each_core(lambda colour: colour.first_arrivals(1))

    left = lax.broadcasted_iota(jnp.int32, (24, LANES), 1) < 64
    begin = ((freq * 3 + 96 - 4) // 2) % ROWS

    def unpack(dx):
        x_at = (x + dx) % 4

        def unpack_one(zl_at, carry):
            low_rows, high_rows = [], []
            for y_at in range(4):
                for colour in range(2):
                    block = blocks[colour, x_at, y_at, zl_at]
                    rounded = block.astype(BF16).astype(F32)
                    rest = block - rounded
                    low_rows.append(jnp.where(left, rounded, half_turn(rest)))
                    high_rows.append(jnp.where(left, half_turn(rounded), rest))
            rows = jnp.concatenate(low_rows + high_rows, axis=0).astype(BF16)
            start = pl.multiple_of(zl_at * 384, 128)
            slab[pl.ds(128 + start, 384), :] = rows
            profile[pl.ds(pl.multiple_of(x_at * SLAB, 128) + start, 384), :] = rows
            return carry

        lax.fori_loop(0, 4, unpack_one, 0)

    def filtered(dx):
        first = ((x + dx) % 4) * 12 - 1 + 2 * ROWS - begin
        lines = []
        for part in range(2):
            for row_block in (0, 2):
                lines.append(
                    jnp.concatenate(
                        [toeplitz[part, (first + step - row_block) % ROWS] for step in range(13)], axis=1
                    )
                )
        rows = jnp.concatenate([slab[0 : 128 + SLAB, :], slab[128 : 256 + SLAB, :]], axis=1)
        value = jnp.dot(jnp.concatenate(lines, axis=0), rows, preferred_element_type=F32)
        total[...] += value

    total[...] = jnp.zeros_like(total)

    def slab_step(index, carry):
        dx = jnp.where(index == 0, 0, jnp.where(index == 1, 3, index - 1))
        swapped(dx)
        unpack(dx)
        filtered(dx)

        @pl.when(index == 0)
        def _():
            for_each_core(arrivals(((3, 3), (3, 1), (3, 2), (1, 3), (1, 1), (1, 2))))

        @pl.when(index == 1)
        def _():
            for_each_core(arrivals(((2, 3), (2, 1), (2, 2))))

        return carry

    lax.fori_loop(0, 4, slab_step, 0)

    for row_block in range(4):
        base = (row_block // 2) * 128
        cut = pl.ds((row_block % 2) * 128, 128)
        value = total[pl.ds(base, 128), cut] + total[pl.ds(256 + base, 128), cut]
        window[0, pl.ds(row_block * 128, 128), :] = value + half_turn(value)
        start = pl.multiple_of(((begin + row_block) % ROWS) * 128, 128)
        value = profile[pl.ds(start, 128), :].astype(F32)
        window[1, pl.ds(row_block * 128, 128), :] = value + half_turn(value)

    skip = pl.multiple_of((freq % 2) * 64, 64)
    for load in loads[3:]:
        load.wait()
    filtered_rows = window[0, pl.ds(skip, 448), :]
    plain_rows = window[1, pl.ds(skip, 448), :]
    quad = jnp.zeros((256, 256), F32)
    numer = jnp.zeros((COMP, CHANNELS), F32)
    stacks = []
    for pair_at in range(RUNS // 2):
        amount = jnp.concatenate([shifts_ref[2 * pair_at : 2 * pair_at + 1], shifts_ref[2 * pair_at + 1 : 2 * pair_at + 2]], axis=1)
        gain = jnp.concatenate(
            [loadings_ref[2 * pair_at : 2 * pair_at + 1], loadings_ref[2 * pair_at + 1 : 2 * pair_at + 2]], axis=1
        )
        moved = jnp.transpose(shifted(filtered_rows, 255 - amount) * gain)
        model_high, model_low = split(shifted(plain_rows, 255 - amount) * gain)
        high, low = split(moved)
        stacks.append((high, low))
        quad = quad + jnp.dot(
            jnp.concatenate([high, low], axis=0),
            jnp.concatenate([model_high, model_low], axis=1),
            preferred_element_type=F32,
        )
    corner = quad[:128, :128] + quad[:128, 128:] + quad[128:, :128]
    gram_own = corner[:64] + half_turn(corner[64:])
    left32 = lax.broadcasted_iota(jnp.int32, (32, LANES), 1) < 64
    gram_send[0] = jnp.where(left32, gram_own[:32], half_turn(gram_own[32:]))
    core_copy = remote(gram_send.at[0], gram_core, gram_sems.at[0], gram_sems.at[1], partner)
    core_copy.start()

    for run in range(RUNS):
        high, low = stacks[run // 2]
        cut = slice((run % 2) * 64, (run % 2) * 64 + 64)
        both = jnp.dot(
            jnp.concatenate([high[cut], low[cut]], axis=0), samples[run], preferred_element_type=F32
        )
        numer = numer + both[:64] + both[64:]
    by_channel = jnp.transpose(numer).reshape(FREQ, 2, 8, COMP)
    num_send[...] = jnp.concatenate([by_channel[:, 0], by_channel[:, 1]], axis=2)

    def num_copy(step):
        to = (freq + step) % FREQ
        return remote(num_send.at[to], num_recv.at[freq], num_sem.at[0], num_sem.at[1], (to, mz))

    def send_num(step, carry):
        num_copy(step).start()
        return carry

    core_copy.wait()
    gram_send[1] = gram_send[0] + gram_core[...]
    x_copies = []
    for step in range(1, 4):
        copy = remote(
            gram_send.at[1],
            gram_x.at[step - 1],
            gram_sems.at[1 + step],
            gram_sems.at[4 + step],
            at((x + step) % 4, y, z_mine, core),
        )
        copy.start()
        x_copies.append(copy)
    for copy in z_copies[1:]:
        copy.wait_send()

    @pl.when(z_hi != core)
    def _():
        z_copies[0].wait_send()

    for spot, sem in ((blocks.at[0, 0, 0:3], second_send), (blocks.at[0, 0:3], third_send), (blocks.at[0], swap_send)):
        remote(spot, spot, sem, z_recv.at[0, 0], partner).wait_send()

    for copy in x_copies:
        copy.wait()
    gram_send[2] = (gram_send[1] + gram_x[0]) + (gram_x[1] + gram_x[2])
    z_grams = []
    for step in range(1, 4):
        copy = remote(
            gram_send.at[2],
            gram_z.at[step - 1],
            gram_sems.at[7 + step],
            gram_sems.at[10 + step],
            at(x, y, z_hi * 4 + (z_lo + step) % 4, core),
        )
        copy.start()
        z_grams.append(copy)
    lax.fori_loop(1, FREQ, send_num, 0)
    for copy in z_grams:
        copy.wait()
    packed = (gram_send[2] + gram_z[0]) + (gram_z[1] + gram_z[2])

    row64 = lax.broadcasted_iota(jnp.int32, (COMP, LANES), 0)
    lane64 = lax.broadcasted_iota(jnp.int32, (COMP, LANES), 1)
    unit = (lane64 == row64 + COMP).astype(F32)
    matrix = jnp.where(lane64 < COMP, jnp.concatenate([packed, half_turn(packed)], axis=0), unit)
    for step in range(0, COMP, 2):
        one = jnp.broadcast_to(matrix[:, step : step + 1], matrix.shape)
        two = jnp.broadcast_to(matrix[:, step + 1 : step + 2], matrix.shape)
        top, low = matrix[step : step + 1], matrix[step + 1 : step + 2]
        one_top, one_low = one[step : step + 1], one[step + 1 : step + 2]
        two_top, two_low = two[step : step + 1], two[step + 1 : step + 2]
        scale = 1.0 / (one_top * two_low - two_top * one_low)
        top_new = (two_low * top - two_top * low) * scale
        low_new = (one_top * low - one_low * top) * scale
        rest = matrix - one * top_new - two * low_new
        matrix = jnp.where(row64 == step, top_new, jnp.where(row64 == step + 1, low_new, rest))
    inverse = matrix[:, COMP:]

    others = num_send.at[0 : FREQ - 1]
    num_all = remote(others, num_recv.at[0 : FREQ - 1], num_sem.at[0], num_sem.at[1], partner)
    num_all.wait_recv()
    num_recv[freq] = num_send[freq]
    summed = jnp.sum(num_recv[...], axis=0)
    own_channels = jnp.concatenate([summed[:, :64], summed[:, 64:]], axis=0)
    out_ref[...] = lax.dot_general(
        own_channels, inverse, (((1,), (1,)), ((), ())), precision=HIGHEST, preferred_element_type=F32
    )

    num_all.wait_send()


def on_device(intensity, elution, loadings, shifts, bin_weight):
    vmem = pl.BlockSpec(memory_space=pltpu.VMEM)
    dma = pltpu.SemaphoreType.DMA
    def held(value):
        return pltpu.with_memory_space_constraint(value, pltpu.HBM)

    by_channel = pl.pallas_call(
        kernel,
        out_shape=jax.ShapeDtypeStruct((OWN, COMP), F32),
        in_specs=[pl.BlockSpec(memory_space=pltpu.HBM)] * 6,
        out_specs=vmem,
        scratch_shapes=[
            pltpu.VMEM((24, COMP), F32),
            pltpu.VMEM((RUNS, COMP), F32),
            pltpu.VMEM((RUNS, COMP), jnp.int32),
            pltpu.VMEM((ROWS, LANES), F32),
            pltpu.VMEM((448, LANES), F32),
            pltpu.VMEM((RUNS, BLOCK, CHANNELS), BF16),
            pltpu.VMEM((16, LANES), F32),
            pltpu.VMEM((4, 2, 16, LANES), F32),
            pltpu.VMEM((2, 4, 4, 4, 24, LANES), F32),
            pltpu.VMEM((LENGTH, LANES), BF16),
            pltpu.VMEM((SLAB + 256, LANES), BF16),
            pltpu.VMEM((3, 16, LANES), F32),
            pltpu.VMEM((LANES, LANES), F32),
            pltpu.VMEM((2, ROWS, LANES, LANES), BF16),
            pltpu.VMEM((512, 256), F32),
            pltpu.VMEM((2, WINDOW, LANES), F32),
            pltpu.VMEM((3, 32, LANES), F32),
            pltpu.VMEM((32, LANES), F32),
            pltpu.VMEM((3, 32, LANES), F32),
            pltpu.VMEM((3, 32, LANES), F32),
            pltpu.VMEM((FREQ, 8, LANES), F32),
            pltpu.VMEM((FREQ, 8, LANES), F32),
            dma((6,)),
            dma((8,)),
            dma((4, 2)),
            dma,
            dma,
            dma((4, 4, 2)),
            dma,
            dma((4, 4, 2)),
            dma((14,)),
            dma((2,)),
        ],
        compiler_params=pltpu.CompilerParams(
            collective_id=0, has_side_effects=True, vmem_limit_bytes=32 * 1024 * 1024
        ),
    )(*map(held, (elution, loadings, shifts, bin_weight.reshape(ROWS, LANES), transform_tables(), intensity)))
    return by_channel.T


def solution(mesh):
    in_specs = (P(None, "freq", "mz"), P(("freq", "mz"), None), P(), P(), P())
    out_specs = P(None, ("mz", "freq"))
    return jax.shard_map(on_device, mesh=mesh, in_specs=in_specs, out_specs=out_specs, check_vma=False)
```

```python
import functools
import math

import jax
import jax.numpy as jnp
import numpy as np
from jax import lax
from jax.experimental import pallas as pl
from jax.experimental.pallas import tpu as pltpu
from jax.sharding import PartitionSpec as P

MESH = pl.DeviceIdType.MESH
HIGHEST = lax.Precision.HIGHEST
F32 = jnp.float32
BF16 = jnp.bfloat16

LENGTH = 6144
ROWS = 48
LANES = 128
RUNS = 8
COMP = 64
BLOCK = 192
CHANNELS = 512
FREQ = 32
OWN = 16
SLAB = 1536
STEPS = (1, 3, 2)
WINDOW = 512


def transform_tables():
    x48 = np.arange(ROWS)
    b128 = np.arange(LANES)
    inner = 2.0 * np.pi / ROWS * ((x48[:, None] * x48[None, :]) % ROWS)
    middle = 2.0 * np.pi / LENGTH * ((x48[:, None] * b128[None, :]) % LENGTH)
    outer = 2.0 * np.pi / LANES * ((b128[:, None] * b128[None, :]) % LANES)
    first = np.concatenate([np.cos(inner), np.sin(inner)], axis=0)
    first = np.pad(first, ((0, 0), (0, LANES - ROWS)))
    turn = np.concatenate([np.cos(middle), np.sin(middle)], axis=0)
    last = np.concatenate([np.cos(outer), -np.sin(outer)], axis=0) / LENGTH
    return jnp.asarray(np.concatenate([first, turn, last], axis=0).astype(np.float32))


def split(value):
    high = value.astype(BF16)
    low = (value - high.astype(F32)).astype(BF16)
    return high, low


def half_turn(value):
    return pltpu.roll(value, 64, 1)


def lag_weights(weight, first, turn, last, flip):
    inner = jnp.dot(first, weight, precision=HIGHEST, preferred_element_type=F32)
    cos_part, sin_part = inner[:ROWS], inner[ROWS:]
    tcos, tsin = turn[:ROWS], turn[ROWS:]
    real = cos_part * tcos - sin_part * tsin
    imag = cos_part * tsin + sin_part * tcos
    both = jnp.concatenate([real, imag], axis=1)
    by_x = jnp.dot(both, last, precision=HIGHEST, preferred_element_type=F32)
    padded = jnp.concatenate([by_x, jnp.zeros((LANES - ROWS, LANES), F32)], axis=0)
    flip[...] = jnp.transpose(padded)
    lane = lax.broadcasted_iota(jnp.int32, (16, LANES), 1)

    def part(index, shift):
        rows = flip[pl.ds(index, 16, stride=8), :]
        return rows if shift == 0 else pltpu.roll(rows, shift, 1)

    first_row = jnp.where(lane < 48, part(0, 0), jnp.where(lane < 96, part(1, 48), part(2, 96)))
    second_row = jnp.where(
        lane < 16, part(2, 96), jnp.where(lane < 64, part(3, 16), jnp.where(lane < 112, part(4, 64), part(5, 112)))
    )
    third_row = jnp.where(lane < 32, part(5, 112), jnp.where(lane < 80, part(6, 32), part(7, 80)))
    return first_row, second_row, third_row


def shifted(window, amount):
    value = window
    for bit in (128, 64, 32, 16, 8):
        rows = BLOCK + bit
        value = jnp.where((amount & bit) != 0, value[bit : bit + rows], value[0:rows])
    for bit in (4, 2, 1):
        value = jnp.where((amount & bit) != 0, pltpu.roll(value, value.shape[0] - bit, 0), value)
    return pltpu.roll(value, value.shape[0] - 1, 0)[0:BLOCK]


def kernel(
    elution_hbm,
    loadings_hbm,
    shifts_hbm,
    weight_hbm,
    tables_hbm,
    intensity_hbm,
    out_ref,
    elution_ref,
    loadings_ref,
    shifts_ref,
    weight_ref,
    tables_ref,
    samples,
    packed_rows,
    gathered,
    blocks,
    profile,
    slab,
    lags,
    flip,
    toeplitz,
    total,
    window,
    gram_send,
    gram_core,
    gram_x,
    gram_z,
    num_send,
    num_core,
    num_half,
    num_recv,
    load_sems,
    z_send,
    z_recv,
    second_send,
    third_send,
    own_recv,
    swap_send,
    swap_recv,
    gram_sems,
    num_sem,
):
    freq = lax.axis_index("freq")
    mz = lax.axis_index("mz")
    core = freq % 2
    z_lo = (freq // 2) % 4
    x = freq // 8
    y = mz // 2
    z_hi = mz % 2
    def at(x_to, y_to, z_to, core_to):
        return (x_to * 8 + (z_to % 4) * 2 + core_to, y_to * 2 + z_to // 4)

    partner = (freq + 1 - 2 * core, mz)
    z_mine = z_hi * 4 + z_lo

    loads = [
        pltpu.make_async_copy(source, target, load_sems.at[index])
        for index, (source, target) in enumerate(
            (
                (elution_hbm, elution_ref),
                (weight_hbm, weight_ref),
                (tables_hbm, tables_ref),
                (loadings_hbm, loadings_ref),
                (shifts_hbm, shifts_ref),
                (intensity_hbm, samples),
            )
        )
    ]
    for load in loads:
        load.start()
    barrier = pltpu.get_barrier_semaphore()

    for step in range(8):
        pl.semaphore_signal(
            barrier,
            inc=1,
            device_id=at(x, y, (1 - z_hi) * 4 + step % 4, step // 4),
            device_id_type=MESH,
        )
    for step in range(1, 4):
        pl.semaphore_signal(
            barrier, inc=1, device_id=(freq, ((y + step) % 4) * 2 + z_hi), device_id_type=MESH
        )
    def greet(step, carry):
        pl.semaphore_signal(barrier, inc=1, device_id=((freq + step) % FREQ, mz), device_id_type=MESH)
        return carry

    lax.fori_loop(1, FREQ, greet, 0)
    loads[0].wait()
    own_rows = elution_ref[...]
    beside = jnp.concatenate([own_rows[16:24], own_rows[16:24]], axis=0)
    packed_rows[...] = jnp.concatenate([own_rows[0:16], beside], axis=1)

    pl.semaphore_wait(barrier, FREQ - 1 + 3 + 8)

    def remote(source, target, send, recv, device):
        return pltpu.make_async_remote_copy(
            src_ref=source, dst_ref=target, send_sem=send, recv_sem=recv, device_id=device, device_id_type=MESH
        )

    z_copies = [
        remote(
            packed_rows,
            gathered.at[z_lo, core],
            z_send.at[step],
            z_recv.at[z_lo, core],
            at(x, y, (z_mine + step) % 8, z_hi),
        )
        for step in range(8)
    ]
    for copy in z_copies[1:]:
        copy.start()

    @pl.when(z_hi != core)
    def _():
        z_copies[0].start()

    @pl.when(z_hi == core)
    def _():
        gathered[z_lo, core] = packed_rows[...]

    close = z_lo // 2
    near = close * (1 - abs(z_hi - core)) + (1 - close) * abs(z_hi - core)

    def half_of(colour_is_own, half):
        return near if (half == 0) == colour_is_own else 1 - near

    left16 = lax.broadcasted_iota(jnp.int32, (16, LANES), 1) < 64
    left8 = left16[:8]

    def merge(half):
        for index in range(2):
            source = 2 * half_of(True, half) + index
            for source_core in range(2):
                itself = jnp.logical_and(z_hi == core, jnp.logical_and(z_lo == source, core == source_core))

                @pl.when(jnp.logical_not(itself))
                def _(source=source, source_core=source_core):
                    spot = gathered.at[source, source_core]
                    remote(packed_rows, spot, z_send.at[0], z_recv.at[source, source_core], partner).wait_recv()

            zero, one = gathered[source, 0], gathered[source, 1]
            blocks[core, x, y, source, 0:16] = jnp.where(left16, zero, half_turn(one))
            blocks[core, x, y, source, 16:24] = jnp.where(left8, half_turn(zero[:8]), one[:8])

    def piece(colour_is_own, colour, dx, dy, half):
        start = 2 * half_of(colour_is_own, half)
        return blocks.at[colour, (x + dx) % 4, (y + dy) % 4, pl.ds(start, 2)]

    class Colour:
        def __init__(self, colour):
            self.colour = colour

        def offsets(self, a, b):
            return (a, b) if self.colour == 0 else (b, a)

        def send(self, a, b, a_step, b_step, half, sem):
            source = piece(True, self.colour, *self.offsets(a, b), half)
            to_x, to_y = self.offsets(a_step, b_step)
            dx, dy = self.offsets((a - a_step) % 4, (b - b_step) % 4)
            device = at((x + to_x) % 4, (y + to_y) % 4, z_mine, self.colour)
            remote(source, source, sem, own_recv.at[dx, dy, half], device).start()

        def second(self, half):
            for step in STEPS:
                self.send(0, 0, step, 0, half, second_send)

        def third(self, a, half):
            for step in STEPS:
                self.send(a, 0, 0, step, half, third_send)

        def arrived(self, a, b, half):
            dx, dy = self.offsets(a, b)
            spot = piece(True, self.colour, dx, dy, half)
            remote(spot, spot, swap_send, own_recv.at[dx, dy, half], partner).wait_recv()
            if b == 0:
                self.third(a, half)
            self.swap(dx, dy, half)

        def swap(self, dx, dy, half):
            spot = piece(True, self.colour, dx, dy, half)
            remote(spot, spot, swap_send, swap_recv.at[dx, dy, half], partner).start()

        def open_up(self, half):
            if self.colour == 0:
                self.third(0, half)
                self.second(half)
            else:
                self.second(half)
                self.third(0, half)
            self.swap(0, 0, half)

        def first_arrivals(self, half):
            for a, b in ((3, 0), (1, 0), (0, 3), (0, 1), (2, 0), (0, 2)):
                self.arrived(a, b, half)

    def for_each_core(action):
        for colour in range(2):
            pl.when(core == colour)(functools.partial(action, Colour(colour)))

    def swapped(dx):
        for half in range(2):
            for dy in range(4):
                spot = piece(False, 1 - core, dx, dy, half)
                remote(spot, spot, swap_send, swap_recv.at[dx, dy, half], partner).wait_recv()

    def arrivals(spots):
        def action(colour):
            for half in range(2):
                for dx, dy in spots:
                    colour.arrived(*colour.offsets(dx, dy), half)

        return action

    loads[1].wait()
    loads[2].wait()
    lag_rows = lag_weights(
        weight_ref[...], tables_ref[:96, :ROWS], tables_ref[96:192], tables_ref[192:448], flip
    )
    for z in range(3):
        lags[z] = lag_rows[z]

    row = lax.broadcasted_iota(jnp.int32, (LANES, LANES), 0)
    lane = lax.broadcasted_iota(jnp.int32, (LANES, LANES), 1)
    upper = lane >= row

    def turned(z, g):
        base = jnp.broadcast_to(lags[z, pl.ds(g, 1), :], (LANES, LANES))
        return pltpu.roll(base, 0, 1, stride=1, stride_axis=0)

    def build(g, before):
        for z in range(3):
            here = turned(z, g)
            high, low = split(jnp.where(upper, here, before))
            toeplitz[0, 3 * g + z] = high
            toeplitz[1, 3 * g + z] = low
            before = here
        return before

    lax.fori_loop(0, 16, build, turned(2, 15))

    merge(0)
    for_each_core(lambda colour: colour.open_up(0))
    merge(1)
    for_each_core(lambda colour: colour.open_up(1))
    slab[0:128, :] = jnp.zeros((128, LANES), BF16)
    slab[128 + SLAB : 256 + SLAB, :] = jnp.zeros((128, LANES), BF16)
    for_each_core(lambda colour: colour.first_arrivals(0))
    for_each_core(lambda colour: colour.first_arrivals(1))

    left = lax.broadcasted_iota(jnp.int32, (24, LANES), 1) < 64
    begin = ((freq * 3 + 96 - 4) // 2) % ROWS

    def unpack(dx):
        x_at = (x + dx) % 4

        def unpack_one(zl_at, carry):
            low_rows, high_rows = [], []
            for y_at in range(4):
                for colour in range(2):
                    block = blocks[colour, x_at, y_at, zl_at]
                    rounded = block.astype(BF16).astype(F32)
                    rest = block - rounded
                    low_rows.append(jnp.where(left, rounded, half_turn(rest)))
                    high_rows.append(jnp.where(left, half_turn(rounded), rest))
            rows = jnp.concatenate(low_rows + high_rows, axis=0).astype(BF16)
            start = pl.multiple_of(zl_at * 384, 128)
            slab[pl.ds(128 + start, 384), :] = rows
            profile[pl.ds(pl.multiple_of(x_at * SLAB, 128) + start, 384), :] = rows
            return carry

        lax.fori_loop(0, 4, unpack_one, 0)

    def filtered(dx):
        first = ((x + dx) % 4) * 12 - 1 + 2 * ROWS - begin
        lines = []
        for part in range(2):
            for row_block in (0, 2):
                lines.append(
                    jnp.concatenate(
                        [toeplitz[part, (first + step - row_block) % ROWS] for step in range(13)], axis=1
                    )
                )
        rows = jnp.concatenate([slab[0 : 128 + SLAB, :], slab[128 : 256 + SLAB, :]], axis=1)
        value = jnp.dot(jnp.concatenate(lines, axis=0), rows, preferred_element_type=F32)
        total[...] += value

    total[...] = jnp.zeros_like(total)

    def slab_step(index, carry):
        dx = jnp.where(index == 0, 0, jnp.where(index == 1, 3, index - 1))
        swapped(dx)
        unpack(dx)
        filtered(dx)

        @pl.when(index == 0)
        def _():
            for_each_core(arrivals(((3, 3), (3, 1), (3, 2), (1, 3), (1, 1), (1, 2))))

        @pl.when(index == 1)
        def _():
            for_each_core(arrivals(((2, 3), (2, 1), (2, 2))))

        return carry

    lax.fori_loop(0, 4, slab_step, 0)

    for row_block in range(4):
        base = (row_block // 2) * 128
        cut = pl.ds((row_block % 2) * 128, 128)
        value = total[pl.ds(base, 128), cut] + total[pl.ds(256 + base, 128), cut]
        window[0, pl.ds(row_block * 128, 128), :] = value + half_turn(value)
        start = pl.multiple_of(((begin + row_block) % ROWS) * 128, 128)
        value = profile[pl.ds(start, 128), :].astype(F32)
        window[1, pl.ds(row_block * 128, 128), :] = value + half_turn(value)

    skip = pl.multiple_of((freq % 2) * 64, 64)
    for load in loads[3:]:
        load.wait()
    filtered_rows = window[0, pl.ds(skip, 448), :]
    plain_rows = window[1, pl.ds(skip, 448), :]
    quad = jnp.zeros((256, 256), F32)
    numer = jnp.zeros((COMP, CHANNELS), F32)
    stacks = []
    for pair_at in range(RUNS // 2):
        amount = jnp.concatenate([shifts_ref[2 * pair_at : 2 * pair_at + 1], shifts_ref[2 * pair_at + 1 : 2 * pair_at + 2]], axis=1)
        gain = jnp.concatenate(
            [loadings_ref[2 * pair_at : 2 * pair_at + 1], loadings_ref[2 * pair_at + 1 : 2 * pair_at + 2]], axis=1
        )
        moved = jnp.transpose(shifted(filtered_rows, 255 - amount) * gain)
        model_high, model_low = split(shifted(plain_rows, 255 - amount) * gain)
        high, low = split(moved)
        stacks.append((high, low))
        quad = quad + jnp.dot(
            jnp.concatenate([high, low], axis=0),
            jnp.concatenate([model_high, model_low], axis=1),
            preferred_element_type=F32,
        )
    corner = quad[:128, :128] + quad[:128, 128:] + quad[128:, :128]
    gram_own = corner[:64] + half_turn(corner[64:])
    left32 = lax.broadcasted_iota(jnp.int32, (32, LANES), 1) < 64
    gram_send[0] = jnp.where(left32, gram_own[:32], half_turn(gram_own[32:]))
    core_copy = remote(gram_send.at[0], gram_core, gram_sems.at[0], gram_sems.at[1], partner)
    core_copy.start()

    for run in range(RUNS):
        high, low = stacks[run // 2]
        cut = slice((run % 2) * 64, (run % 2) * 64 + 64)
        both = jnp.dot(
            jnp.concatenate([high[cut], low[cut]], axis=0), samples[run], preferred_element_type=F32
        )
        numer = numer + both[:64] + both[64:]
    by_channel = jnp.transpose(numer).reshape(FREQ // 2, 2, 2, 8, COMP)
    for side in range(2):
        num_send[side] = jnp.concatenate([by_channel[:, side, 0], by_channel[:, side, 1]], axis=2)
    num_swap = remote(num_send.at[1 - core], num_core, num_sem.at[2], num_sem.at[3], partner)
    num_swap.start()
    chip = freq // 2

    def send_num(step, carry):
        to = (chip + step) % (FREQ // 2)
        remote(num_half.at[to], num_recv.at[chip], num_sem.at[0], num_sem.at[1], (2 * to + core, mz)).start()
        return carry

    core_copy.wait()
    gram_send[1] = gram_send[0] + gram_core[...]
    x_copies = []
    for step in range(1, 4):
        copy = remote(
            gram_send.at[1],
            gram_x.at[step - 1],
            gram_sems.at[1 + step],
            gram_sems.at[4 + step],
            at((x + step) % 4, y, z_mine, core),
        )
        copy.start()
        x_copies.append(copy)
    for copy in z_copies[1:]:
        copy.wait_send()

    @pl.when(z_hi != core)
    def _():
        z_copies[0].wait_send()

    for spot, sem in ((blocks.at[0, 0, 0:3], second_send), (blocks.at[0, 0:3], third_send), (blocks.at[0], swap_send)):
        remote(spot, spot, sem, z_recv.at[0, 0], partner).wait_send()

    for copy in x_copies:
        copy.wait()
    gram_send[2] = (gram_send[1] + gram_x[0]) + (gram_x[1] + gram_x[2])
    z_grams = []
    for step in range(1, 4):
        copy = remote(
            gram_send.at[2],
            gram_z.at[step - 1],
            gram_sems.at[7 + step],
            gram_sems.at[10 + step],
            at(x, y, z_hi * 4 + (z_lo + step) % 4, core),
        )
        copy.start()
        z_grams.append(copy)
    num_swap.wait()
    num_half[...] = num_send[core] + num_core[...]
    lax.fori_loop(1, FREQ // 2, send_num, 0)
    for copy in z_grams:
        copy.wait()
    packed = (gram_send[2] + gram_z[0]) + (gram_z[1] + gram_z[2])

    row64 = lax.broadcasted_iota(jnp.int32, (COMP, LANES), 0)
    lane64 = lax.broadcasted_iota(jnp.int32, (COMP, LANES), 1)
    unit = (lane64 == row64 + COMP).astype(F32)
    matrix = jnp.where(lane64 < COMP, jnp.concatenate([packed, half_turn(packed)], axis=0), unit)
    def clear(value, top, low, columns, step):
        one, two = columns
        one_top, one_low = one[step : step + 1], one[step + 1 : step + 2]
        two_top, two_low = two[step : step + 1], two[step + 1 : step + 2]
        scale = 1.0 / (one_top * two_low - two_top * one_low)
        top_new = (two_low * top - two_top * low) * scale
        low_new = (one_top * low - one_low * top) * scale
        rest = value - one * top_new - two * low_new
        return jnp.where(row64 == step, top_new, jnp.where(row64 == step + 1, low_new, rest))

    for step in range(0, COMP, 4):
        columns = [jnp.broadcast_to(matrix[:, at_ : at_ + 1], matrix.shape) for at_ in range(step, step + 4)]
        first_two = columns[:2]
        last_two = [
            clear(value, value[step : step + 1], value[step + 1 : step + 2], first_two, step) for value in columns[2:]
        ]
        matrix = clear(matrix, matrix[step : step + 1], matrix[step + 1 : step + 2], first_two, step)
        matrix = clear(matrix, matrix[step + 2 : step + 3], matrix[step + 3 : step + 4], last_two, step + 2)
    inverse = matrix[:, COMP:]

    others = num_recv.at[0 : FREQ // 2 - 1]
    num_all = remote(others, others, num_sem.at[0], num_sem.at[1], partner)
    num_all.wait_recv()
    num_recv[chip] = num_half[chip]
    summed = jnp.sum(num_recv[...], axis=0)
    own_channels = jnp.concatenate([summed[:, :64], summed[:, 64:]], axis=0)
    out_ref[...] = lax.dot_general(
        own_channels, inverse, (((1,), (1,)), ((), ())), precision=HIGHEST, preferred_element_type=F32
    )

    num_all.wait_send()


def on_device(intensity, elution, loadings, shifts, bin_weight):
    vmem = pl.BlockSpec(memory_space=pltpu.VMEM)
    dma = pltpu.SemaphoreType.DMA
    def held(value):
        return pltpu.with_memory_space_constraint(value, pltpu.HBM)

    by_channel = pl.pallas_call(
        kernel,
        out_shape=jax.ShapeDtypeStruct((OWN, COMP), F32),
        in_specs=[pl.BlockSpec(memory_space=pltpu.HBM)] * 6,
        out_specs=vmem,
        scratch_shapes=[
            pltpu.VMEM((24, COMP), F32),
            pltpu.VMEM((RUNS, COMP), F32),
            pltpu.VMEM((RUNS, COMP), jnp.int32),
            pltpu.VMEM((ROWS, LANES), F32),
            pltpu.VMEM((448, LANES), F32),
            pltpu.VMEM((RUNS, BLOCK, CHANNELS), BF16),
            pltpu.VMEM((16, LANES), F32),
            pltpu.VMEM((4, 2, 16, LANES), F32),
            pltpu.VMEM((2, 4, 4, 4, 24, LANES), F32),
            pltpu.VMEM((LENGTH, LANES), BF16),
            pltpu.VMEM((SLAB + 256, LANES), BF16),
            pltpu.VMEM((3, 16, LANES), F32),
            pltpu.VMEM((LANES, LANES), F32),
            pltpu.VMEM((2, ROWS, LANES, LANES), BF16),
            pltpu.VMEM((512, 256), F32),
            pltpu.VMEM((2, WINDOW, LANES), F32),
            pltpu.VMEM((3, 32, LANES), F32),
            pltpu.VMEM((32, LANES), F32),
            pltpu.VMEM((3, 32, LANES), F32),
            pltpu.VMEM((3, 32, LANES), F32),
            pltpu.VMEM((2, FREQ // 2, 8, LANES), F32),
            pltpu.VMEM((FREQ // 2, 8, LANES), F32),
            pltpu.VMEM((FREQ // 2, 8, LANES), F32),
            pltpu.VMEM((FREQ // 2, 8, LANES), F32),
            dma((6,)),
            dma((8,)),
            dma((4, 2)),
            dma,
            dma,
            dma((4, 4, 2)),
            dma,
            dma((4, 4, 2)),
            dma((14,)),
            dma((4,)),
        ],
        compiler_params=pltpu.CompilerParams(
            collective_id=0, has_side_effects=True, vmem_limit_bytes=32 * 1024 * 1024
        ),
    )(*map(held, (elution, loadings, shifts, bin_weight.reshape(ROWS, LANES), transform_tables(), intensity)))
    return by_channel.T


def solution(mesh):
    in_specs = (P(None, "freq", "mz"), P(("freq", "mz"), None), P(), P(), P())
    out_specs = P(None, ("mz", "freq"))
    return jax.shard_map(on_device, mesh=mesh, in_specs=in_specs, out_specs=out_specs, check_vma=False)
```

```python
import functools
import math

import jax
import jax.numpy as jnp
import numpy as np
from jax import lax
from jax.experimental import pallas as pl
from jax.experimental.pallas import tpu as pltpu
from jax.sharding import PartitionSpec as P

MESH = pl.DeviceIdType.MESH
HIGHEST = lax.Precision.HIGHEST
F32 = jnp.float32
BF16 = jnp.bfloat16

LENGTH = 6144
ROWS = 48
LANES = 128
RUNS = 8
COMP = 64
BLOCK = 192
CHANNELS = 512
FREQ = 32
OWN = 16
SLAB = 768
STEPS = (1, 3, 2)
WINDOW = 640


def transform_tables():
    x48 = np.arange(ROWS)
    b128 = np.arange(LANES)
    inner = 2.0 * np.pi / ROWS * ((x48[:, None] * x48[None, :]) % ROWS)
    middle = 2.0 * np.pi / LENGTH * ((x48[:, None] * b128[None, :]) % LENGTH)
    outer = 2.0 * np.pi / LANES * ((b128[:, None] * b128[None, :]) % LANES)
    first = np.concatenate([np.cos(inner), np.sin(inner)], axis=0)
    first = np.pad(first, ((0, 0), (0, LANES - ROWS)))
    turn = np.concatenate([np.cos(middle), np.sin(middle)], axis=0)
    last = np.concatenate([np.cos(outer), -np.sin(outer)], axis=0) / LENGTH
    return jnp.asarray(np.concatenate([first, turn, last], axis=0).astype(np.float32))


def split(value):
    high = value.astype(BF16)
    low = (value - high.astype(F32)).astype(BF16)
    return high, low


def half_turn(value):
    return pltpu.roll(value, 64, 1)


def lag_weights(weight, first, turn, last, flip):
    inner = jnp.dot(first, weight, precision=HIGHEST, preferred_element_type=F32)
    cos_part, sin_part = inner[:ROWS], inner[ROWS:]
    tcos, tsin = turn[:ROWS], turn[ROWS:]
    real = cos_part * tcos - sin_part * tsin
    imag = cos_part * tsin + sin_part * tcos
    both = jnp.concatenate([real, imag], axis=1)
    by_x = jnp.dot(both, last, precision=HIGHEST, preferred_element_type=F32)
    padded = jnp.concatenate([by_x, jnp.zeros((LANES - ROWS, LANES), F32)], axis=0)
    flip[...] = jnp.transpose(padded)
    lane = lax.broadcasted_iota(jnp.int32, (16, LANES), 1)

    def part(index, shift):
        rows = flip[pl.ds(index, 16, stride=8), :]
        return rows if shift == 0 else pltpu.roll(rows, shift, 1)

    first_row = jnp.where(lane < 48, part(0, 0), jnp.where(lane < 96, part(1, 48), part(2, 96)))
    second_row = jnp.where(
        lane < 16, part(2, 96), jnp.where(lane < 64, part(3, 16), jnp.where(lane < 112, part(4, 64), part(5, 112)))
    )
    third_row = jnp.where(lane < 32, part(5, 112), jnp.where(lane < 80, part(6, 32), part(7, 80)))
    return first_row, second_row, third_row


def shifted(window, amount):
    value = window
    for bit in (128, 64, 32, 16, 8):
        rows = BLOCK + bit
        value = jnp.where((amount & bit) != 0, value[bit : bit + rows], value[0:rows])
    for bit in (4, 2, 1):
        value = jnp.where((amount & bit) != 0, pltpu.roll(value, value.shape[0] - bit, 0), value)
    return pltpu.roll(value, value.shape[0] - 1, 0)[0:BLOCK]


def kernel(
    elution_hbm,
    loadings_hbm,
    shifts_hbm,
    weight_hbm,
    tables_hbm,
    intensity_hbm,
    out_ref,
    elution_ref,
    loadings_ref,
    shifts_ref,
    weight_ref,
    tables_ref,
    samples,
    packed_rows,
    gathered,
    blocks,
    profile,
    slab,
    lags,
    flip,
    toeplitz,
    total,
    window,
    exchange_send,
    exchange_recv,
    models,
    gram_send,
    gram_core,
    gram_x,
    gram_z,
    num_send,
    num_core,
    num_half,
    num_recv,
    load_sems,
    z_send,
    z_recv,
    second_send,
    third_send,
    own_recv,
    exchange_sem,
    gram_sems,
    num_sem,
):
    freq = lax.axis_index("freq")
    mz = lax.axis_index("mz")
    core = freq % 2
    z_lo = (freq // 2) % 4
    x = freq // 8
    y = mz // 2
    z_hi = mz % 2
    def at(x_to, y_to, z_to, core_to):
        return (x_to * 8 + (z_to % 4) * 2 + core_to, y_to * 2 + z_to // 4)

    partner = (freq + 1 - 2 * core, mz)
    z_mine = z_hi * 4 + z_lo

    loads = [
        pltpu.make_async_copy(source, target, load_sems.at[index])
        for index, (source, target) in enumerate(
            (
                (elution_hbm, elution_ref),
                (weight_hbm, weight_ref),
                (tables_hbm, tables_ref),
                (loadings_hbm, loadings_ref),
                (shifts_hbm, shifts_ref),
                (intensity_hbm, samples),
            )
        )
    ]
    for load in loads:
        load.start()
    barrier = pltpu.get_barrier_semaphore()

    def greet(device):
        pl.semaphore_signal(barrier, inc=1, device_id=device, device_id_type=MESH)

    for step in (4, 3, 5, 2, 6, 1, 7):
        for core_at in range(2):
            greet(at(x, y, (z_mine + step) % 8, core_at))
    for step in (2, 1, 3):
        greet((freq, ((y + step) % 4) * 2 + z_hi))
        greet((((x + step) % 4) * 8 + freq % 8, mz))
    greet(partner)
    loads[0].wait()
    for group in range(3):
        start = 4 * group
        packed_rows[group] = jnp.concatenate(
            [elution_ref[start : start + 4, :], elution_ref[12 + start : 16 + start, :]], axis=1
        )

    pl.semaphore_wait(barrier, 14 + 6 + 1)

    def remote(source, target, send, recv, device):
        return pltpu.make_async_remote_copy(
            src_ref=source, dst_ref=target, send_sem=send, recv_sem=recv, device_id=device, device_id_type=MESH
        )

    z_copies = [
        remote(
            packed_rows,
            gathered.at[z_hi, z_lo % 2, core],
            z_send.at[step],
            z_recv.at[z_hi, z_lo % 2, core],
            at(x, y, (z_mine + step) % 8, z_lo // 2),
        )
        for step in range(8)
    ]
    for step in (4, 3, 5, 2, 6, 1, 7):
        z_copies[step].start()

    @pl.when(z_lo // 2 != core)
    def _():
        z_copies[0].start()

    @pl.when(z_lo // 2 == core)
    def _():
        gathered[z_hi, z_lo % 2, core] = packed_rows[...]

    left4 = lax.broadcasted_iota(jnp.int32, (4, LANES), 1) < 64

    def merge():
        for zh_at in range(2):
            for zl_at in range(2):
                for source_core in range(2):
                    spot = gathered.at[zh_at, zl_at, source_core]
                    itself = jnp.logical_and(
                        jnp.logical_and(z_lo // 2 == core, z_hi == zh_at),
                        jnp.logical_and(z_lo % 2 == zl_at, core == source_core),
                    )

                    @pl.when(jnp.logical_not(itself))
                    def _(spot=spot, sem=z_recv.at[zh_at, zl_at, source_core]):
                        remote(packed_rows, spot, z_send.at[0], sem, partner).wait_recv()

        for zh_at in range(2):
            for zl_at in range(2):
                for group in range(3):
                    zero, one = gathered[zh_at, zl_at, 0, group], gathered[zh_at, zl_at, 1, group]
                    start = 24 * zh_at + 4 * group
                    blocks[x, y, zl_at, start : start + 4] = jnp.where(left4, zero, half_turn(one))
                    blocks[x, y, zl_at, start + 12 : start + 16] = jnp.where(left4, half_turn(zero), one)

    def piece(dx, dy):
        return blocks.at[(x + dx) % 4, (y + dy) % 4]

    class Colour:
        def __init__(self, colour):
            self.colour = colour

        def offsets(self, a, b):
            return (a, b) if self.colour == 0 else (b, a)

        def send(self, a, b, a_step, b_step, sem):
            source = piece(*self.offsets(a, b))
            to_x, to_y = self.offsets(a_step, b_step)
            dx, dy = self.offsets((a - a_step) % 4, (b - b_step) % 4)
            device = at((x + to_x) % 4, (y + to_y) % 4, z_mine, self.colour)
            remote(source, source, sem, own_recv.at[dx, dy], device).start()

        def second(self):
            for step in STEPS:
                self.send(0, 0, step, 0, second_send)

        def third(self, a, steps):
            for step in steps:
                self.send(a, 0, 0, step, third_send)

        def open_up(self):
            if self.colour == 0:
                self.third(0, STEPS)
                self.second()
            else:
                self.second()
                self.third(0, STEPS[:2])

        def pass_on(self):
            for a in (3, 1, 2):
                arrived(*self.offsets(a, 0))
                self.third(a, STEPS if self.colour == 0 else STEPS[:2])
            if self.colour == 1:
                for a in (0, 3, 1, 2):
                    self.third(a, STEPS[2:])

    def arrived(dx, dy):
        spot = piece(dx, dy)
        remote(spot, spot, second_send, own_recv.at[dx, dy], partner).wait_recv()

    def for_each_core(action):
        for colour in range(2):
            pl.when(core == colour)(functools.partial(action, Colour(colour)))

    def slab_arrived(dx):
        @pl.when(core == 0)
        def _():
            for dy in (3, 1, 2):
                arrived(dx, dy)

        @pl.when(jnp.logical_and(core == 1, dx != 0))
        def _():
            for dy in (0, 3, 1, 2):
                arrived(dx, dy)

    loads[1].wait()
    loads[2].wait()
    lag_rows = lag_weights(
        weight_ref[...], tables_ref[:96, :ROWS], tables_ref[96:192], tables_ref[192:448], flip
    )
    for z in range(3):
        lags[z] = lag_rows[z]

    row = lax.broadcasted_iota(jnp.int32, (LANES, LANES), 0)
    lane = lax.broadcasted_iota(jnp.int32, (LANES, LANES), 1)
    upper = lane >= row

    def turned(z, g):
        base = jnp.broadcast_to(lags[z, pl.ds(g, 1), :], (LANES, LANES))
        return pltpu.roll(base, 0, 1, stride=1, stride_axis=0)

    def build(g, before):
        for z in range(3):
            here = turned(z, g)
            high, low = split(jnp.where(upper, here, before))
            toeplitz[0, 3 * g + z] = high
            toeplitz[1, 3 * g + z] = low
            before = here
        return before

    lax.fori_loop(0, 16, build, turned(2, 15))

    merge()
    for_each_core(lambda colour: colour.open_up())
    slab[0:128, :] = jnp.zeros((128, LANES), BF16)
    slab[128 + SLAB : 256 + SLAB, :] = jnp.zeros((128, LANES), BF16)
    total[...] = jnp.zeros_like(total)
    for_each_core(lambda colour: colour.pass_on())

    left48 = lax.broadcasted_iota(jnp.int32, (48, LANES), 1) < 64
    begin = ((freq // 2) * 3 + ROWS - 2) % ROWS

    def unpack(x_at):
        def unpack_one(zl_at, carry):
            low_rows, high_rows = [], []
            for y_at in range(4):
                block = blocks[x_at, y_at, zl_at]
                rounded = block.astype(BF16).astype(F32)
                rest = block - rounded
                low_rows.append(jnp.where(left48, rounded, half_turn(rest)))
                high_rows.append(jnp.where(left48, half_turn(rounded), rest))
            rows = jnp.concatenate(low_rows + high_rows, axis=0).astype(BF16)
            start = pl.multiple_of(zl_at * 384, 128)
            slab[pl.ds(128 + start, 384), :] = rows
            profile[pl.ds(pl.multiple_of(x_at * SLAB, 128) + start, 384), :] = rows
            return carry

        lax.fori_loop(0, 2, unpack_one, 0)

    def filtered(x_at):
        first = x_at * 12 + core * 6 - 1 + 2 * ROWS - begin
        lines = []
        for part in range(2):
            for row_block in (0, 2, 4):
                lines.append(
                    jnp.concatenate(
                        [toeplitz[part, (first + step - row_block) % ROWS] for step in range(7)], axis=1
                    )
                )
        rows = jnp.concatenate([slab[0 : 128 + SLAB, :], slab[128 : 256 + SLAB, :]], axis=1)
        total[...] += jnp.dot(jnp.concatenate(lines, axis=0), rows, preferred_element_type=F32)

    left224 = lax.broadcasted_iota(jnp.int32, (224, LANES), 1) < 64

    def exchange(kind):
        return remote(exchange_send.at[kind], exchange_recv.at[kind], exchange_sem.at[kind, 0], exchange_sem.at[kind, 1], partner)

    def give(kind):
        start = pl.multiple_of((1 - core) * 192, 64)
        top = window[kind, pl.ds(start, 224), :]
        exchange_send[kind] = jnp.where(left224, top, window[kind, pl.ds(start + 224, 224), :])
        exchange(kind).start()

    def take(kind):
        exchange(kind).wait()
        both = exchange_recv[kind]
        turned_both = half_turn(both)
        top = jnp.where(left224, both, turned_both)
        rest = jnp.where(left224, turned_both, both)
        own = window[kind, pl.ds(pl.multiple_of(core * 192, 64), 448), :]
        return own + jnp.concatenate([top, rest], axis=0)

    def give_profile():
        for row_block in range(5):
            at_block = (begin + row_block) % ROWS
            cut = pl.ds(row_block * 128, 128)
            held_here = (at_block % 12) // 6 == core

            @pl.when(held_here)
            def _(at_block=at_block, cut=cut):
                start = pl.multiple_of((at_block // 12) * SLAB + (at_block % 6) * 128, 128)
                value = profile[pl.ds(start, 128), :].astype(F32)
                window[1, cut, :] = value + half_turn(value)

            @pl.when(jnp.logical_not(held_here))
            def _(cut=cut):
                window[1, cut, :] = jnp.zeros((128, LANES), F32)

        give(1)

    def slab_step(index, carry):
        dx = jnp.where(index == 0, 0, jnp.where(index == 1, 3, index - 1))
        x_at = (x + dx) % 4
        slab_arrived(dx)
        unpack(x_at)
        filtered(x_at)

        @pl.when(index == 1)
        def _():
            give_profile()

        return carry

    lax.fori_loop(0, 4, slab_step, 0)

    for row_block in range(5):
        base = (row_block // 2) * 128
        cut = pl.ds((row_block % 2) * 128, 128)
        value = total[pl.ds(base, 128), cut] + total[pl.ds(384 + base, 128), cut]
        window[0, pl.ds(row_block * 128, 128), :] = value + half_turn(value)
    give(0)
    for load in loads[3:]:
        load.wait()

    def by_pair(ref, pair_at):
        return jnp.concatenate([ref[2 * pair_at : 2 * pair_at + 1], ref[2 * pair_at + 1 : 2 * pair_at + 2]], axis=1)

    plain_rows = take(1)
    for pair_at in range(RUNS // 2):
        moved = shifted(plain_rows, 255 - by_pair(shifts_ref, pair_at)) * by_pair(loadings_ref, pair_at)
        high, low = split(moved)
        models[pair_at] = jnp.concatenate([high, low], axis=1)
    filtered_rows = take(0)
    quad = jnp.zeros((256, 256), F32)
    numer = jnp.zeros((COMP, CHANNELS), F32)
    stacks = []
    for pair_at in range(RUNS // 2):
        moved = shifted(filtered_rows, 255 - by_pair(shifts_ref, pair_at)) * by_pair(loadings_ref, pair_at)
        high, low = split(jnp.transpose(moved))
        stacks.append((high, low))
        quad = quad + jnp.dot(jnp.concatenate([high, low], axis=0), models[pair_at], preferred_element_type=F32)
    corner = quad[:128, :128] + quad[:128, 128:] + quad[128:, :128]
    gram_own = corner[:64] + half_turn(corner[64:])
    left32 = lax.broadcasted_iota(jnp.int32, (32, LANES), 1) < 64
    gram_send[0] = jnp.where(left32, gram_own[:32], half_turn(gram_own[32:]))
    core_copy = remote(gram_send.at[0], gram_core, gram_sems.at[0], gram_sems.at[1], partner)
    core_copy.start()

    for run in range(RUNS):
        high, low = stacks[run // 2]
        cut = slice((run % 2) * 64, (run % 2) * 64 + 64)
        both = jnp.dot(
            jnp.concatenate([high[cut], low[cut]], axis=0), samples[run], preferred_element_type=F32
        )
        numer = numer + both[:64] + both[64:]
    by_channel = jnp.transpose(numer).reshape(FREQ // 2, 2, 2, 8, COMP)
    for side in range(2):
        num_send[side] = jnp.concatenate([by_channel[:, side, 0], by_channel[:, side, 1]], axis=2)
    num_swap = remote(num_send.at[1 - core], num_core, num_sem.at[2], num_sem.at[3], partner)
    num_swap.start()
    chip = freq // 2

    def send_num(step, carry):
        to = (chip + step) % (FREQ // 2)
        remote(num_half.at[to], num_recv.at[chip], num_sem.at[0], num_sem.at[1], (2 * to + core, mz)).start()
        return carry

    core_copy.wait()
    gram_send[1] = gram_send[0] + gram_core[...]
    x_copies = []
    for step in range(1, 4):
        copy = remote(
            gram_send.at[1],
            gram_x.at[step - 1],
            gram_sems.at[1 + step],
            gram_sems.at[4 + step],
            at((x + step) % 4, y, z_mine, core),
        )
        copy.start()
        x_copies.append(copy)
    for copy in z_copies[1:]:
        copy.wait_send()

    @pl.when(z_lo // 2 != core)
    def _():
        z_copies[0].wait_send()

    for spot, sem in ((blocks.at[0, 0:3], second_send), (blocks.at[0:3], third_send)):
        remote(spot, spot, sem, exchange_sem.at[0, 1], partner).wait_send()

    for copy in x_copies:
        copy.wait()
    gram_send[2] = (gram_send[1] + gram_x[0]) + (gram_x[1] + gram_x[2])
    z_grams = []
    for step in range(1, 4):
        copy = remote(
            gram_send.at[2],
            gram_z.at[step - 1],
            gram_sems.at[7 + step],
            gram_sems.at[10 + step],
            at(x, y, z_hi * 4 + (z_lo + step) % 4, core),
        )
        copy.start()
        z_grams.append(copy)
    num_swap.wait()
    num_half[...] = num_send[core] + num_core[...]
    lax.fori_loop(1, FREQ // 2, send_num, 0)
    for copy in z_grams:
        copy.wait()
    packed = (gram_send[2] + gram_z[0]) + (gram_z[1] + gram_z[2])

    row64 = lax.broadcasted_iota(jnp.int32, (COMP, LANES), 0)
    lane64 = lax.broadcasted_iota(jnp.int32, (COMP, LANES), 1)
    unit = (lane64 == row64 + COMP).astype(F32)
    matrix = jnp.where(lane64 < COMP, jnp.concatenate([packed, half_turn(packed)], axis=0), unit)
    def clear(value, top, low, columns, step):
        one, two = columns
        one_top, one_low = one[step : step + 1], one[step + 1 : step + 2]
        two_top, two_low = two[step : step + 1], two[step + 1 : step + 2]
        scale = 1.0 / (one_top * two_low - two_top * one_low)
        top_new = (two_low * top - two_top * low) * scale
        low_new = (one_top * low - one_low * top) * scale
        rest = value - one * top_new - two * low_new
        return jnp.where(row64 == step, top_new, jnp.where(row64 == step + 1, low_new, rest))

    for step in range(0, COMP, 4):
        columns = [jnp.broadcast_to(matrix[:, at_ : at_ + 1], matrix.shape) for at_ in range(step, step + 4)]
        first_two = columns[:2]
        last_two = [
            clear(value, value[step : step + 1], value[step + 1 : step + 2], first_two, step) for value in columns[2:]
        ]
        matrix = clear(matrix, matrix[step : step + 1], matrix[step + 1 : step + 2], first_two, step)
        matrix = clear(matrix, matrix[step + 2 : step + 3], matrix[step + 3 : step + 4], last_two, step + 2)
    inverse = matrix[:, COMP:]

    others = num_recv.at[0 : FREQ // 2 - 1]
    num_all = remote(others, others, num_sem.at[0], num_sem.at[1], partner)
    num_all.wait_recv()
    num_recv[chip] = num_half[chip]
    summed = jnp.sum(num_recv[...], axis=0)
    own_channels = jnp.concatenate([summed[:, :64], summed[:, 64:]], axis=0)
    out_ref[...] = lax.dot_general(
        own_channels, inverse, (((1,), (1,)), ((), ())), precision=HIGHEST, preferred_element_type=F32
    )

    num_all.wait_send()


def on_device(intensity, elution, loadings, shifts, bin_weight):
    vmem = pl.BlockSpec(memory_space=pltpu.VMEM)
    dma = pltpu.SemaphoreType.DMA
    def held(value):
        return pltpu.with_memory_space_constraint(value, pltpu.HBM)

    by_channel = pl.pallas_call(
        kernel,
        out_shape=jax.ShapeDtypeStruct((OWN, COMP), F32),
        in_specs=[pl.BlockSpec(memory_space=pltpu.HBM)] * 6,
        out_specs=vmem,
        scratch_shapes=[
            pltpu.VMEM((24, COMP), F32),
            pltpu.VMEM((RUNS, COMP), F32),
            pltpu.VMEM((RUNS, COMP), jnp.int32),
            pltpu.VMEM((ROWS, LANES), F32),
            pltpu.VMEM((448, LANES), F32),
            pltpu.VMEM((RUNS, BLOCK, CHANNELS), BF16),
            pltpu.VMEM((3, 4, LANES), F32),
            pltpu.VMEM((2, 2, 2, 3, 4, LANES), F32),
            pltpu.VMEM((4, 4, 2, 48, LANES), F32),
            pltpu.VMEM((4 * SLAB, LANES), BF16),
            pltpu.VMEM((SLAB + 256, LANES), BF16),
            pltpu.VMEM((3, 16, LANES), F32),
            pltpu.VMEM((LANES, LANES), F32),
            pltpu.VMEM((2, ROWS, LANES, LANES), BF16),
            pltpu.VMEM((768, 256), F32),
            pltpu.VMEM((2, WINDOW, LANES), F32),
            pltpu.VMEM((2, 224, LANES), F32),
            pltpu.VMEM((2, 224, LANES), F32),
            pltpu.VMEM((RUNS // 2, BLOCK, 2 * LANES), BF16),
            pltpu.VMEM((3, 32, LANES), F32),
            pltpu.VMEM((32, LANES), F32),
            pltpu.VMEM((3, 32, LANES), F32),
            pltpu.VMEM((3, 32, LANES), F32),
            pltpu.VMEM((2, FREQ // 2, 8, LANES), F32),
            pltpu.VMEM((FREQ // 2, 8, LANES), F32),
            pltpu.VMEM((FREQ // 2, 8, LANES), F32),
            pltpu.VMEM((FREQ // 2, 8, LANES), F32),
            dma((6,)),
            dma((8,)),
            dma((2, 2, 2)),
            dma,
            dma,
            dma((4, 4)),
            dma((2, 2)),
            dma((14,)),
            dma((4,)),
        ],
        compiler_params=pltpu.CompilerParams(
            collective_id=0, has_side_effects=True, vmem_limit_bytes=32 * 1024 * 1024
        ),
    )(*map(held, (elution, loadings, shifts, bin_weight.reshape(ROWS, LANES), transform_tables(), intensity)))
    return by_channel.T


def solution(mesh):
    in_specs = (P(None, "freq", "mz"), P(("freq", "mz"), None), P(), P(), P())
    out_specs = P(None, ("mz", "freq"))
    return jax.shard_map(on_device, mesh=mesh, in_specs=in_specs, out_specs=out_specs, check_vma=False)
```

```python
import functools
import math

import jax
import jax.numpy as jnp
import numpy as np
from jax import lax
from jax.experimental import pallas as pl
from jax.experimental.pallas import tpu as pltpu
from jax.sharding import PartitionSpec as P

MESH = pl.DeviceIdType.MESH
HIGHEST = lax.Precision.HIGHEST
F32 = jnp.float32
BF16 = jnp.bfloat16

LENGTH = 6144
ROWS = 48
LANES = 128
RUNS = 8
COMP = 64
BLOCK = 192
CHANNELS = 512
FREQ = 32
OWN = 16
SLAB = 768
STEPS = (1, 3, 2)
WINDOW = 640


def transform_tables():
    x48 = np.arange(ROWS)
    b128 = np.arange(LANES)
    inner = 2.0 * np.pi / ROWS * ((x48[:, None] * x48[None, :]) % ROWS)
    middle = 2.0 * np.pi / LENGTH * ((x48[:, None] * b128[None, :]) % LENGTH)
    outer = 2.0 * np.pi / LANES * ((b128[:, None] * b128[None, :]) % LANES)
    first = np.concatenate([np.cos(inner), np.sin(inner)], axis=0)
    first = np.pad(first, ((0, 0), (0, LANES - ROWS)))
    turn = np.concatenate([np.cos(middle), np.sin(middle)], axis=0)
    last = np.concatenate([np.cos(outer), -np.sin(outer)], axis=0) / LENGTH
    return jnp.asarray(np.concatenate([first, turn, last], axis=0).astype(np.float32))


def split(value):
    high = value.astype(BF16)
    low = (value - high.astype(F32)).astype(BF16)
    return high, low


def half_turn(value):
    return pltpu.roll(value, 64, 1)


def lag_weights(weight, first, turn, last, flip):
    inner = jnp.dot(first, weight, precision=HIGHEST, preferred_element_type=F32)
    cos_part, sin_part = inner[:ROWS], inner[ROWS:]
    tcos, tsin = turn[:ROWS], turn[ROWS:]
    real = cos_part * tcos - sin_part * tsin
    imag = cos_part * tsin + sin_part * tcos
    both = jnp.concatenate([real, imag], axis=1)
    by_x = jnp.dot(both, last, precision=HIGHEST, preferred_element_type=F32)
    padded = jnp.concatenate([by_x, jnp.zeros((LANES - ROWS, LANES), F32)], axis=0)
    flip[...] = jnp.transpose(padded)
    lane = lax.broadcasted_iota(jnp.int32, (16, LANES), 1)

    def part(index, shift):
        rows = flip[pl.ds(index, 16, stride=8), :]
        return rows if shift == 0 else pltpu.roll(rows, shift, 1)

    first_row = jnp.where(lane < 48, part(0, 0), jnp.where(lane < 96, part(1, 48), part(2, 96)))
    second_row = jnp.where(
        lane < 16, part(2, 96), jnp.where(lane < 64, part(3, 16), jnp.where(lane < 112, part(4, 64), part(5, 112)))
    )
    third_row = jnp.where(lane < 32, part(5, 112), jnp.where(lane < 80, part(6, 32), part(7, 80)))
    return first_row, second_row, third_row


def shifted(window, amount):
    value = window
    for bit in (128, 64, 32, 16, 8):
        rows = BLOCK + bit
        value = jnp.where((amount & bit) != 0, value[bit : bit + rows], value[0:rows])
    for bit in (4, 2, 1):
        value = jnp.where((amount & bit) != 0, pltpu.roll(value, value.shape[0] - bit, 0), value)
    return pltpu.roll(value, value.shape[0] - 1, 0)[0:BLOCK]


def kernel(
    elution_hbm,
    loadings_hbm,
    shifts_hbm,
    weight_hbm,
    tables_hbm,
    intensity_hbm,
    out_ref,
    elution_ref,
    loadings_ref,
    shifts_ref,
    weight_ref,
    tables_ref,
    samples,
    packed_rows,
    gathered,
    blocks,
    profile,
    slab,
    lags,
    flip,
    toeplitz,
    total,
    window,
    exchange_send,
    exchange_recv,
    models,
    gram_send,
    gram_core,
    gram_x,
    gram_z,
    num_send,
    num_core,
    num_half,
    num_recv,
    load_sems,
    z_send,
    z_recv,
    second_send,
    third_send,
    own_recv,
    exchange_sem,
    gram_sems,
    num_sem,
):
    freq = lax.axis_index("freq")
    mz = lax.axis_index("mz")
    core = freq % 2
    z_lo = (freq // 2) % 4
    x = freq // 8
    y = mz // 2
    z_hi = mz % 2
    def at(x_to, y_to, z_to, core_to):
        return (x_to * 8 + (z_to % 4) * 2 + core_to, y_to * 2 + z_to // 4)

    partner = (freq + 1 - 2 * core, mz)
    z_mine = z_hi * 4 + z_lo

    loads = [
        pltpu.make_async_copy(source, target, load_sems.at[index])
        for index, (source, target) in enumerate(
            (
                (elution_hbm, elution_ref),
                (weight_hbm, weight_ref),
                (tables_hbm, tables_ref),
                (loadings_hbm, loadings_ref),
                (shifts_hbm, shifts_ref),
                (intensity_hbm, samples),
            )
        )
    ]
    for load in loads:
        load.start()
    barrier = pltpu.get_barrier_semaphore()

    def greet(device):
        pl.semaphore_signal(barrier, inc=1, device_id=device, device_id_type=MESH)

    for step in (4, 3, 5, 2, 6, 1, 7):
        for core_at in range(2):
            greet(at(x, y, (z_mine + step) % 8, core_at))
    for step in (2, 1, 3):
        greet((freq, ((y + step) % 4) * 2 + z_hi))
        greet((((x + step) % 4) * 8 + freq % 8, mz))
    greet(partner)
    loads[0].wait()
    for group in range(3):
        start = 4 * group
        packed_rows[group] = jnp.concatenate(
            [elution_ref[start : start + 4, :], elution_ref[12 + start : 16 + start, :]], axis=1
        )

    pl.semaphore_wait(barrier, 14 + 6 + 1)

    def remote(source, target, send, recv, device):
        return pltpu.make_async_remote_copy(
            src_ref=source, dst_ref=target, send_sem=send, recv_sem=recv, device_id=device, device_id_type=MESH
        )

    z_copies = [
        remote(
            packed_rows,
            gathered.at[z_hi, z_lo % 2, core],
            z_send.at[step],
            z_recv.at[z_hi, z_lo % 2, core],
            at(x, y, (z_mine + step) % 8, z_lo // 2),
        )
        for step in range(8)
    ]
    for step in (4, 3, 5, 2, 6, 1, 7):
        z_copies[step].start()

    @pl.when(z_lo // 2 != core)
    def _():
        z_copies[0].start()

    @pl.when(z_lo // 2 == core)
    def _():
        gathered[z_hi, z_lo % 2, core] = packed_rows[...]

    left4 = lax.broadcasted_iota(jnp.int32, (4, LANES), 1) < 64

    def merge():
        for zh_at in range(2):
            for zl_at in range(2):
                for source_core in range(2):
                    spot = gathered.at[zh_at, zl_at, source_core]
                    itself = jnp.logical_and(
                        jnp.logical_and(z_lo // 2 == core, z_hi == zh_at),
                        jnp.logical_and(z_lo % 2 == zl_at, core == source_core),
                    )

                    @pl.when(jnp.logical_not(itself))
                    def _(spot=spot, sem=z_recv.at[zh_at, zl_at, source_core]):
                        remote(packed_rows, spot, z_send.at[0], sem, partner).wait_recv()

        for zh_at in range(2):
            for zl_at in range(2):
                for group in range(3):
                    zero, one = gathered[zh_at, zl_at, 0, group], gathered[zh_at, zl_at, 1, group]
                    start = 24 * zh_at + 4 * group
                    blocks[x, y, zl_at, start : start + 4] = jnp.where(left4, zero, half_turn(one))
                    blocks[x, y, zl_at, start + 12 : start + 16] = jnp.where(left4, half_turn(zero), one)

    def piece(dx, dy):
        return blocks.at[(x + dx) % 4, (y + dy) % 4]

    class Colour:
        def __init__(self, colour):
            self.colour = colour

        def offsets(self, a, b):
            return (a, b) if self.colour == 0 else (b, a)

        def send(self, a, b, a_step, b_step, sem):
            source = piece(*self.offsets(a, b))
            to_x, to_y = self.offsets(a_step, b_step)
            dx, dy = self.offsets((a - a_step) % 4, (b - b_step) % 4)
            device = at((x + to_x) % 4, (y + to_y) % 4, z_mine, self.colour)
            remote(source, source, sem, own_recv.at[dx, dy], device).start()

        def second(self):
            for step in STEPS:
                self.send(0, 0, step, 0, second_send)

        def third(self, a, steps):
            for step in steps:
                self.send(a, 0, 0, step, third_send)

        def open_up(self):
            self.second()
            self.third(0, STEPS if self.colour == 0 else STEPS[:2])

        def pass_on(self):
            for a in (3, 1, 2):
                arrived(*self.offsets(a, 0))
                self.third(a, STEPS if self.colour == 0 else STEPS[:2])
            if self.colour == 1:
                for a in (0, 3, 1, 2):
                    self.third(a, STEPS[2:])

    def arrived(dx, dy):
        spot = piece(dx, dy)
        remote(spot, spot, second_send, own_recv.at[dx, dy], partner).wait_recv()

    def for_each_core(action):
        for colour in range(2):
            pl.when(core == colour)(functools.partial(action, Colour(colour)))

    def slab_arrived(dx):
        @pl.when(core == 0)
        def _():
            for dy in (3, 1, 2):
                arrived(dx, dy)

        @pl.when(jnp.logical_and(core == 1, dx != 0))
        def _():
            for dy in (0, 3, 1, 2):
                arrived(dx, dy)

    loads[1].wait()
    loads[2].wait()
    lag_rows = lag_weights(
        weight_ref[...], tables_ref[:96, :ROWS], tables_ref[96:192], tables_ref[192:448], flip
    )
    for z in range(3):
        lags[z] = lag_rows[z]

    row = lax.broadcasted_iota(jnp.int32, (LANES, LANES), 0)
    lane = lax.broadcasted_iota(jnp.int32, (LANES, LANES), 1)
    upper = lane >= row

    def turned(z, g):
        base = jnp.broadcast_to(lags[z, pl.ds(g, 1), :], (LANES, LANES))
        return pltpu.roll(base, 0, 1, stride=1, stride_axis=0)

    def build(g, before):
        for z in range(3):
            here = turned(z, g)
            high, low = split(jnp.where(upper, here, before))
            toeplitz[0, 3 * g + z] = high
            toeplitz[1, 3 * g + z] = low
            before = here
        return before

    lax.fori_loop(0, 16, build, turned(2, 15))

    merge()
    for_each_core(lambda colour: colour.open_up())
    slab[0:128, :] = jnp.zeros((128, LANES), BF16)
    slab[128 + SLAB : 256 + SLAB, :] = jnp.zeros((128, LANES), BF16)
    total[...] = jnp.zeros_like(total)
    for_each_core(lambda colour: colour.pass_on())

    left48 = lax.broadcasted_iota(jnp.int32, (48, LANES), 1) < 64
    begin = ((freq // 2) * 3 + ROWS - 2) % ROWS

    def unpack(x_at):
        def unpack_one(zl_at, carry):
            low_rows, high_rows = [], []
            for y_at in range(4):
                block = blocks[x_at, y_at, zl_at]
                rounded = block.astype(BF16).astype(F32)
                rest = block - rounded
                low_rows.append(jnp.where(left48, rounded, half_turn(rest)))
                high_rows.append(jnp.where(left48, half_turn(rounded), rest))
            rows = jnp.concatenate(low_rows + high_rows, axis=0).astype(BF16)
            start = pl.multiple_of(zl_at * 384, 128)
            slab[pl.ds(128 + start, 384), :] = rows
            profile[pl.ds(pl.multiple_of(x_at * SLAB, 128) + start, 384), :] = rows
            return carry

        lax.fori_loop(0, 2, unpack_one, 0)

    def filtered(x_at):
        first = x_at * 12 + core * 6 - 1 + 2 * ROWS - begin
        lines = []
        for part in range(2):
            for row_block in (0, 2, 4):
                lines.append(
                    jnp.concatenate(
                        [toeplitz[part, (first + step - row_block) % ROWS] for step in range(7)], axis=1
                    )
                )
        rows = jnp.concatenate([slab[0 : 128 + SLAB, :], slab[128 : 256 + SLAB, :]], axis=1)
        total[...] += jnp.dot(jnp.concatenate(lines, axis=0), rows, preferred_element_type=F32)

    left224 = lax.broadcasted_iota(jnp.int32, (224, LANES), 1) < 64

    def exchange(kind):
        return remote(exchange_send.at[kind], exchange_recv.at[kind], exchange_sem.at[kind, 0], exchange_sem.at[kind, 1], partner)

    def give(kind):
        start = pl.multiple_of((1 - core) * 192, 64)
        top = window[kind, pl.ds(start, 224), :]
        exchange_send[kind] = jnp.where(left224, top, window[kind, pl.ds(start + 224, 224), :])
        exchange(kind).start()

    def take(kind):
        exchange(kind).wait()
        both = exchange_recv[kind]
        turned_both = half_turn(both)
        top = jnp.where(left224, both, turned_both)
        rest = jnp.where(left224, turned_both, both)
        own = window[kind, pl.ds(pl.multiple_of(core * 192, 64), 448), :]
        return own + jnp.concatenate([top, rest], axis=0)

    def give_profile():
        for row_block in range(5):
            at_block = (begin + row_block) % ROWS
            cut = pl.ds(row_block * 128, 128)
            held_here = (at_block % 12) // 6 == core

            @pl.when(held_here)
            def _(at_block=at_block, cut=cut):
                start = pl.multiple_of((at_block // 12) * SLAB + (at_block % 6) * 128, 128)
                value = profile[pl.ds(start, 128), :].astype(F32)
                window[1, cut, :] = value + half_turn(value)

            @pl.when(jnp.logical_not(held_here))
            def _(cut=cut):
                window[1, cut, :] = jnp.zeros((128, LANES), F32)

        give(1)

    def slab_step(index, carry):
        dx = jnp.where(index == 0, 0, jnp.where(index == 1, 3, index - 1))
        x_at = (x + dx) % 4
        slab_arrived(dx)
        unpack(x_at)
        filtered(x_at)

        @pl.when(index == 1)
        def _():
            give_profile()

        return carry

    lax.fori_loop(0, 4, slab_step, 0)

    for row_block in range(5):
        base = (row_block // 2) * 128
        cut = pl.ds((row_block % 2) * 128, 128)
        value = total[pl.ds(base, 128), cut] + total[pl.ds(384 + base, 128), cut]
        window[0, pl.ds(row_block * 128, 128), :] = value + half_turn(value)
    give(0)
    for load in loads[3:]:
        load.wait()

    def by_pair(ref, pair_at):
        return jnp.concatenate([ref[2 * pair_at : 2 * pair_at + 1], ref[2 * pair_at + 1 : 2 * pair_at + 2]], axis=1)

    plain_rows = take(1)
    for pair_at in range(RUNS // 2):
        moved = shifted(plain_rows, 255 - by_pair(shifts_ref, pair_at)) * by_pair(loadings_ref, pair_at)
        high, low = split(moved)
        models[pair_at] = jnp.concatenate([high, low], axis=1)
    filtered_rows = take(0)
    quad = jnp.zeros((256, 256), F32)
    numer = jnp.zeros((COMP, CHANNELS), F32)
    stacks = []
    for pair_at in range(RUNS // 2):
        moved = shifted(filtered_rows, 255 - by_pair(shifts_ref, pair_at)) * by_pair(loadings_ref, pair_at)
        high, low = split(jnp.transpose(moved))
        stacks.append((high, low))
        quad = quad + jnp.dot(jnp.concatenate([high, low], axis=0), models[pair_at], preferred_element_type=F32)
    corner = quad[:128, :128] + quad[:128, 128:] + quad[128:, :128]
    gram_own = corner[:64] + half_turn(corner[64:])
    left32 = lax.broadcasted_iota(jnp.int32, (32, LANES), 1) < 64
    gram_send[0] = jnp.where(left32, gram_own[:32], half_turn(gram_own[32:]))
    core_copy = remote(gram_send.at[0], gram_core, gram_sems.at[0], gram_sems.at[1], partner)
    core_copy.start()

    for run in range(RUNS):
        high, low = stacks[run // 2]
        cut = slice((run % 2) * 64, (run % 2) * 64 + 64)
        both = jnp.dot(
            jnp.concatenate([high[cut], low[cut]], axis=0), samples[run], preferred_element_type=F32
        )
        numer = numer + both[:64] + both[64:]
    by_channel = jnp.transpose(numer).reshape(FREQ // 2, 2, 2, 8, COMP)
    for side in range(2):
        num_send[side] = jnp.concatenate([by_channel[:, side, 0], by_channel[:, side, 1]], axis=2)
    num_swap = remote(num_send.at[1 - core], num_core, num_sem.at[2], num_sem.at[3], partner)
    num_swap.start()
    chip = freq // 2

    def send_num(step, carry):
        to = (chip + step) % (FREQ // 2)
        remote(num_half.at[to], num_recv.at[chip], num_sem.at[0], num_sem.at[1], (2 * to + core, mz)).start()
        return carry

    core_copy.wait()
    gram_send[1] = gram_send[0] + gram_core[...]
    x_copies = []
    for step in range(1, 4):
        copy = remote(
            gram_send.at[1],
            gram_x.at[step - 1],
            gram_sems.at[1 + step],
            gram_sems.at[4 + step],
            at((x + step) % 4, y, z_mine, core),
        )
        copy.start()
        x_copies.append(copy)
    for copy in z_copies[1:]:
        copy.wait_send()

    @pl.when(z_lo // 2 != core)
    def _():
        z_copies[0].wait_send()

    for spot, sem in ((blocks.at[0, 0:3], second_send), (blocks.at[0:3], third_send)):
        remote(spot, spot, sem, exchange_sem.at[0, 1], partner).wait_send()

    num_swap.wait()
    num_half[...] = num_send[core] + num_core[...]
    lax.fori_loop(1, FREQ // 2, send_num, 0)
    for copy in x_copies:
        copy.wait()
    gram_send[2] = (gram_send[1] + gram_x[0]) + (gram_x[1] + gram_x[2])
    z_grams = []
    for step in range(1, 4):
        copy = remote(
            gram_send.at[2],
            gram_z.at[step - 1],
            gram_sems.at[7 + step],
            gram_sems.at[10 + step],
            at(x, y, z_hi * 4 + (z_lo + step) % 4, core),
        )
        copy.start()
        z_grams.append(copy)
    for copy in z_grams:
        copy.wait()
    packed = (gram_send[2] + gram_z[0]) + (gram_z[1] + gram_z[2])

    row64 = lax.broadcasted_iota(jnp.int32, (COMP, LANES), 0)
    lane64 = lax.broadcasted_iota(jnp.int32, (COMP, LANES), 1)
    row8 = row64[:8]
    gram = jnp.concatenate([packed, half_turn(packed)], axis=0)
    diagonal = jnp.where(lane64 == row64, gram, 0.0)
    scale_rows = jnp.broadcast_to(lax.rsqrt(jnp.sum(diagonal, axis=1, keepdims=True)), gram.shape)
    scale_lanes = lax.rsqrt(jnp.sum(diagonal, axis=0, keepdims=True))
    unit = jnp.where(lane64 == row64 + COMP, scale_rows, 0.0)
    whole = jnp.where(lane64 < COMP, gram * scale_rows * scale_lanes, unit)
    matrix = [whole[8 * at_ : 8 * at_ + 8] for at_ in range(8)]

    def line(value, step):
        return value[step // 8][step % 8 : step % 8 + 1]

    def pivot(columns, step):
        one, two = columns
        return line(one, step) * line(two, step + 1) - line(two, step) * line(one, step + 1)

    def clear(value, columns, step, scale):
        one, two = columns
        at_, row_at = step // 8, step % 8
        top, low = line(value, step), line(value, step + 1)
        top_new = (line(two, step + 1) * top - line(two, step) * low) * scale
        low_new = (line(one, step) * low - line(one, step + 1) * top) * scale
        rest = [v - o * top_new - t * low_new for v, o, t in zip(value, one, two)]
        rest[at_] = jnp.where(row8 == row_at, top_new, jnp.where(row8 == row_at + 1, low_new, rest[at_]))
        return rest

    for step in range(0, COMP, 8):
        columns = [
            [jnp.broadcast_to(block[:, at_ : at_ + 1], block.shape) for block in matrix] for at_ in range(step, step + 8)
        ]
        for at_ in range(step, step + 8, 2):
            pair, columns = columns[:2], columns[2:]
            scale = 1.0 / pivot(pair, at_)
            columns = [clear(value, pair, at_, scale) for value in columns]
            matrix = clear(matrix, pair, at_, scale)
    inverse = (jnp.concatenate(matrix, axis=0) * scale_rows)[:, COMP:]

    inverse_both = jnp.concatenate(split(inverse), axis=0)
    others = num_recv.at[0 : FREQ // 2 - 1]
    num_all = remote(others, others, num_sem.at[0], num_sem.at[1], partner)
    num_all.wait_recv()
    num_recv[chip] = num_half[chip]
    summed = jnp.sum(num_recv[...], axis=0)
    own_channels = jnp.concatenate([summed[:, :64], summed[:, 64:]], axis=0)
    high, low = split(own_channels)
    parts = lax.dot_general(
        jnp.concatenate([high, low], axis=0), inverse_both, (((1,), (1,)), ((), ())), preferred_element_type=F32
    )
    out_ref[...] = (parts[:OWN, :COMP] + parts[:OWN, COMP:]) + parts[OWN:, :COMP]

    num_all.wait_send()


def on_device(intensity, elution, loadings, shifts, bin_weight):
    vmem = pl.BlockSpec(memory_space=pltpu.VMEM)
    dma = pltpu.SemaphoreType.DMA
    def held(value):
        return pltpu.with_memory_space_constraint(value, pltpu.HBM)

    by_channel = pl.pallas_call(
        kernel,
        out_shape=jax.ShapeDtypeStruct((OWN, COMP), F32),
        in_specs=[pl.BlockSpec(memory_space=pltpu.HBM)] * 6,
        out_specs=vmem,
        scratch_shapes=[
            pltpu.VMEM((24, COMP), F32),
            pltpu.VMEM((RUNS, COMP), F32),
            pltpu.VMEM((RUNS, COMP), jnp.int32),
            pltpu.VMEM((ROWS, LANES), F32),
            pltpu.VMEM((448, LANES), F32),
            pltpu.VMEM((RUNS, BLOCK, CHANNELS), BF16),
            pltpu.VMEM((3, 4, LANES), F32),
            pltpu.VMEM((2, 2, 2, 3, 4, LANES), F32),
            pltpu.VMEM((4, 4, 2, 48, LANES), F32),
            pltpu.VMEM((4 * SLAB, LANES), BF16),
            pltpu.VMEM((SLAB + 256, LANES), BF16),
            pltpu.VMEM((3, 16, LANES), F32),
            pltpu.VMEM((LANES, LANES), F32),
            pltpu.VMEM((2, ROWS, LANES, LANES), BF16),
            pltpu.VMEM((768, 256), F32),
            pltpu.VMEM((2, WINDOW, LANES), F32),
            pltpu.VMEM((2, 224, LANES), F32),
            pltpu.VMEM((2, 224, LANES), F32),
            pltpu.VMEM((RUNS // 2, BLOCK, 2 * LANES), BF16),
            pltpu.VMEM((3, 32, LANES), F32),
            pltpu.VMEM((32, LANES), F32),
            pltpu.VMEM((3, 32, LANES), F32),
            pltpu.VMEM((3, 32, LANES), F32),
            pltpu.VMEM((2, FREQ // 2, 8, LANES), F32),
            pltpu.VMEM((FREQ // 2, 8, LANES), F32),
            pltpu.VMEM((FREQ // 2, 8, LANES), F32),
            pltpu.VMEM((FREQ // 2, 8, LANES), F32),
            dma((6,)),
            dma((8,)),
            dma((2, 2, 2)),
            dma,
            dma,
            dma((4, 4)),
            dma((2, 2)),
            dma((14,)),
            dma((4,)),
        ],
        compiler_params=pltpu.CompilerParams(
            collective_id=0, has_side_effects=True, vmem_limit_bytes=32 * 1024 * 1024
        ),
    )(*map(held, (elution, loadings, shifts, bin_weight.reshape(ROWS, LANES), transform_tables(), intensity)))
    return by_channel.T


def solution(mesh):
    in_specs = (P(None, "freq", "mz"), P(("freq", "mz"), None), P(), P(), P())
    out_specs = P(None, ("mz", "freq"))
    return jax.shard_map(on_device, mesh=mesh, in_specs=in_specs, out_specs=out_specs, check_vma=False)
```

```python
import functools
import math

import jax
import jax.numpy as jnp
import numpy as np
from jax import lax
from jax.experimental import pallas as pl
from jax.experimental.pallas import tpu as pltpu
from jax.sharding import PartitionSpec as P

MESH = pl.DeviceIdType.MESH
HIGHEST = lax.Precision.HIGHEST
F32 = jnp.float32
BF16 = jnp.bfloat16

LENGTH = 6144
ROWS = 48
LANES = 128
RUNS = 8
COMP = 64
BLOCK = 192
CHANNELS = 512
FREQ = 32
OWN = 16
SLAB = 768
STEPS = (1, 3, 2)
WINDOW = 640


def transform_tables():
    x48 = np.arange(ROWS)
    b128 = np.arange(LANES)
    inner = 2.0 * np.pi / ROWS * ((x48[:, None] * x48[None, :]) % ROWS)
    middle = 2.0 * np.pi / LENGTH * ((x48[:, None] * b128[None, :]) % LENGTH)
    outer = 2.0 * np.pi / LANES * ((b128[:, None] * b128[None, :]) % LANES)
    first = np.concatenate([np.cos(inner), np.sin(inner)], axis=0)
    first = np.pad(first, ((0, 0), (0, LANES - ROWS)))
    turn = np.concatenate([np.cos(middle), np.sin(middle)], axis=0)
    last = np.concatenate([np.cos(outer), -np.sin(outer)], axis=0) / LENGTH
    return jnp.asarray(np.concatenate([first, turn, last], axis=0).astype(np.float32))


def split(value):
    high = value.astype(BF16)
    low = (value - high.astype(F32)).astype(BF16)
    return high, low


def half_turn(value):
    return pltpu.roll(value, 64, 1)


def lag_weights(weight, first, turn, last, flip):
    inner = jnp.dot(first, weight, precision=HIGHEST, preferred_element_type=F32)
    cos_part, sin_part = inner[:ROWS], inner[ROWS:]
    tcos, tsin = turn[:ROWS], turn[ROWS:]
    real = cos_part * tcos - sin_part * tsin
    imag = cos_part * tsin + sin_part * tcos
    both = jnp.concatenate([real, imag], axis=1)
    by_x = jnp.dot(both, last, precision=HIGHEST, preferred_element_type=F32)
    padded = jnp.concatenate([by_x, jnp.zeros((LANES - ROWS, LANES), F32)], axis=0)
    flip[...] = jnp.transpose(padded)
    lane = lax.broadcasted_iota(jnp.int32, (16, LANES), 1)

    def part(index, shift):
        rows = flip[pl.ds(index, 16, stride=8), :]
        return rows if shift == 0 else pltpu.roll(rows, shift, 1)

    first_row = jnp.where(lane < 48, part(0, 0), jnp.where(lane < 96, part(1, 48), part(2, 96)))
    second_row = jnp.where(
        lane < 16, part(2, 96), jnp.where(lane < 64, part(3, 16), jnp.where(lane < 112, part(4, 64), part(5, 112)))
    )
    third_row = jnp.where(lane < 32, part(5, 112), jnp.where(lane < 80, part(6, 32), part(7, 80)))
    return first_row, second_row, third_row


def shifted(window, amount):
    value = window
    for bit in (128, 64, 32, 16, 8):
        rows = BLOCK + bit
        value = jnp.where((amount & bit) != 0, value[bit : bit + rows], value[0:rows])
    for bit in (4, 2, 1):
        value = jnp.where((amount & bit) != 0, pltpu.roll(value, value.shape[0] - bit, 0), value)
    return pltpu.roll(value, value.shape[0] - 1, 0)[0:BLOCK]


def kernel(
    elution_hbm,
    loadings_hbm,
    shifts_hbm,
    weight_hbm,
    tables_hbm,
    intensity_hbm,
    out_ref,
    elution_ref,
    loadings_ref,
    shifts_ref,
    weight_ref,
    tables_ref,
    samples,
    packed_rows,
    gathered,
    blocks,
    profile,
    slab,
    lags,
    flip,
    toeplitz,
    total,
    window,
    exchange_send,
    exchange_recv,
    models,
    gram_send,
    gram_core,
    gram_x,
    gram_z,
    num_send,
    num_core,
    num_half,
    num_recv,
    load_sems,
    z_send,
    z_recv,
    second_send,
    third_send,
    own_recv,
    exchange_sem,
    gram_sems,
    num_sem,
):
    freq = lax.axis_index("freq")
    mz = lax.axis_index("mz")
    core = freq % 2
    z_lo = (freq // 2) % 4
    x = freq // 8
    y = mz // 2
    z_hi = mz % 2
    def at(x_to, y_to, z_to, core_to):
        return (x_to * 8 + (z_to % 4) * 2 + core_to, y_to * 2 + z_to // 4)

    partner = (freq + 1 - 2 * core, mz)
    z_mine = z_hi * 4 + z_lo

    loads = [
        pltpu.make_async_copy(source, target, load_sems.at[index])
        for index, (source, target) in enumerate(
            (
                (elution_hbm, elution_ref),
                (weight_hbm, weight_ref),
                (tables_hbm, tables_ref),
                (loadings_hbm, loadings_ref),
                (shifts_hbm, shifts_ref),
                (intensity_hbm, samples),
            )
        )
    ]
    for load in loads:
        load.start()
    barrier = pltpu.get_barrier_semaphore()

    def greet(device):
        pl.semaphore_signal(barrier, inc=1, device_id=device, device_id_type=MESH)

    for step in (4, 3, 5, 2, 6, 1, 7):
        for core_at in range(2):
            greet(at(x, y, (z_mine + step) % 8, core_at))
    for step in (2, 1, 3):
        greet((freq, ((y + step) % 4) * 2 + z_hi))
        greet((((x + step) % 4) * 8 + freq % 8, mz))
    greet(partner)
    loads[0].wait()
    for group in range(3):
        start = 4 * group
        packed_rows[group] = jnp.concatenate(
            [elution_ref[start : start + 4, :], elution_ref[12 + start : 16 + start, :]], axis=1
        )

    pl.semaphore_wait(barrier, 14 + 6 + 1)

    def remote(source, target, send, recv, device):
        return pltpu.make_async_remote_copy(
            src_ref=source, dst_ref=target, send_sem=send, recv_sem=recv, device_id=device, device_id_type=MESH
        )

    z_copies = [
        remote(
            packed_rows,
            gathered.at[z_hi, z_lo % 2, core],
            z_send.at[step],
            z_recv.at[z_hi, z_lo % 2, core],
            at(x, y, (z_mine + step) % 8, z_lo // 2),
        )
        for step in range(8)
    ]
    for step in (4, 3, 5, 2, 6, 1, 7):
        z_copies[step].start()

    @pl.when(z_lo // 2 != core)
    def _():
        z_copies[0].start()

    @pl.when(z_lo // 2 == core)
    def _():
        gathered[z_hi, z_lo % 2, core] = packed_rows[...]

    left4 = lax.broadcasted_iota(jnp.int32, (4, LANES), 1) < 64

    def merge():
        for zh_at in range(2):
            for zl_at in range(2):
                for source_core in range(2):
                    spot = gathered.at[zh_at, zl_at, source_core]
                    itself = jnp.logical_and(
                        jnp.logical_and(z_lo // 2 == core, z_hi == zh_at),
                        jnp.logical_and(z_lo % 2 == zl_at, core == source_core),
                    )

                    @pl.when(jnp.logical_not(itself))
                    def _(spot=spot, sem=z_recv.at[zh_at, zl_at, source_core]):
                        remote(packed_rows, spot, z_send.at[0], sem, partner).wait_recv()

        for zh_at in range(2):
            for zl_at in range(2):
                for group in range(3):
                    zero, one = gathered[zh_at, zl_at, 0, group], gathered[zh_at, zl_at, 1, group]
                    start = 24 * zh_at + 4 * group
                    blocks[x, y, zl_at, start : start + 4] = jnp.where(left4, zero, half_turn(one))
                    blocks[x, y, zl_at, start + 12 : start + 16] = jnp.where(left4, half_turn(zero), one)

    def piece(dx, dy):
        return blocks.at[(x + dx) % 4, (y + dy) % 4]

    class Colour:
        def __init__(self, colour):
            self.colour = colour

        def offsets(self, a, b):
            return (a, b) if self.colour == 0 else (b, a)

        def send(self, a, b, a_step, b_step, sem):
            source = piece(*self.offsets(a, b))
            to_x, to_y = self.offsets(a_step, b_step)
            dx, dy = self.offsets((a - a_step) % 4, (b - b_step) % 4)
            device = at((x + to_x) % 4, (y + to_y) % 4, z_mine, self.colour)
            remote(source, source, sem, own_recv.at[dx, dy], device).start()

        def second(self):
            for step in STEPS:
                self.send(0, 0, step, 0, second_send)

        def third(self, a, steps):
            for step in steps:
                self.send(a, 0, 0, step, third_send)

        def open_up(self):
            self.second()
            self.third(0, STEPS if self.colour == 0 else STEPS[:2])

        def pass_on(self):
            for a in (3, 1, 2):
                arrived(*self.offsets(a, 0))
                self.third(a, STEPS if self.colour == 0 else STEPS[:2])
            if self.colour == 1:
                for a in (0, 3, 1, 2):
                    self.third(a, STEPS[2:])

    def arrived(dx, dy):
        spot = piece(dx, dy)
        remote(spot, spot, second_send, own_recv.at[dx, dy], partner).wait_recv()

    def for_each_core(action):
        for colour in range(2):
            pl.when(core == colour)(functools.partial(action, Colour(colour)))

    def slab_arrived(dx):
        @pl.when(core == 0)
        def _():
            for dy in (3, 1, 2):
                arrived(dx, dy)

        @pl.when(jnp.logical_and(core == 1, dx != 0))
        def _():
            for dy in (0, 3, 1, 2):
                arrived(dx, dy)

    loads[1].wait()
    loads[2].wait()
    lag_rows = lag_weights(
        weight_ref[...], tables_ref[:96, :ROWS], tables_ref[96:192], tables_ref[192:448], flip
    )
    for z in range(3):
        lags[z] = lag_rows[z]

    row = lax.broadcasted_iota(jnp.int32, (LANES, LANES), 0)
    lane = lax.broadcasted_iota(jnp.int32, (LANES, LANES), 1)
    upper = lane >= row

    def turned(z, g):
        base = jnp.broadcast_to(lags[z, pl.ds(g, 1), :], (LANES, LANES))
        return pltpu.roll(base, 0, 1, stride=1, stride_axis=0)

    def build(g, before):
        for z in range(3):
            here = turned(z, g)
            high, low = split(jnp.where(upper, here, before))
            toeplitz[0, 3 * g + z] = high
            toeplitz[1, 3 * g + z] = low
            before = here
        return before

    lax.fori_loop(0, 16, build, turned(2, 15))

    merge()
    for_each_core(lambda colour: colour.open_up())
    slab[0:128, :] = jnp.zeros((128, LANES), BF16)
    slab[128 + SLAB : 256 + SLAB, :] = jnp.zeros((128, LANES), BF16)
    total[...] = jnp.zeros_like(total)
    for_each_core(lambda colour: colour.pass_on())

    left48 = lax.broadcasted_iota(jnp.int32, (48, LANES), 1) < 64
    begin = ((freq // 2) * 3 + ROWS - 2) % ROWS

    def unpack(x_at):
        for zl_at in range(2):
            low_rows, high_rows = [], []
            for y_at in range(4):
                block = blocks[x_at, y_at, zl_at]
                rounded = block.astype(BF16).astype(F32)
                rest = block - rounded
                low_rows.append(jnp.where(left48, rounded, half_turn(rest)))
                high_rows.append(jnp.where(left48, half_turn(rounded), rest))
            rows = jnp.concatenate(low_rows + high_rows, axis=0).astype(BF16)
            start = zl_at * 384
            slab[128 + start : 512 + start, :] = rows
            profile[pl.ds(pl.multiple_of(x_at * SLAB, 128) + start, 384), :] = rows

    def filtered(x_at):
        first = x_at * 12 + core * 6 - 1 + 2 * ROWS - begin
        lines = []
        for part in range(2):
            for row_block in (0, 2, 4):
                lines.append(
                    jnp.concatenate(
                        [toeplitz[part, (first + step - row_block) % ROWS] for step in range(7)], axis=1
                    )
                )
        rows = jnp.concatenate([slab[0 : 128 + SLAB, :], slab[128 : 256 + SLAB, :]], axis=1)
        total[...] += jnp.dot(jnp.concatenate(lines, axis=0), rows, preferred_element_type=F32)

    left224 = lax.broadcasted_iota(jnp.int32, (224, LANES), 1) < 64

    def exchange(kind):
        return remote(exchange_send.at[kind], exchange_recv.at[kind], exchange_sem.at[kind, 0], exchange_sem.at[kind, 1], partner)

    def give(kind):
        start = pl.multiple_of((1 - core) * 192, 64)
        top = window[kind, pl.ds(start, 224), :]
        exchange_send[kind] = jnp.where(left224, top, window[kind, pl.ds(start + 224, 224), :])
        exchange(kind).start()

    def take(kind):
        exchange(kind).wait()
        both = exchange_recv[kind]
        turned_both = half_turn(both)
        top = jnp.where(left224, both, turned_both)
        rest = jnp.where(left224, turned_both, both)
        own = window[kind, pl.ds(pl.multiple_of(core * 192, 64), 448), :]
        return own + jnp.concatenate([top, rest], axis=0)

    def give_profile():
        for row_block in range(5):
            at_block = (begin + row_block) % ROWS
            cut = pl.ds(row_block * 128, 128)
            held_here = (at_block % 12) // 6 == core

            @pl.when(held_here)
            def _(at_block=at_block, cut=cut):
                start = pl.multiple_of((at_block // 12) * SLAB + (at_block % 6) * 128, 128)
                value = profile[pl.ds(start, 128), :].astype(F32)
                window[1, cut, :] = value + half_turn(value)

            @pl.when(jnp.logical_not(held_here))
            def _(cut=cut):
                window[1, cut, :] = jnp.zeros((128, LANES), F32)

        give(1)

    def slab_step(index, carry):
        dx = jnp.where(index == 0, 0, jnp.where(index == 1, 3, index - 1))
        x_at = (x + dx) % 4
        slab_arrived(dx)
        unpack(x_at)
        filtered(x_at)

        @pl.when(index == 1)
        def _():
            give_profile()

        return carry

    lax.fori_loop(0, 4, slab_step, 0)

    for row_block in range(5):
        base = (row_block // 2) * 128
        cut = pl.ds((row_block % 2) * 128, 128)
        value = total[pl.ds(base, 128), cut] + total[pl.ds(384 + base, 128), cut]
        window[0, pl.ds(row_block * 128, 128), :] = value + half_turn(value)
    give(0)
    for load in loads[3:]:
        load.wait()

    def by_pair(ref, pair_at):
        return jnp.concatenate([ref[2 * pair_at : 2 * pair_at + 1], ref[2 * pair_at + 1 : 2 * pair_at + 2]], axis=1)

    plain_rows = take(1)
    for pair_at in range(RUNS // 2):
        moved = shifted(plain_rows, 255 - by_pair(shifts_ref, pair_at)) * by_pair(loadings_ref, pair_at)
        high, low = split(moved)
        models[pair_at] = jnp.concatenate([high, low], axis=1)
    filtered_rows = take(0)
    quad = jnp.zeros((256, 256), F32)
    numer = jnp.zeros((COMP, CHANNELS), F32)
    stacks = []
    for pair_at in range(RUNS // 2):
        moved = shifted(filtered_rows, 255 - by_pair(shifts_ref, pair_at)) * by_pair(loadings_ref, pair_at)
        high, low = (jnp.transpose(part) for part in split(moved))
        stacks.append((high, low))
        quad = quad + jnp.dot(jnp.concatenate([high, low], axis=0), models[pair_at], preferred_element_type=F32)
    corner = quad[:128, :128] + quad[:128, 128:] + quad[128:, :128]
    gram_own = corner[:64] + half_turn(corner[64:])
    left32 = lax.broadcasted_iota(jnp.int32, (32, LANES), 1) < 64
    gram_send[0] = jnp.where(left32, gram_own[:32], half_turn(gram_own[32:]))
    core_copy = remote(gram_send.at[0], gram_core, gram_sems.at[0], gram_sems.at[1], partner)
    core_copy.start()

    for run in range(RUNS):
        high, low = stacks[run // 2]
        cut = slice((run % 2) * 64, (run % 2) * 64 + 64)
        both = jnp.dot(
            jnp.concatenate([high[cut], low[cut]], axis=0), samples[run], preferred_element_type=F32
        )
        numer = numer + both[:64] + both[64:]
    by_channel = jnp.transpose(numer).reshape(FREQ // 2, 2, 2, 8, COMP)
    for side in range(2):
        num_send[side] = jnp.concatenate([by_channel[:, side, 0], by_channel[:, side, 1]], axis=2)
    num_swap = remote(num_send.at[1 - core], num_core, num_sem.at[2], num_sem.at[3], partner)
    num_swap.start()
    chip = freq // 2

    def send_num(step, carry):
        to = (chip + step) % (FREQ // 2)
        remote(num_half.at[to], num_recv.at[chip], num_sem.at[0], num_sem.at[1], (2 * to + core, mz)).start()
        return carry

    core_copy.wait()
    gram_send[1] = gram_send[0] + gram_core[...]
    x_copies = []
    for step in range(1, 4):
        copy = remote(
            gram_send.at[1],
            gram_x.at[step - 1],
            gram_sems.at[1 + step],
            gram_sems.at[4 + step],
            at((x + step) % 4, y, z_mine, core),
        )
        copy.start()
        x_copies.append(copy)
    for copy in z_copies[1:]:
        copy.wait_send()

    @pl.when(z_lo // 2 != core)
    def _():
        z_copies[0].wait_send()

    for spot, sem in ((blocks.at[0, 0:3], second_send), (blocks.at[0:3], third_send)):
        remote(spot, spot, sem, exchange_sem.at[0, 1], partner).wait_send()

    num_swap.wait()
    num_half[...] = num_send[core] + num_core[...]
    lax.fori_loop(1, FREQ // 2, send_num, 0)
    for copy in x_copies:
        copy.wait()
    gram_send[2] = (gram_send[1] + gram_x[0]) + (gram_x[1] + gram_x[2])
    z_grams = []
    for step in range(1, 4):
        copy = remote(
            gram_send.at[2],
            gram_z.at[step - 1],
            gram_sems.at[7 + step],
            gram_sems.at[10 + step],
            at(x, y, z_hi * 4 + (z_lo + step) % 4, core),
        )
        copy.start()
        z_grams.append(copy)
    for copy in z_grams:
        copy.wait()
    packed = (gram_send[2] + gram_z[0]) + (gram_z[1] + gram_z[2])

    row64 = lax.broadcasted_iota(jnp.int32, (COMP, LANES), 0)
    lane64 = lax.broadcasted_iota(jnp.int32, (COMP, LANES), 1)
    row8 = row64[:8]
    gram = jnp.concatenate([packed, half_turn(packed)], axis=0)
    diagonal = jnp.where(lane64 == row64, gram, 0.0)
    scale_rows = jnp.broadcast_to(lax.rsqrt(jnp.sum(diagonal, axis=1, keepdims=True)), gram.shape)
    scale_lanes = lax.rsqrt(jnp.sum(diagonal, axis=0, keepdims=True))
    unit = jnp.where(lane64 == row64 + COMP, scale_rows, 0.0)
    whole = jnp.where(lane64 < COMP, gram * scale_rows * scale_lanes, unit)
    matrix = [whole[8 * at_ : 8 * at_ + 8] for at_ in range(8)]

    def line(value, step):
        return value[step // 8][step % 8 : step % 8 + 1]

    def pivot(columns, step):
        one, two = columns
        return line(one, step) * line(two, step + 1) - line(two, step) * line(one, step + 1)

    def clear(value, columns, step, scale):
        one, two = columns
        at_, row_at = step // 8, step % 8
        top, low = line(value, step), line(value, step + 1)
        top_new = (line(two, step + 1) * top - line(two, step) * low) * scale
        low_new = (line(one, step) * low - line(one, step + 1) * top) * scale
        rest = [v - o * top_new - t * low_new for v, o, t in zip(value, one, two)]
        rest[at_] = jnp.where(row8 == row_at, top_new, jnp.where(row8 == row_at + 1, low_new, rest[at_]))
        return rest

    for step in range(0, COMP, 8):
        columns = [
            [jnp.broadcast_to(block[:, at_ : at_ + 1], block.shape) for block in matrix] for at_ in range(step, step + 8)
        ]
        for at_ in range(step, step + 8, 2):
            pair, columns = columns[:2], columns[2:]
            scale = 1.0 / pivot(pair, at_)
            columns = [clear(value, pair, at_, scale) for value in columns]
            matrix = clear(matrix, pair, at_, scale)
    inverse = (jnp.concatenate(matrix, axis=0) * scale_rows)[:, COMP:]

    inverse_both = jnp.concatenate(split(inverse), axis=0)
    others = num_recv.at[0 : FREQ // 2 - 1]
    num_all = remote(others, others, num_sem.at[0], num_sem.at[1], partner)
    num_all.wait_recv()
    num_recv[chip] = num_half[chip]
    summed = jnp.sum(num_recv[...], axis=0)
    own_channels = jnp.concatenate([summed[:, :64], summed[:, 64:]], axis=0)
    high, low = split(own_channels)
    parts = lax.dot_general(
        jnp.concatenate([high, low], axis=0), inverse_both, (((1,), (1,)), ((), ())), preferred_element_type=F32
    )
    out_ref[...] = (parts[:OWN, :COMP] + parts[:OWN, COMP:]) + parts[OWN:, :COMP]

    num_all.wait_send()


def on_device(intensity, elution, loadings, shifts, bin_weight):
    vmem = pl.BlockSpec(memory_space=pltpu.VMEM)
    dma = pltpu.SemaphoreType.DMA
    def held(value):
        return pltpu.with_memory_space_constraint(value, pltpu.HBM)

    by_channel = pl.pallas_call(
        kernel,
        out_shape=jax.ShapeDtypeStruct((OWN, COMP), F32),
        in_specs=[pl.BlockSpec(memory_space=pltpu.HBM)] * 6,
        out_specs=vmem,
        scratch_shapes=[
            pltpu.VMEM((24, COMP), F32),
            pltpu.VMEM((RUNS, COMP), F32),
            pltpu.VMEM((RUNS, COMP), jnp.int32),
            pltpu.VMEM((ROWS, LANES), F32),
            pltpu.VMEM((448, LANES), F32),
            pltpu.VMEM((RUNS, BLOCK, CHANNELS), BF16),
            pltpu.VMEM((3, 4, LANES), F32),
            pltpu.VMEM((2, 2, 2, 3, 4, LANES), F32),
            pltpu.VMEM((4, 4, 2, 48, LANES), F32),
            pltpu.VMEM((4 * SLAB, LANES), BF16),
            pltpu.VMEM((SLAB + 256, LANES), BF16),
            pltpu.VMEM((3, 16, LANES), F32),
            pltpu.VMEM((LANES, LANES), F32),
            pltpu.VMEM((2, ROWS, LANES, LANES), BF16),
            pltpu.VMEM((768, 256), F32),
            pltpu.VMEM((2, WINDOW, LANES), F32),
            pltpu.VMEM((2, 224, LANES), F32),
            pltpu.VMEM((2, 224, LANES), F32),
            pltpu.VMEM((RUNS // 2, BLOCK, 2 * LANES), BF16),
            pltpu.VMEM((3, 32, LANES), F32),
            pltpu.VMEM((32, LANES), F32),
            pltpu.VMEM((3, 32, LANES), F32),
            pltpu.VMEM((3, 32, LANES), F32),
            pltpu.VMEM((2, FREQ // 2, 8, LANES), F32),
            pltpu.VMEM((FREQ // 2, 8, LANES), F32),
            pltpu.VMEM((FREQ // 2, 8, LANES), F32),
            pltpu.VMEM((FREQ // 2, 8, LANES), F32),
            dma((6,)),
            dma((8,)),
            dma((2, 2, 2)),
            dma,
            dma,
            dma((4, 4)),
            dma((2, 2)),
            dma((14,)),
            dma((4,)),
        ],
        compiler_params=pltpu.CompilerParams(
            collective_id=0, has_side_effects=True, vmem_limit_bytes=32 * 1024 * 1024
        ),
    )(*map(held, (elution, loadings, shifts, bin_weight.reshape(ROWS, LANES), transform_tables(), intensity)))
    return by_channel.T


def solution(mesh):
    in_specs = (P(None, "freq", "mz"), P(("freq", "mz"), None), P(), P(), P())
    out_specs = P(None, ("mz", "freq"))
    return jax.shard_map(on_device, mesh=mesh, in_specs=in_specs, out_specs=out_specs, check_vma=False)
```

```python
import functools
import math

import jax
import jax.numpy as jnp
import numpy as np
from jax import lax
from jax.experimental import pallas as pl
from jax.experimental.pallas import tpu as pltpu
from jax.sharding import PartitionSpec as P

MESH = pl.DeviceIdType.MESH
HIGHEST = lax.Precision.HIGHEST
F32 = jnp.float32
BF16 = jnp.bfloat16

LENGTH = 6144
ROWS = 48
LANES = 128
RUNS = 8
COMP = 64
BLOCK = 192
CHANNELS = 512
FREQ = 32
OWN = 16
SLAB = 768
STEPS = (1, 3, 2)
WINDOW = 640


def transform_tables():
    x48 = np.arange(ROWS)
    b128 = np.arange(LANES)
    inner = 2.0 * np.pi / ROWS * ((x48[:, None] * x48[None, :]) % ROWS)
    middle = 2.0 * np.pi / LENGTH * ((x48[:, None] * b128[None, :]) % LENGTH)
    outer = 2.0 * np.pi / LANES * ((b128[:, None] * b128[None, :]) % LANES)
    first = np.concatenate([np.cos(inner), np.sin(inner)], axis=0)
    first = np.pad(first, ((0, 0), (0, LANES - ROWS)))
    turn = np.concatenate([np.cos(middle), np.sin(middle)], axis=0)
    last = np.concatenate([np.cos(outer), -np.sin(outer)], axis=0) / LENGTH
    return jnp.asarray(np.concatenate([first, turn, last], axis=0).astype(np.float32))


def split(value):
    high = value.astype(BF16)
    low = (value - high.astype(F32)).astype(BF16)
    return high, low


def half_turn(value):
    return pltpu.roll(value, 64, 1)


def lag_weights(weight, first, turn, last, flip):
    inner = jnp.dot(first, weight, precision=HIGHEST, preferred_element_type=F32)
    cos_part, sin_part = inner[:ROWS], inner[ROWS:]
    tcos, tsin = turn[:ROWS], turn[ROWS:]
    real = cos_part * tcos - sin_part * tsin
    imag = cos_part * tsin + sin_part * tcos
    both = jnp.concatenate([real, imag], axis=1)
    by_x = jnp.dot(both, last, precision=HIGHEST, preferred_element_type=F32)
    padded = jnp.concatenate([by_x, jnp.zeros((LANES - ROWS, LANES), F32)], axis=0)
    flip[...] = jnp.transpose(padded)
    lane = lax.broadcasted_iota(jnp.int32, (16, LANES), 1)

    def part(index, shift):
        rows = flip[pl.ds(index, 16, stride=8), :]
        return rows if shift == 0 else pltpu.roll(rows, shift, 1)

    first_row = jnp.where(lane < 48, part(0, 0), jnp.where(lane < 96, part(1, 48), part(2, 96)))
    second_row = jnp.where(
        lane < 16, part(2, 96), jnp.where(lane < 64, part(3, 16), jnp.where(lane < 112, part(4, 64), part(5, 112)))
    )
    third_row = jnp.where(lane < 32, part(5, 112), jnp.where(lane < 80, part(6, 32), part(7, 80)))
    return first_row, second_row, third_row


def shifted(window, amount):
    value = window
    for bit in (128, 64, 32, 16, 8):
        rows = BLOCK + bit
        value = jnp.where((amount & bit) != 0, value[bit : bit + rows], value[0:rows])
    for bit in (4, 2, 1):
        value = jnp.where((amount & bit) != 0, pltpu.roll(value, value.shape[0] - bit, 0), value)
    return pltpu.roll(value, value.shape[0] - 1, 0)[0:BLOCK]


def kernel(
    elution_hbm,
    loadings_hbm,
    shifts_hbm,
    weight_hbm,
    tables_hbm,
    intensity_hbm,
    out_ref,
    elution_ref,
    loadings_ref,
    shifts_ref,
    weight_ref,
    tables_ref,
    samples,
    packed_rows,
    gathered,
    blocks,
    profile,
    slab,
    lags,
    flip,
    toeplitz,
    total,
    window,
    exchange_send,
    exchange_recv,
    models,
    gram_send,
    gram_core,
    gram_x,
    gram_z,
    num_send,
    num_core,
    num_half,
    num_recv,
    load_sems,
    z_send,
    z_recv,
    second_send,
    third_send,
    own_recv,
    exchange_sem,
    gram_sems,
    num_sem,
):
    freq = lax.axis_index("freq")
    mz = lax.axis_index("mz")
    core = freq % 2
    z_lo = (freq // 2) % 4
    x = freq // 8
    y = mz // 2
    z_hi = mz % 2
    def at(x_to, y_to, z_to, core_to):
        return (x_to * 8 + (z_to % 4) * 2 + core_to, y_to * 2 + z_to // 4)

    partner = (freq + 1 - 2 * core, mz)
    z_mine = z_hi * 4 + z_lo

    loads = [
        pltpu.make_async_copy(source, target, load_sems.at[index])
        for index, (source, target) in enumerate(
            (
                (elution_hbm, elution_ref),
                (weight_hbm, weight_ref),
                (tables_hbm, tables_ref),
                (loadings_hbm, loadings_ref),
                (shifts_hbm, shifts_ref),
                (intensity_hbm, samples),
            )
        )
    ]
    for load in loads:
        load.start()
    barrier = pltpu.get_barrier_semaphore()

    def greet(device):
        pl.semaphore_signal(barrier, inc=1, device_id=device, device_id_type=MESH)

    for step in (4, 3, 5, 2, 6, 1, 7):
        for core_at in range(2):
            greet(at(x, y, (z_mine + step) % 8, core_at))
    for step in (2, 1, 3):
        greet((freq, ((y + step) % 4) * 2 + z_hi))
        greet((((x + step) % 4) * 8 + freq % 8, mz))
    greet(partner)
    loads[0].wait()
    for group in range(3):
        start = 4 * group
        packed_rows[group] = jnp.concatenate(
            [elution_ref[start : start + 4, :], elution_ref[12 + start : 16 + start, :]], axis=1
        )

    pl.semaphore_wait(barrier, 14 + 6 + 1)

    def remote(source, target, send, recv, device):
        return pltpu.make_async_remote_copy(
            src_ref=source, dst_ref=target, send_sem=send, recv_sem=recv, device_id=device, device_id_type=MESH
        )

    z_copies = [
        remote(
            packed_rows,
            gathered.at[z_hi, z_lo % 2, core],
            z_send.at[step],
            z_recv.at[z_hi, z_lo % 2, core],
            at(x, y, (z_mine + step) % 8, z_lo // 2),
        )
        for step in range(8)
    ]
    for step in (4, 3, 5, 2, 6, 1, 7):
        z_copies[step].start()

    @pl.when(z_lo // 2 != core)
    def _():
        z_copies[0].start()

    @pl.when(z_lo // 2 == core)
    def _():
        gathered[z_hi, z_lo % 2, core] = packed_rows[...]

    left4 = lax.broadcasted_iota(jnp.int32, (4, LANES), 1) < 64

    def merge():
        for zh_at in range(2):
            for zl_at in range(2):
                for source_core in range(2):
                    spot = gathered.at[zh_at, zl_at, source_core]
                    itself = jnp.logical_and(
                        jnp.logical_and(z_lo // 2 == core, z_hi == zh_at),
                        jnp.logical_and(z_lo % 2 == zl_at, core == source_core),
                    )

                    @pl.when(jnp.logical_not(itself))
                    def _(spot=spot, sem=z_recv.at[zh_at, zl_at, source_core]):
                        remote(packed_rows, spot, z_send.at[0], sem, partner).wait_recv()

        for zh_at in range(2):
            for zl_at in range(2):
                for group in range(3):
                    zero, one = gathered[zh_at, zl_at, 0, group], gathered[zh_at, zl_at, 1, group]
                    start = 24 * zh_at + 4 * group
                    blocks[x, y, zl_at, start : start + 4] = jnp.where(left4, zero, half_turn(one))
                    blocks[x, y, zl_at, start + 12 : start + 16] = jnp.where(left4, half_turn(zero), one)

    def piece(dx, dy):
        return blocks.at[(x + dx) % 4, (y + dy) % 4]

    class Colour:
        def __init__(self, colour):
            self.colour = colour

        def offsets(self, a, b):
            return (a, b) if self.colour == 0 else (b, a)

        def send(self, a, b, a_step, b_step, sem):
            source = piece(*self.offsets(a, b))
            to_x, to_y = self.offsets(a_step, b_step)
            dx, dy = self.offsets((a - a_step) % 4, (b - b_step) % 4)
            device = at((x + to_x) % 4, (y + to_y) % 4, z_mine, self.colour)
            remote(source, source, sem, own_recv.at[dx, dy], device).start()

        def second(self):
            for step in STEPS:
                self.send(0, 0, step, 0, second_send)

        def third(self, a, steps):
            for step in steps:
                self.send(a, 0, 0, step, third_send)

        def open_up(self):
            self.second()
            self.third(0, STEPS if self.colour == 0 else STEPS[:2])

        def pass_on(self):
            for a in (3, 1, 2):
                arrived(*self.offsets(a, 0))
                self.third(a, STEPS if self.colour == 0 else STEPS[:2])
            if self.colour == 1:
                for a in (0, 3, 1, 2):
                    self.third(a, STEPS[2:])

    def arrived(dx, dy):
        spot = piece(dx, dy)
        remote(spot, spot, second_send, own_recv.at[dx, dy], partner).wait_recv()

    def for_each_core(action):
        for colour in range(2):
            pl.when(core == colour)(functools.partial(action, Colour(colour)))

    def slab_arrived(dx):
        @pl.when(core == 0)
        def _():
            for dy in (3, 1, 2):
                arrived(dx, dy)

        @pl.when(jnp.logical_and(core == 1, dx != 0))
        def _():
            for dy in (0, 3, 1, 2):
                arrived(dx, dy)

    loads[1].wait()
    loads[2].wait()
    lag_rows = lag_weights(
        weight_ref[...], tables_ref[:96, :ROWS], tables_ref[96:192], tables_ref[192:448], flip
    )
    for z in range(3):
        lags[z] = lag_rows[z]

    row = lax.broadcasted_iota(jnp.int32, (LANES, LANES), 0)
    lane = lax.broadcasted_iota(jnp.int32, (LANES, LANES), 1)
    upper = lane >= row

    def turned(z, g):
        base = jnp.broadcast_to(lags[z, pl.ds(g, 1), :], (LANES, LANES))
        return pltpu.roll(base, 0, 1, stride=1, stride_axis=0)

    def build(g, before):
        for z in range(3):
            here = turned(z, g)
            high, low = split(jnp.where(upper, here, before))
            toeplitz[0, 3 * g + z] = high
            toeplitz[1, 3 * g + z] = low
            before = here
        return before

    lax.fori_loop(0, 16, build, turned(2, 15))

    merge()
    for_each_core(lambda colour: colour.open_up())
    slab[0:128, :] = jnp.zeros((128, LANES), BF16)
    slab[128 + SLAB : 256 + SLAB, :] = jnp.zeros((128, LANES), BF16)
    total[...] = jnp.zeros_like(total)
    for_each_core(lambda colour: colour.pass_on())

    left48 = lax.broadcasted_iota(jnp.int32, (48, LANES), 1) < 64
    begin = ((freq // 2) * 3 + ROWS - 2) % ROWS

    def unpack(x_at):
        for zl_at in range(2):
            low_rows, high_rows = [], []
            for y_at in range(4):
                block = blocks[x_at, y_at, zl_at]
                rounded = block.astype(BF16).astype(F32)
                rest = block - rounded
                low_rows.append(jnp.where(left48, rounded, half_turn(rest)))
                high_rows.append(jnp.where(left48, half_turn(rounded), rest))
            rows = jnp.concatenate(low_rows + high_rows, axis=0).astype(BF16)
            start = zl_at * 384
            slab[128 + start : 512 + start, :] = rows
            profile[pl.ds(pl.multiple_of(x_at * SLAB, 128) + start, 384), :] = rows

    def filtered(x_at):
        first = x_at * 12 + core * 6 - 1 + 2 * ROWS - begin
        lines = []
        for part in range(2):
            for row_block in (0, 2, 4):
                lines.append(
                    jnp.concatenate(
                        [toeplitz[part, (first + step - row_block) % ROWS] for step in range(7)], axis=1
                    )
                )
        rows = jnp.concatenate([slab[0 : 128 + SLAB, :], slab[128 : 256 + SLAB, :]], axis=1)
        total[...] += jnp.dot(jnp.concatenate(lines, axis=0), rows, preferred_element_type=F32)

    left224 = lax.broadcasted_iota(jnp.int32, (224, LANES), 1) < 64

    def exchange(kind):
        return remote(exchange_send.at[kind], exchange_recv.at[kind], exchange_sem.at[kind, 0], exchange_sem.at[kind, 1], partner)

    def give(kind):
        start = pl.multiple_of((1 - core) * 192, 64)
        top = window[kind, pl.ds(start, 224), :]
        exchange_send[kind] = jnp.where(left224, top, window[kind, pl.ds(start + 224, 224), :])
        exchange(kind).start()

    def take(kind):
        exchange(kind).wait()
        both = exchange_recv[kind]
        turned_both = half_turn(both)
        top = jnp.where(left224, both, turned_both)
        rest = jnp.where(left224, turned_both, both)
        own = window[kind, pl.ds(pl.multiple_of(core * 192, 64), 448), :]
        return own + jnp.concatenate([top, rest], axis=0)

    def give_profile():
        for row_block in range(5):
            at_block = (begin + row_block) % ROWS
            cut = pl.ds(row_block * 128, 128)
            held_here = (at_block % 12) // 6 == core

            @pl.when(held_here)
            def _(at_block=at_block, cut=cut):
                start = pl.multiple_of((at_block // 12) * SLAB + (at_block % 6) * 128, 128)
                value = profile[pl.ds(start, 128), :].astype(F32)
                window[1, cut, :] = value + half_turn(value)

            @pl.when(jnp.logical_not(held_here))
            def _(cut=cut):
                window[1, cut, :] = jnp.zeros((128, LANES), F32)

        give(1)

    def slab_step(index, carry):
        dx = jnp.where(index == 0, 0, jnp.where(index == 1, 3, index - 1))
        x_at = (x + dx) % 4
        slab_arrived(dx)
        unpack(x_at)
        filtered(x_at)

        @pl.when(index == jnp.where(z_lo == 0, 1, 0))
        def _():
            give_profile()

        return carry

    lax.fori_loop(0, 4, slab_step, 0)

    for row_block in range(5):
        base = (row_block // 2) * 128
        cut = pl.ds((row_block % 2) * 128, 128)
        value = total[pl.ds(base, 128), cut] + total[pl.ds(384 + base, 128), cut]
        window[0, pl.ds(row_block * 128, 128), :] = value + half_turn(value)
    give(0)
    for load in loads[3:]:
        load.wait()

    def by_pair(ref, pair_at):
        return jnp.concatenate([ref[2 * pair_at : 2 * pair_at + 1], ref[2 * pair_at + 1 : 2 * pair_at + 2]], axis=1)

    plain_rows = take(1)
    for pair_at in range(RUNS // 2):
        moved = shifted(plain_rows, 255 - by_pair(shifts_ref, pair_at)) * by_pair(loadings_ref, pair_at)
        high, low = split(moved)
        models[pair_at] = jnp.concatenate([high, low], axis=1)
    filtered_rows = take(0)
    quad = jnp.zeros((256, 256), F32)
    numer = jnp.zeros((COMP, CHANNELS), F32)
    stacks = []
    for pair_at in range(RUNS // 2):
        moved = shifted(filtered_rows, 255 - by_pair(shifts_ref, pair_at)) * by_pair(loadings_ref, pair_at)
        high, low = (jnp.transpose(part) for part in split(moved))
        stacks.append((high, low))
        quad = quad + jnp.dot(jnp.concatenate([high, low], axis=0), models[pair_at], preferred_element_type=F32)
    corner = quad[:128, :128] + quad[:128, 128:] + quad[128:, :128]
    gram_own = corner[:64] + half_turn(corner[64:])
    left32 = lax.broadcasted_iota(jnp.int32, (32, LANES), 1) < 64
    gram_send[0] = jnp.where(left32, gram_own[:32], half_turn(gram_own[32:]))
    core_copy = remote(gram_send.at[0], gram_core, gram_sems.at[0], gram_sems.at[1], partner)
    core_copy.start()

    for run in range(RUNS):
        high, low = stacks[run // 2]
        cut = slice((run % 2) * 64, (run % 2) * 64 + 64)
        both = jnp.dot(
            jnp.concatenate([high[cut], low[cut]], axis=0), samples[run], preferred_element_type=F32
        )
        numer = numer + both[:64] + both[64:]
    by_channel = jnp.transpose(numer).reshape(FREQ // 2, 2, 2, 8, COMP)
    for side in range(2):
        num_send[side] = jnp.concatenate([by_channel[:, side, 0], by_channel[:, side, 1]], axis=2)
    num_swap = remote(num_send.at[1 - core], num_core, num_sem.at[2], num_sem.at[3], partner)
    num_swap.start()
    chip = freq // 2

    def send_num(step, carry):
        to = (chip + step) % (FREQ // 2)
        remote(num_half.at[to], num_recv.at[chip], num_sem.at[0], num_sem.at[1], (2 * to + core, mz)).start()
        return carry

    core_copy.wait()
    gram_send[1] = gram_send[0] + gram_core[...]
    x_copies = []
    for step in range(1, 4):
        copy = remote(
            gram_send.at[1],
            gram_x.at[step - 1],
            gram_sems.at[1 + step],
            gram_sems.at[4 + step],
            at((x + step) % 4, y, z_mine, core),
        )
        copy.start()
        x_copies.append(copy)
    for copy in z_copies[1:]:
        copy.wait_send()

    @pl.when(z_lo // 2 != core)
    def _():
        z_copies[0].wait_send()

    for spot, sem in ((blocks.at[0, 0:3], second_send), (blocks.at[0:3], third_send)):
        remote(spot, spot, sem, exchange_sem.at[0, 1], partner).wait_send()

    num_swap.wait()
    num_half[...] = num_send[core] + num_core[...]
    lax.fori_loop(1, FREQ // 2, send_num, 0)
    for copy in x_copies:
        copy.wait()
    gram_send[2] = (gram_send[1] + gram_x[0]) + (gram_x[1] + gram_x[2])
    z_grams = []
    for step in range(1, 4):
        copy = remote(
            gram_send.at[2],
            gram_z.at[step - 1],
            gram_sems.at[7 + step],
            gram_sems.at[10 + step],
            at(x, y, z_hi * 4 + (z_lo + step) % 4, core),
        )
        copy.start()
        z_grams.append(copy)
    for copy in z_grams:
        copy.wait()
    packed = (gram_send[2] + gram_z[0]) + (gram_z[1] + gram_z[2])

    row64 = lax.broadcasted_iota(jnp.int32, (COMP, LANES), 0)
    lane64 = lax.broadcasted_iota(jnp.int32, (COMP, LANES), 1)
    row8 = row64[:8]
    gram = jnp.concatenate([packed, half_turn(packed)], axis=0)
    diagonal = jnp.where(lane64 == row64, gram, 0.0)
    scale_rows = jnp.broadcast_to(lax.rsqrt(jnp.sum(diagonal, axis=1, keepdims=True)), gram.shape)
    scale_lanes = lax.rsqrt(jnp.sum(diagonal, axis=0, keepdims=True))
    unit = jnp.where(lane64 == row64 + COMP, scale_rows, 0.0)
    whole = jnp.where(lane64 < COMP, gram * scale_rows * scale_lanes, unit)
    matrix = [whole[8 * at_ : 8 * at_ + 8] for at_ in range(8)]

    def line(value, step):
        return value[step // 8][step % 8 : step % 8 + 1]

    def pivot(columns, step):
        one, two = columns
        return line(one, step) * line(two, step + 1) - line(two, step) * line(one, step + 1)

    def clear(value, columns, step, scale):
        one, two = columns
        at_, row_at = step // 8, step % 8
        top, low = line(value, step), line(value, step + 1)
        top_new = (line(two, step + 1) * top - line(two, step) * low) * scale
        low_new = (line(one, step) * low - line(one, step + 1) * top) * scale
        rest = [v - o * top_new - t * low_new for v, o, t in zip(value, one, two)]
        rest[at_] = jnp.where(row8 == row_at, top_new, jnp.where(row8 == row_at + 1, low_new, rest[at_]))
        return rest

    for step in range(0, COMP, 8):
        columns = [
            [jnp.broadcast_to(block[:, at_ : at_ + 1], block.shape) for block in matrix] for at_ in range(step, step + 8)
        ]
        for at_ in range(step, step + 8, 2):
            pair, columns = columns[:2], columns[2:]
            scale = 1.0 / pivot(pair, at_)
            columns = [clear(value, pair, at_, scale) for value in columns]
            matrix = clear(matrix, pair, at_, scale)
    inverse = (jnp.concatenate(matrix, axis=0) * scale_rows)[:, COMP:]

    inverse_both = jnp.concatenate(split(inverse), axis=0)
    others = num_recv.at[0 : FREQ // 2 - 1]
    num_all = remote(others, others, num_sem.at[0], num_sem.at[1], partner)
    num_all.wait_recv()
    num_recv[chip] = num_half[chip]
    summed = jnp.sum(num_recv[...], axis=0)
    own_channels = jnp.concatenate([summed[:, :64], summed[:, 64:]], axis=0)
    high, low = split(own_channels)
    parts = lax.dot_general(
        jnp.concatenate([high, low], axis=0), inverse_both, (((1,), (1,)), ((), ())), preferred_element_type=F32
    )
    out_ref[...] = (parts[:OWN, :COMP] + parts[:OWN, COMP:]) + parts[OWN:, :COMP]

    num_all.wait_send()


def on_device(intensity, elution, loadings, shifts, bin_weight):
    vmem = pl.BlockSpec(memory_space=pltpu.VMEM)
    dma = pltpu.SemaphoreType.DMA
    def held(value):
        return pltpu.with_memory_space_constraint(value, pltpu.HBM)

    by_channel = pl.pallas_call(
        kernel,
        out_shape=jax.ShapeDtypeStruct((OWN, COMP), F32),
        in_specs=[pl.BlockSpec(memory_space=pltpu.HBM)] * 6,
        out_specs=vmem,
        scratch_shapes=[
            pltpu.VMEM((24, COMP), F32),
            pltpu.VMEM((RUNS, COMP), F32),
            pltpu.VMEM((RUNS, COMP), jnp.int32),
            pltpu.VMEM((ROWS, LANES), F32),
            pltpu.VMEM((448, LANES), F32),
            pltpu.VMEM((RUNS, BLOCK, CHANNELS), BF16),
            pltpu.VMEM((3, 4, LANES), F32),
            pltpu.VMEM((2, 2, 2, 3, 4, LANES), F32),
            pltpu.VMEM((4, 4, 2, 48, LANES), F32),
            pltpu.VMEM((4 * SLAB, LANES), BF16),
            pltpu.VMEM((SLAB + 256, LANES), BF16),
            pltpu.VMEM((3, 16, LANES), F32),
            pltpu.VMEM((LANES, LANES), F32),
            pltpu.VMEM((2, ROWS, LANES, LANES), BF16),
            pltpu.VMEM((768, 256), F32),
            pltpu.VMEM((2, WINDOW, LANES), F32),
            pltpu.VMEM((2, 224, LANES), F32),
            pltpu.VMEM((2, 224, LANES), F32),
            pltpu.VMEM((RUNS // 2, BLOCK, 2 * LANES), BF16),
            pltpu.VMEM((3, 32, LANES), F32),
            pltpu.VMEM((32, LANES), F32),
            pltpu.VMEM((3, 32, LANES), F32),
            pltpu.VMEM((3, 32, LANES), F32),
            pltpu.VMEM((2, FREQ // 2, 8, LANES), F32),
            pltpu.VMEM((FREQ // 2, 8, LANES), F32),
            pltpu.VMEM((FREQ // 2, 8, LANES), F32),
            pltpu.VMEM((FREQ // 2, 8, LANES), F32),
            dma((6,)),
            dma((8,)),
            dma((2, 2, 2)),
            dma,
            dma,
            dma((4, 4)),
            dma((2, 2)),
            dma((14,)),
            dma((4,)),
        ],
        compiler_params=pltpu.CompilerParams(
            collective_id=0, has_side_effects=True, vmem_limit_bytes=32 * 1024 * 1024
        ),
    )(*map(held, (elution, loadings, shifts, bin_weight.reshape(ROWS, LANES), transform_tables(), intensity)))
    return by_channel.T


def solution(mesh):
    in_specs = (P(None, "freq", "mz"), P(("freq", "mz"), None), P(), P(), P())
    out_specs = P(None, ("mz", "freq"))
    return jax.shard_map(on_device, mesh=mesh, in_specs=in_specs, out_specs=out_specs, check_vma=False)
```
